32 devices in a mesh: row: 4 (over y, core), col: 8 (over z, x).
Axes of the slice: x: 2, y: 2, z: 4, core: 2. Of those that a mesh axis runs over, the one named last changes fastest.
Arguments:
- patches: float32 [32, 64, 2, 128, 128], P('row', 'col'), may hold values from -6 to 6
- right_offset: int32 [32, 64], P('row', 'col'), may hold values from 57 to 112, as said below
- right_width: int32 [32, 64], P('row', 'col'), may hold values from 16 to 64
- down_offset: int32 [32, 64], P('row', 'col'), may hold values from 57 to 112, as said below
- down_width: int32 [32, 64], P('row', 'col'), may hold values from 16 to 64
Outputs:
- blended: float32 [32, 64, 2, 128, 128], P('row', 'col')
- phases: float32 [2, 32, 64], P(None, 'row', 'col')
The draws below stay inside these ranges and needn't reach their ends.
Inputs may be any that keep to these rules, and one draw needn't show every extreme that they name: right_offset + right_width lies above 120 and at most 128. down_offset + down_width lies above 120 and at most 128.
All inputs are finite; a program needn't handle non-finite values.
Results may differ from the reference program's by a relative error of at most 0.0003.
Values sent between devices are 32-bit elements; how exact they have to be, the bound alone decides.
A program may use at most 128 MiB of HBM per device.

```python
import jax
import jax.numpy as jnp
from jax import lax

PATCH = 128
STRIP_MIN = 16
STRIP_MAX = 64
JITTER = 8
ITERS = 2
GRID_ROWS = 32
GRID_COLS = 64


def draw_patches(key, part):
    shape = (GRID_ROWS, GRID_COLS, 2, PATCH, PATCH)
    return jnp.clip(jax.random.normal(jax.random.fold_in(key, 5), shape, jnp.float32), -6.0, 6.0)


def strip_table(key, salt):
    base = jax.random.fold_in(key, salt)
    width_key, jitter_key = jax.random.split(base)
    width = jax.random.randint(width_key, (GRID_ROWS, GRID_COLS), STRIP_MIN, STRIP_MAX + 1)
    jitter = jax.random.randint(jitter_key, (GRID_ROWS, GRID_COLS), 0, JITTER)
    width = width.at[0, 0].set(STRIP_MAX).at[1, 1].set(STRIP_MIN)
    jitter = jitter.at[0, 0].set(JITTER - 1).at[1, 1].set(0)
    return (width.astype(jnp.int32), (PATCH - width - jitter).astype(jnp.int32))


def draw_right_offset(key, part):
    return strip_table(key, 11)[1]


def draw_right_width(key, part):
    return strip_table(key, 11)[0]


def draw_down_offset(key, part):
    return strip_table(key, 23)[1]


def draw_down_width(key, part):
    return strip_table(key, 23)[0]


def setup_inputs(seed: int = 0) -> dict:
    seeds = jax.random.split(jax.random.key(seed), 6)
    return {
        "patches": draw_patches(jax.random.fold_in(seeds[5], 71), 0),
        "right_offset": draw_right_offset(jax.random.fold_in(seeds[5], 71), 0),
        "right_width": draw_right_width(jax.random.fold_in(seeds[5], 71), 0),
        "down_offset": draw_down_offset(jax.random.fold_in(seeds[5], 71), 0),
        "down_width": draw_down_width(jax.random.fold_in(seeds[5], 71), 0),
    }


eps_norm = 1.0

def gather_lanes(field, index, axis):
    return jnp.take_along_axis(field, jnp.broadcast_to(index, field.shape), axis=axis)

def correlate(shifted, partner, width_table):
    real_part = lax.optimization_barrier(jnp.sum(shifted[..., 0, :, :] * partner[..., 0, :, :] + shifted[..., 1, :, :] * partner[..., 1, :, :], axis=(-2, -1)))
    imag_part = lax.optimization_barrier(jnp.sum(shifted[..., 0, :, :] * partner[..., 1, :, :] - shifted[..., 1, :, :] * partner[..., 0, :, :], axis=(-2, -1)))
    scale = 1.0 / jnp.sqrt(PATCH * width_table.astype(jnp.float32))
    return jnp.stack([real_part * scale, imag_part * scale])

def complex_times(factor, field):
    return jnp.stack([factor[0] * field[0] - factor[1] * field[1], factor[0] * field[1] + factor[1] * field[0]])

def conj_times(factor, field):
    return jnp.stack([factor[0] * field[0] + factor[1] * field[1], factor[0] * field[1] - factor[1] * field[0]])

def rotate(factor, field):
    real_part = factor[..., 0:1, :, :] * field[..., 0:1, :, :] - factor[..., 1:2, :, :] * field[..., 1:2, :, :]
    imag_part = factor[..., 0:1, :, :] * field[..., 1:2, :, :] + factor[..., 1:2, :, :] * field[..., 0:1, :, :]
    return jnp.concatenate([real_part, imag_part], axis=-3)

def from_east(field):
    return jnp.pad(field[:, :, 1:], ((0, 0), (0, 0), (0, 1)))

def from_south(field):
    return jnp.pad(field[:, 1:, :], ((0, 0), (0, 1), (0, 0)))

def from_west(field):
    return jnp.pad(field[:, :, :-1], ((0, 0), (0, 0), (1, 0)))

def from_north(field):
    return jnp.pad(field[:, :-1, :], ((0, 0), (1, 0), (0, 0)))

def reference(patches, right_offset, right_width, down_offset, down_width):
    lane_index = jnp.arange(PATCH, dtype=jnp.int32)

    def row_fields(row):
        here = lax.dynamic_index_in_dim(patches, row, 0, False)
        below = lax.dynamic_index_in_dim(patches, jnp.minimum(row + 1, GRID_ROWS - 1).astype(jnp.int32), 0, False)
        below = below * jnp.where(row + 1 < GRID_ROWS, 1.0, 0.0).astype(jnp.float32)
        east = jnp.concatenate([here[1:], jnp.zeros_like(here[:1])], axis=0)
        east_off = lax.dynamic_index_in_dim(right_offset, row, 0, False)
        east_wid = lax.dynamic_index_in_dim(right_width, row, 0, False)
        south_off = lax.dynamic_index_in_dim(down_offset, row, 0, False)
        south_wid = lax.dynamic_index_in_dim(down_width, row, 0, False)
        return (here, below, east, east_off, east_wid, south_off, south_wid)

    def corr_row(row):
        here, below, east, east_off, east_wid, south_off, south_wid = row_fields(row)
        east_index = jnp.clip(lane_index[None, :] + east_off[:, None], 0, PATCH - 1)
        east_keep = (lane_index[None, :] < east_wid[:, None]).astype(jnp.float32)
        east_shifted = gather_lanes(here, east_index[:, None, None, :], 3) * east_keep[:, None, None, :]
        south_index = jnp.clip(lane_index[None, :] + south_off[:, None], 0, PATCH - 1)
        south_keep = (lane_index[None, :] < south_wid[:, None]).astype(jnp.float32)
        south_shifted = gather_lanes(here, south_index[:, None, :, None], 2) * south_keep[:, None, :, None]
        return jnp.concatenate([correlate(east_shifted, east, east_wid), correlate(south_shifted, below, south_wid)])
    rows = jnp.arange(GRID_ROWS, dtype=jnp.int32)
    corr = jnp.transpose(lax.map(corr_row, rows), (1, 0, 2))
    corr_east = corr[0:2]
    corr_south = corr[2:4]
    phase_now = jnp.stack([jnp.ones((GRID_ROWS, GRID_COLS), jnp.float32), jnp.zeros((GRID_ROWS, GRID_COLS), jnp.float32)])
    for step in range(ITERS):
        image = complex_times(corr_east, from_east(phase_now)) + complex_times(corr_south, from_south(phase_now))
        image = image + conj_times(from_west(corr_east), from_west(phase_now)) + conj_times(from_north(corr_south), from_north(phase_now))
        mean_square = jnp.sum(image * image) / (GRID_ROWS * GRID_COLS)
        phase_now = image / jnp.sqrt(mean_square + eps_norm)
    east_phase = from_east(phase_now)
    south_phase = from_south(phase_now)
    col_live = (jnp.arange(GRID_COLS, dtype=jnp.int32) < GRID_COLS - 1).astype(jnp.float32)

    def blend_row(row):
        here, below, east, east_off, east_wid, south_off, south_wid = row_fields(row)
        east_index = jnp.clip(lane_index[None, :] - east_off[:, None], 0, PATCH - 1)
        east_mask = ((lane_index[None, :] >= east_off[:, None]) & (lane_index[None, :] < east_off[:, None] + east_wid[:, None])).astype(jnp.float32)
        east_place = gather_lanes(east, east_index[:, None, None, :], 3) * east_mask[:, None, None, :]
        south_index = jnp.clip(lane_index[None, :] - south_off[:, None], 0, PATCH - 1)
        south_mask = ((lane_index[None, :] >= south_off[:, None]) & (lane_index[None, :] < south_off[:, None] + south_wid[:, None])).astype(jnp.float32)
        south_place = gather_lanes(below, south_index[:, None, :, None], 2) * south_mask[:, None, :, None]
        own = jnp.transpose(lax.dynamic_index_in_dim(phase_now, row, 1, False))[:, :, None, None]
        east_factor = jnp.transpose(lax.dynamic_index_in_dim(east_phase, row, 1, False))[:, :, None, None]
        south_factor = jnp.transpose(lax.dynamic_index_in_dim(south_phase, row, 1, False))[:, :, None, None]
        numer = rotate(own, here) + rotate(east_factor, east_place) + rotate(south_factor, south_place)
        south_live = jnp.where(row + 1 < GRID_ROWS, 1.0, 0.0).astype(jnp.float32)
        weight = 1.0 + (east_mask * col_live[:, None])[:, None, None, :] + (south_mask * south_live)[:, None, :, None]
        return numer / weight
    blended = lax.map(blend_row, rows)
    return (blended, phase_now)
```

```python
import functools

import jax
import jax.numpy as jnp
from jax import lax
from jax.experimental import pallas as pl
from jax.experimental.pallas import tpu as pltpu
from jax.sharding import PartitionSpec as P

ITERS = 2
PAD = 64
eps_norm = 1.0
highest = lax.Precision.HIGHEST
MESH = pl.DeviceIdType.MESH
f32 = jnp.float32


def fold_rows(x):
    return jnp.sum(x, axis=0, keepdims=True)


def doubling(pos, n, at):
    if n == 1:
        return []
    rounds = [[at(-1) + (pos > 0, pos < n - 1)]]
    known = 1
    while known < n - 1:
        rounds.append([
            at(-known) + (pos >= known, pos < n - known),
            at(known) + (pos < n - known, pos >= known),
        ])
        known *= 2
    return rounds


def n_rounds(n):
    return len(doubling(0, n, lambda k: (0, 0)))


def sync_kernel(
    dims, patches, ro_in, rw_in, do_in, dw_in, pv, east_recv, south_recv, phase_out,
    epack, acc, send_buf, recv, fields, ro, rw, do, dw,
    col_sem, rest_sem, e_send, e_recv, s_send, s_recv, g_send, g_recv, table_sem, round_sem,
):
    R, C, S, nr, nc = dims
    H, ndev = S // 2, nr * nc
    lo = H - 8
    my_row, my_col = lax.axis_index("row"), lax.axis_index("col")
    me = my_row * nc + my_col

    turn_rows = [lax.rem(my_row + k, nr) for k in range(nr)]
    turn_cols = [lax.rem(my_col + k, nc) for k in range(nc)]
    others = [
        (turn_rows[a], turn_cols[b]) for a in range(nr) for b in range(nc) if a or b
    ]
    barrier = pltpu.get_barrier_semaphore()

    def signal(sem, row, col, there):
        @pl.when(there)
        def _():
            pl.semaphore_signal(sem, inc=1, device_id=(row, col), device_id_type=MESH)

    def await_all(sem, *due):
        amount = sum(one.astype(jnp.int32) for one in due)

        @pl.when(amount > 0)
        def _():
            pl.semaphore_wait(sem, amount)

    steps = doubling(my_row, nr, lambda k: (my_row + k, my_col))
    steps += doubling(my_col, nc, lambda k: (my_row, my_col + k))

    def tell(k):
        for row, col, there, _ in steps[k]:
            signal(round_sem.at[k], row, col, there)

    def hear(k):
        await_all(round_sem.at[k], *(here for _, _, _, here in steps[k]))

    def spread(k):
        if k < len(steps):
            hear(k)
            if k + 1 < len(steps):
                tell(k + 1)

    cols = [
        pltpu.make_async_copy(
            patches.at[pl.ds(i * C * 2 * S, 2 * S)],
            pv.at[pl.ds(PAD + i * C * 2 * S, 2 * S)],
            col_sem.at[i],
        )
        for i in range(R)
    ]
    rests = [
        pltpu.make_async_copy(
            patches.at[pl.ds((i * C + 1) * 2 * S, (C - 1) * 2 * S)],
            pv.at[pl.ds(PAD + (i * C + 1) * 2 * S, (C - 1) * 2 * S)],
            rest_sem.at[i],
        )
        for i in range(R)
    ]
    tables = [
        pltpu.make_async_copy(here, there, table_sem.at[k])
        for k, (here, there) in enumerate(zip((ro_in, rw_in, do_in, dw_in), (ro, rw, do, dw)))
    ]
    for copy in cols:
        copy.start()
    signal(barrier, my_row + 1, my_col, my_row < nr - 1)
    signal(barrier, my_row, my_col + 1, my_col < nc - 1)
    for copy in tables:
        copy.start()
    for copy in rests:
        copy.start()
    lane = lax.broadcasted_iota(jnp.int32, (S, S), 1)

    def pack(i):
        base = PAD + i * C * 2 * S
        cols[i].wait()
        re = pv[pl.ds(base, S), :]
        im = pv[pl.ds(base + S, S), :]
        epack[pl.ds(i * S, S), :] = jnp.where(lane < H, re, pltpu.roll(im, H, 1))

    def south_copy(k, row):
        return pltpu.make_async_remote_copy(
            src_ref=patches.at[pl.ds(k * S, H)],
            dst_ref=south_recv.at[pl.ds(PAD + k * H, H)],
            send_sem=s_send.at[k],
            recv_sem=s_recv.at[k],
            device_id=(row, my_col),
            device_id_type=MESH,
        )

    def east_copy(k, col):
        return pltpu.make_async_remote_copy(
            src_ref=epack.at[pl.ds(k * S, S)],
            dst_ref=east_recv.at[pl.ds(k * S, S)],
            send_sem=e_send.at[k],
            recv_sem=e_recv.at[k],
            device_id=(my_row, col),
            device_id_type=MESH,
        )

    def send_east(i):
        @pl.when(my_col > 0)
        def _():
            east_copy(i, my_col - 1).start()

    for i in range(2):
        pack(i)
    await_all(barrier, my_row > 0, my_col > 0)
    for i in range(2):
        send_east(i)

    @pl.when(my_row > 0)
    def _():
        for k in range(2 * C):
            south_copy(k, my_row - 1).start()

    if steps:
        tell(0)
    for i in range(2, R):
        pack(i)
        send_east(i)
    acc[...] = jnp.zeros_like(acc)
    for copy in tables:
        copy.wait()
    for copy in rests:
        copy.wait()

    lane1 = lax.broadcasted_iota(jnp.int32, (1, S), 1)
    row8 = lax.broadcasted_iota(jnp.int32, (8, S), 0)

    def put(plane, p, re, im, width):
        scale = 1.0 / jnp.sqrt(jnp.full((1, S), S * width, jnp.int32).astype(f32))
        acc[pl.ds(plane * R * C + p, 1), :] = fold_rows(re) * scale
        acc[pl.ds((plane + 1) * R * C + p, 1), :] = fold_rows(im) * scale

    def gathered(pieces):
        re, im = None, None
        for a_re, a_im, b_re, b_im in pieces:
            u, v = a_re * b_re + a_im * b_im, a_re * b_im - a_im * b_re
            re, im = (u, v) if re is None else (re + u, im + v)
        return re, im

    def east_store(i, j, load_b):
        p = i * C + j
        o, w = ro[i, j], rw[i, j]
        base = PAD + p * 2 * S
        re, im = gathered(
            (pv[pl.ds(pl.multiple_of(base + q, 8), 8), :],
             pv[pl.ds(pl.multiple_of(base + S + q, 8), 8), :]) + load_b(q, o)
            for q in range(0, S, 8)
        )
        keep = (lane1 >= o) & (lane1 < o + w)
        put(0, p, jnp.where(keep, re, 0.0), jnp.where(keep, im, 0.0), w)

    def east_inner(i, carry):
        for j in range(C - 1):
            base = PAD + (i * C + j + 1) * 2 * S

            def load_b(q, o):
                return (
                    pltpu.roll(pv[pl.ds(pl.multiple_of(base + q, 8), 8), :], o, 1),
                    pltpu.roll(pv[pl.ds(pl.multiple_of(base + S + q, 8), 8), :], o, 1),
                )

            east_store(i, j, load_b)
        return carry

    def south_store(i, j, ref, start, gap):
        p = i * C + j
        o, w = do[i, j], dw[i, j]
        base = PAD + p * 2 * S

        def piece(q):
            keep = row8 >= o - q if q < S - 8 else row8 < o + w - q
            b_re = ref[pl.ds(start + (q - o), 8), :]
            b_im = ref[pl.ds(start + gap + (q - o), 8), :]
            return (
                pv[pl.ds(pl.multiple_of(base + q, 8), 8), :],
                pv[pl.ds(pl.multiple_of(base + S + q, 8), 8), :],
                jnp.where(keep, b_re, 0.0),
                jnp.where(keep, b_im, 0.0),
            )

        re, im = gathered(piece(q) for q in range(lo, S, 8))
        put(2, p, re, im, w)

    def south_inner(i, carry):
        for j in range(C):
            south_store(i, j, pv, PAD + ((i + 1) * C + j) * 2 * S, S)
        return carry

    spread(0)
    lax.fori_loop(0, R // 2, east_inner, 0)
    spread(1)
    lax.fori_loop(R // 2, R, east_inner, 0)
    spread(2)
    lax.fori_loop(0, R // 2, south_inner, 0)
    spread(3)
    lax.fori_loop(R // 2, R - 1, south_inner, 0)
    spread(4)

    @pl.when(my_row < nr - 1)
    def _():
        for k in range(2 * C):
            south_copy(k, my_row).wait_recv()

    @pl.when(my_row == nr - 1)
    def _():
        south_recv[...] = jnp.zeros_like(south_recv)

    for j in range(C):
        south_store(R - 1, j, south_recv, PAD + j * 2 * H, H)

    for k in range(5, len(steps)):
        spread(k)

    @pl.when(my_col == nc - 1)
    def _():
        east_recv[...] = jnp.zeros_like(east_recv)

    for i in range(R):

        @pl.when(my_col < nc - 1)
        def _():
            east_copy(i, my_col).wait_recv()

        def load_b(q, o):
            both = east_recv[pl.ds(i * S + q, 8), :]
            return pltpu.roll(both, o, 1), pltpu.roll(both, lax.rem(o + H, S), 1)

        east_store(i, C - 1, load_b)

    sums = lax.dot_general(
        jnp.ones((8, S), f32), acc[...], (((1,), (1,)), ((), ())),
        precision=highest, preferred_element_type=f32,
    )
    mine = jnp.concatenate([sums[0:1, :S], sums[0:1, S:]], axis=0)
    send_buf[...] = mine
    recv[me] = mine

    def index(d):
        return d[0] * nc + d[1]

    def gather_copy(target, source):
        return pltpu.make_async_remote_copy(
            src_ref=send_buf,
            dst_ref=recv.at[index(source)],
            send_sem=g_send.at[index(target)],
            recv_sem=g_recv.at[index(source)],
            device_id=target,
            device_id_type=MESH,
        )

    for other in others:
        gather_copy(other, (my_row, my_col)).start()
    for other in others:
        gather_copy(other, other).wait_recv()

    got = recv[...]
    east, south = got[:, 0, :], got[:, 1, :]
    field = lax.broadcasted_iota(jnp.int32, (ndev, S), 0)
    slot = lax.broadcasted_iota(jnp.int32, (ndev, S), 1)
    valid = slot < R * C
    j_of, i_of = slot % C, (slot // C) % R
    dc, dr = field % nc, field // nc

    def roll(x, by, axis):
        return pltpu.roll(x, by % x.shape[axis], axis)

    def from_east(x):
        far = roll(roll(x, -1, 0), C - 1, 1)
        far = jnp.where(dc < nc - 1, far, 0.0)
        return jnp.where(j_of < C - 1, roll(x, -1, 1), far)

    def from_west(x):
        far = roll(roll(x, 1, 0), 1 - C, 1)
        far = jnp.where(dc > 0, far, 0.0)
        return jnp.where(j_of > 0, roll(x, 1, 1), far)

    def from_south(x):
        far = roll(roll(x, -nc, 0), (R - 1) * C, 1)
        far = jnp.where(dr < nr - 1, far, 0.0)
        return jnp.where(i_of < R - 1, roll(x, -C, 1), far)

    def from_north(x):
        far = roll(roll(x, nc, 0), -(R - 1) * C, 1)
        far = jnp.where(dr > 0, far, 0.0)
        return jnp.where(i_of > 0, roll(x, C, 1), far)

    ce = (jnp.where(valid, east, 0.0), jnp.where(valid, roll(east, -R * C, 1), 0.0))
    cs = (jnp.where(valid, south, 0.0), jnp.where(valid, roll(south, -R * C, 1), 0.0))
    cw = tuple(from_west(x) for x in ce)
    cn = tuple(from_north(x) for x in cs)
    count = float(ndev * R * C)

    def times(a, b):
        return (a[0] * b[0] - a[1] * b[1], a[0] * b[1] + a[1] * b[0])

    def conj_times(a, b):
        return (a[0] * b[0] + a[1] * b[1], a[0] * b[1] - a[1] * b[0])

    now = (jnp.ones((ndev, S), f32), jnp.zeros((ndev, S), f32))
    for step in range(ITERS):
        terms = (
            times(ce, tuple(from_east(x) for x in now)),
            times(cs, tuple(from_south(x) for x in now)),
            conj_times(cw, tuple(from_west(x) for x in now)),
            conj_times(cn, tuple(from_north(x) for x in now)),
        )
        image = tuple(
            jnp.where(valid, terms[0][q] + terms[1][q] + terms[2][q] + terms[3][q], 0.0)
            for q in range(2)
        )
        total = jnp.sum(image[0] * image[0] + image[1] * image[1], axis=0, keepdims=True)
        total = jnp.sum(total, axis=1, keepdims=True)
        factor = 1.0 / jnp.sqrt(total / count + eps_norm)
        now = (image[0] * factor, image[1] * factor)
    outs = now + tuple(from_east(x) for x in now) + tuple(from_south(x) for x in now)
    for q in range(6):
        fields[q] = outs[q]
    for q in range(6):
        phase_out[q : q + 1, :] = fields[q, pl.ds(me, 1), :]
    phase_out[6:8, :] = jnp.zeros((2, S), f32)

    for other in others:
        gather_copy(other, (my_row, my_col)).wait_send()

    @pl.when(my_col > 0)
    def _():
        for k in range(R):
            east_copy(k, my_col - 1).wait_send()

    @pl.when(my_row > 0)
    def _():
        for k in range(2 * C):
            south_copy(k, my_row - 1).wait_send()


def blend_kernel(
    dims, pv, ev, sv, ro, rw, do, dw, g, out, phases, ov, out_sem,
):
    R, C, S, nr, nc = dims
    H = S // 2
    lo = H - 8
    row_size = C * 2 * S
    last_col = lax.axis_index("col") == nc - 1
    last_row = lax.axis_index("row") == nr - 1

    def save(i):
        return pltpu.make_async_copy(
            ov.at[pl.ds(i * row_size, row_size)],
            out.at[pl.ds(i * row_size, row_size)],
            out_sem.at[i],
        )

    lane = lax.broadcasted_iota(jnp.int32, (1, S), 1)
    row8 = lax.broadcasted_iota(jnp.int32, (8, S), 0)

    def at(ref, row):
        return ref[pl.ds(pl.multiple_of(row, 8), 8), :]

    def place(i, j, east, ref, start, gap):
        p = i * C + j
        oe, we, os, ws = ro[i, j], rw[i, j], do[i, j], dw[i, j]
        g_re, g_im = g[0, p], g[1, p]
        ge_re, ge_im, gs_re, gs_im = g[2, p], g[3, p], g[4, p], g[5, p]
        phases[0, i, j] = g_re
        phases[1, i, j] = g_im
        base = PAD + p * 2 * S
        to = p * 2 * S
        keep_e = (lane >= oe) & (lane < oe + we)
        live_e = keep_e & jnp.logical_not((j == C - 1) & last_col)
        half = jnp.where(live_e, f32(0.5), f32(1.0))
        third = jnp.where(live_e, f32(1.0 / 3.0), f32(0.5))
        down = jnp.logical_not((i == R - 1) & last_row)
        third = jnp.where(jnp.full((1, S), down), third, half)
        half, third = jnp.broadcast_to(half, (8, S)), jnp.broadcast_to(third, (8, S))
        e_re = jnp.broadcast_to(jnp.where(keep_e, ge_re, 0.0), (8, S))
        e_im = jnp.broadcast_to(jnp.where(keep_e, ge_im, 0.0), (8, S))
        h_re, h_im, x_re, x_im = g_re * half, g_im * half, e_re * half, e_im * half
        for q in range(0, S, 8):
            a_re, a_im = at(pv, base + q), at(pv, base + S + q)
            b_re, b_im = east(q, oe)
            if q < lo:
                n_re = (h_re * a_re - h_im * a_im) + (x_re * b_re - x_im * b_im)
                n_im = (h_re * a_im + h_im * a_re) + (x_re * b_im + x_im * b_re)
            else:
                keep = row8 >= os - q if q < S - 8 else row8 < os + ws - q
                s_re = ref[pl.ds(start + (q - os), 8), :]
                s_im = ref[pl.ds(start + gap + (q - os), 8), :]
                n_re = (g_re * a_re - g_im * a_im) + (e_re * b_re - e_im * b_im)
                n_im = (g_re * a_im + g_im * a_re) + (e_re * b_im + e_im * b_re)
                inv = jnp.where(keep, third, half)
                n_re = (n_re + jnp.where(keep, gs_re * s_re - gs_im * s_im, 0.0)) * inv
                n_im = (n_im + jnp.where(keep, gs_re * s_im + gs_im * s_re, 0.0)) * inv
            ov[pl.ds(pl.multiple_of(to + q, 8), 8), :] = n_re
            ov[pl.ds(pl.multiple_of(to + S + q, 8), 8), :] = n_im

    def east_of(i, j):
        base = PAD + (i * C + j + 1) * 2 * S

        def east(q, o):
            return pltpu.roll(at(pv, base + q), o, 1), pltpu.roll(at(pv, base + S + q), o, 1)

        return east

    def east_rim(i):
        def east(q, o):
            both = at(ev, i * S + q)
            return pltpu.roll(both, o, 1), pltpu.roll(both, lax.rem(o + H, S), 1)

        return east

    def south_of(i, j):
        return pv, PAD + ((i + 1) * C + j) * 2 * S, S

    def south_rim(j):
        return sv, PAD + j * 2 * H, H

    def rows(i, carry):
        for j in range(C):
            place(i, j, east_of(i, j) if j < C - 1 else east_rim(i), *south_of(i, j))
        save(i).start()
        return carry

    lax.fori_loop(0, R - 1, rows, 0)
    for j in range(C):
        place(R - 1, j, east_of(R - 1, j) if j < C - 1 else east_rim(R - 1), *south_rim(j))
    save(R - 1).start()
    for i in range(R):
        save(i).wait()


def local(nr, nc, patches, right_offset, right_width, down_offset, down_width):
    R, C, _, S, _ = patches.shape
    H, ndev = S // 2, nr * nc
    dims = (R, C, S, nr, nc)
    flat = patches.reshape(R * C * 2 * S, S)
    anyspec = pl.BlockSpec(memory_space=pl.ANY)
    smem = pl.BlockSpec(memory_space=pltpu.SMEM)
    vmem = pl.BlockSpec(memory_space=pltpu.VMEM)
    dma = pltpu.SemaphoreType.DMA
    tables = (right_offset, right_width, down_offset, down_width)
    pv, east_halo, south_halo, phase = pl.pallas_call(
        functools.partial(sync_kernel, dims),
        out_shape=(
            pltpu.VMEM((PAD + R * C * 2 * S, S), f32),
            pltpu.VMEM((R * S, S), f32),
            pltpu.VMEM((2 * PAD + 2 * C * H, S), f32),
            jax.ShapeDtypeStruct((8, S), f32),
        ),
        in_specs=[pl.BlockSpec(memory_space=pltpu.HBM)] * 5,
        out_specs=(vmem,) * 4,
        scratch_shapes=[
            pltpu.VMEM((R * S, S), f32),
            pltpu.VMEM((4 * R * C, S), f32),
            pltpu.VMEM((2, S), f32),
            pltpu.VMEM((ndev, 2, S), f32),
            pltpu.VMEM((6, ndev, S), f32),
        ] + [pltpu.SMEM((R, C), jnp.int32)] * 4 + [
            dma((R,)), dma((R,)),
            dma((R,)), dma((R,)),
            dma((2 * C,)), dma((2 * C,)),
            dma((ndev,)), dma((ndev,)),
            dma((4,)),
            pltpu.SemaphoreType.REGULAR((n_rounds(nr) + n_rounds(nc),)),
        ],
        compiler_params=pltpu.CompilerParams(
            collective_id=0, has_side_effects=True, vmem_limit_bytes=16 << 20
        ),
        name="sync_patches",
    )(*(pltpu.with_memory_space_constraint(x, pltpu.HBM) for x in (flat, *tables)))
    blended, phases = pl.pallas_call(
        functools.partial(blend_kernel, dims),
        out_shape=(
            jax.ShapeDtypeStruct((R * C * 2 * S, S), f32),
            jax.ShapeDtypeStruct((2, R, C), f32),
        ),
        in_specs=[vmem] * 3 + [smem] * 5,
        out_specs=(anyspec, smem),
        scratch_shapes=[
            pltpu.VMEM((R * C * 2 * S, S), f32),
            dma((R,)),
        ],
        compiler_params=pltpu.CompilerParams(vmem_limit_bytes=24 << 20),
        name="blend_patches",
    )(pv, east_halo, south_halo, *tables, phase)
    return blended.reshape(patches.shape), phases


def solution(mesh):
    return jax.shard_map(
        functools.partial(local, mesh.shape["row"], mesh.shape["col"]),
        mesh=mesh,
        in_specs=(P("row", "col", None, None, None),) + (P("row", "col"),) * 4,
        out_specs=(P("row", "col", None, None, None), P(None, "row", "col")),
        check_vma=False,
    )
```

```python
import functools

import jax
import jax.numpy as jnp
from jax import lax
from jax.experimental import pallas as pl
from jax.experimental.pallas import tpu as pltpu
from jax.sharding import PartitionSpec as P

ITERS = 2
PAD = 64
eps_norm = 1.0
highest = lax.Precision.HIGHEST
MESH = pl.DeviceIdType.MESH
f32 = jnp.float32


def fold_rows(x):
    return jnp.sum(x, axis=0, keepdims=True)


def doubling(pos, n, at):
    if n == 1:
        return []
    rounds = [[at(-1) + (pos > 0, pos < n - 1)]]
    known = 1
    while known < n - 1:
        rounds.append([
            at(-known) + (pos >= known, pos < n - known),
            at(known) + (pos < n - known, pos >= known),
        ])
        known *= 2
    return rounds


def n_rounds(n):
    return len(doubling(0, n, lambda k: (0, 0)))


def sync_kernel(
    dims, patches, ro_in, rw_in, do_in, dw_in, aw, ew, sw, factors, phase_out,
    pv, east_recv, south_recv,
    epack, acc, send_buf, recv, fields, ro, rw, do, dw,
    col_sem, rest_sem, e_send, e_recv, s_send, s_recv, g_send, g_recv, table_sem, round_sem,
):
    R, C, S, nr, nc = dims
    H, ndev = S // 2, nr * nc
    lo = H - 8
    T = S - lo
    my_row, my_col = lax.axis_index("row"), lax.axis_index("col")
    me = my_row * nc + my_col
    last_col, last_row = my_col == nc - 1, my_row == nr - 1

    turn_rows = [lax.rem(my_row + k, nr) for k in range(nr)]
    turn_cols = [lax.rem(my_col + k, nc) for k in range(nc)]
    others = [
        (turn_rows[a], turn_cols[b]) for a in range(nr) for b in range(nc) if a or b
    ]
    barrier = pltpu.get_barrier_semaphore()

    def signal(sem, row, col, there):
        @pl.when(there)
        def _():
            pl.semaphore_signal(sem, inc=1, device_id=(row, col), device_id_type=MESH)

    def await_all(sem, *due):
        amount = sum(one.astype(jnp.int32) for one in due)

        @pl.when(amount > 0)
        def _():
            pl.semaphore_wait(sem, amount)

    steps = doubling(my_row, nr, lambda k: (my_row + k, my_col))
    steps += doubling(my_col, nc, lambda k: (my_row, my_col + k))

    def tell(k):
        for row, col, there, _ in steps[k]:
            signal(round_sem.at[k], row, col, there)

    def spread(k):
        if k < len(steps):
            await_all(round_sem.at[k], *(here for _, _, _, here in steps[k]))
            if k + 1 < len(steps):
                tell(k + 1)

    cols = [
        pltpu.make_async_copy(
            patches.at[pl.ds(i * C * 2 * S, 2 * S)],
            pv.at[pl.ds(PAD + i * C * 2 * S, 2 * S)],
            col_sem.at[i],
        )
        for i in range(R)
    ]
    rests = [
        pltpu.make_async_copy(
            patches.at[pl.ds((i * C + 1) * 2 * S, (C - 1) * 2 * S)],
            pv.at[pl.ds(PAD + (i * C + 1) * 2 * S, (C - 1) * 2 * S)],
            rest_sem.at[i],
        )
        for i in range(R)
    ]
    tables = [
        pltpu.make_async_copy(here, there, table_sem.at[k])
        for k, (here, there) in enumerate(zip((ro_in, rw_in, do_in, dw_in), (ro, rw, do, dw)))
    ]
    for copy in cols:
        copy.start()
    signal(barrier, my_row + 1, my_col, my_row < nr - 1)
    signal(barrier, my_row, my_col + 1, my_col < nc - 1)
    for copy in tables:
        copy.start()
    for copy in rests:
        copy.start()
    lane = lax.broadcasted_iota(jnp.int32, (S, S), 1)

    def pack(i):
        base = PAD + i * C * 2 * S
        cols[i].wait()
        re = pv[pl.ds(base, S), :]
        im = pv[pl.ds(base + S, S), :]
        epack[pl.ds(i * S, S), :] = jnp.where(lane < H, re, pltpu.roll(im, H, 1))

    def south_copy(k, row):
        return pltpu.make_async_remote_copy(
            src_ref=patches.at[pl.ds(k * S, H)],
            dst_ref=south_recv.at[pl.ds(PAD + k * H, H)],
            send_sem=s_send.at[k],
            recv_sem=s_recv.at[k],
            device_id=(row, my_col),
            device_id_type=MESH,
        )

    def east_copy(k, col):
        return pltpu.make_async_remote_copy(
            src_ref=epack.at[pl.ds(k * S, S)],
            dst_ref=east_recv.at[pl.ds(k * S, S)],
            send_sem=e_send.at[k],
            recv_sem=e_recv.at[k],
            device_id=(my_row, col),
            device_id_type=MESH,
        )

    def send_east(i):
        @pl.when(my_col > 0)
        def _():
            east_copy(i, my_col - 1).start()

    for i in range(2):
        pack(i)
    await_all(barrier, my_row > 0, my_col > 0)
    for i in range(2):
        send_east(i)

    @pl.when(my_row > 0)
    def _():
        for k in range(2 * C):
            south_copy(k, my_row - 1).start()

    if steps:
        tell(0)
    for i in range(2, R):
        pack(i)
        send_east(i)
    acc[...] = jnp.zeros_like(acc)
    for copy in tables:
        copy.wait()
    for copy in rests:
        copy.wait()

    lane1 = lax.broadcasted_iota(jnp.int32, (1, S), 1)
    row8 = lax.broadcasted_iota(jnp.int32, (8, S), 0)

    def at(ref, row):
        return ref[pl.ds(pl.multiple_of(row, 8), 8), :]

    def put_at(ref, row, value):
        ref[pl.ds(pl.multiple_of(row, 8), 8), :] = value

    def put(plane, p, re, im, width):
        scale = 1.0 / jnp.sqrt(jnp.full((1, S), S * width, jnp.int32).astype(f32))
        acc[pl.ds(plane * R * C + p, 1), :] = fold_rows(re) * scale
        acc[pl.ds((plane + 1) * R * C + p, 1), :] = fold_rows(im) * scale

    def gathered(pieces):
        re, im = None, None
        for a_re, a_im, b_re, b_im in pieces:
            u, v = a_re * b_re + a_im * b_im, a_re * b_im - a_im * b_re
            re, im = (u, v) if re is None else (re + u, im + v)
        return re, im

    def weights(i, j, within):
        o, w = ro[i, j], rw[i, j]
        keep = (lane1 >= o) & (lane1 < o + w)
        live = keep if j < C - 1 else keep & jnp.logical_not(last_col)
        half = jnp.where(live, f32(0.5), f32(1.0))
        third = jnp.where(live, f32(1.0 / 3.0), f32(0.5))
        down = jnp.logical_not((i == R - 1) & last_row)
        third = jnp.where(jnp.full((1, S), down), third, half)
        if within:
            half, third = jnp.where(keep, half, 0.0), jnp.where(keep, third, 0.0)
        return jnp.broadcast_to(half, (8, S)), jnp.broadcast_to(third, (8, S))

    def reached(i, j, q):
        o, w = do[i, j], dw[i, j]
        return row8 >= o - q if q < S - 8 else row8 < o + w - q

    def weight_at(i, j, q, half, third):
        return half if q < lo else jnp.where(reached(i, j, q), third, half)

    def rows_of(p):
        return PAD + p * 2 * S

    def east_of(i, j):
        base = rows_of(i * C + j + 1)

        def load(q, o):
            return pltpu.roll(at(pv, base + q), o, 1), pltpu.roll(at(pv, base + S + q), o, 1)

        return load

    def east_rim(i):
        def load(q, o):
            both = at(east_recv, i * S + q)
            return pltpu.roll(both, o, 1), pltpu.roll(both, lax.rem(o + H, S), 1)

        return load

    def place_east(i, j, q, b, half, third):
        to = (i * C + j) * 2 * S + q
        weight = weight_at(i, j, q, half, third)
        put_at(ew, to, b[0] * weight)
        put_at(ew, to + S, b[1] * weight)

    def east_store(i, j, load, place):
        p = i * C + j
        o, w = ro[i, j], rw[i, j]
        base = rows_of(p)
        half, third = weights(i, j, True)

        def piece(q):
            b = load(q, o)
            if place:
                place_east(i, j, q, b, half, third)
            return (at(pv, base + q), at(pv, base + S + q)) + b

        re, im = gathered(piece(q) for q in range(0, S, 8))
        keep = (lane1 >= o) & (lane1 < o + w)
        put(0, p, jnp.where(keep, re, 0.0), jnp.where(keep, im, 0.0), w)

    def east_inner(i, carry):
        for j in range(C - 1):
            east_store(i, j, east_of(i, j), True)
        return carry

    def south_store(i, j, ref, start, gap):
        p = i * C + j
        o, w = do[i, j], dw[i, j]
        base = rows_of(p)
        _, third = weights(i, j, False)

        def piece(q):
            keep = reached(i, j, q)
            b_re = jnp.where(keep, ref[pl.ds(start + (q - o), 8), :], 0.0)
            b_im = jnp.where(keep, ref[pl.ds(start + gap + (q - o), 8), :], 0.0)
            to = p * 2 * T + q - lo
            put_at(sw, to, b_re * third)
            put_at(sw, to + T, b_im * third)
            return at(pv, base + q), at(pv, base + S + q), b_re, b_im

        re, im = gathered(piece(q) for q in range(lo, S, 8))
        put(2, p, re, im, w)

    def south_inner(i, carry):
        for j in range(C):
            south_store(i, j, pv, rows_of((i + 1) * C + j), S)
        return carry

    spread(0)
    lax.fori_loop(0, R // 2, east_inner, 0)
    spread(1)
    lax.fori_loop(R // 2, R, east_inner, 0)
    spread(2)
    lax.fori_loop(0, R // 2, south_inner, 0)
    spread(3)
    lax.fori_loop(R // 2, R - 1, south_inner, 0)
    spread(4)

    @pl.when(my_row < nr - 1)
    def _():
        for k in range(2 * C):
            south_copy(k, my_row).wait_recv()

    @pl.when(last_row)
    def _():
        south_recv[...] = jnp.zeros_like(south_recv)

    for j in range(C):
        south_store(R - 1, j, south_recv, PAD + j * 2 * H, H)

    for k in range(5, len(steps)):
        spread(k)

    @pl.when(last_col)
    def _():
        east_recv[...] = jnp.zeros_like(east_recv)

    for i in range(R):

        @pl.when(my_col < nc - 1)
        def _():
            east_copy(i, my_col).wait_recv()

        east_store(i, C - 1, east_rim(i), False)

    sums = lax.dot_general(
        jnp.ones((8, S), f32), acc[...], (((1,), (1,)), ((), ())),
        precision=highest, preferred_element_type=f32,
    )
    mine = jnp.concatenate([sums[0:1, :S], sums[0:1, S:]], axis=0)
    send_buf[...] = mine
    recv[me] = mine

    def index(d):
        return d[0] * nc + d[1]

    def gather_copy(target, source):
        return pltpu.make_async_remote_copy(
            src_ref=send_buf,
            dst_ref=recv.at[index(source)],
            send_sem=g_send.at[index(target)],
            recv_sem=g_recv.at[index(source)],
            device_id=target,
            device_id_type=MESH,
        )

    for other in others:
        gather_copy(other, (my_row, my_col)).start()

    def weigh(i, carry):
        for j in range(C):
            half, third = weights(i, j, False)
            base, to = rows_of(i * C + j), (i * C + j) * 2 * S
            for q in range(0, S, 8):
                weight = weight_at(i, j, q, half, third)
                put_at(aw, to + q, at(pv, base + q) * weight)
                put_at(aw, to + S + q, at(pv, base + S + q) * weight)
        half, third = weights(i, C - 1, True)
        load, o = east_rim(i), ro[i, C - 1]
        for q in range(0, S, 8):
            place_east(i, C - 1, q, load(q, o), half, third)
        return carry

    lax.fori_loop(0, R, weigh, 0)

    for other in others:
        gather_copy(other, other).wait_recv()

    got = recv[...]
    east, south = got[:, 0, :], got[:, 1, :]
    field = lax.broadcasted_iota(jnp.int32, (ndev, S), 0)
    slot = lax.broadcasted_iota(jnp.int32, (ndev, S), 1)
    valid = slot < R * C
    j_of, i_of = slot % C, (slot // C) % R
    dc, dr = field % nc, field // nc

    def roll(x, by, axis):
        return pltpu.roll(x, by % x.shape[axis], axis)

    def from_east(x):
        far = roll(roll(x, -1, 0), C - 1, 1)
        far = jnp.where(dc < nc - 1, far, 0.0)
        return jnp.where(j_of < C - 1, roll(x, -1, 1), far)

    def from_west(x):
        far = roll(roll(x, 1, 0), 1 - C, 1)
        far = jnp.where(dc > 0, far, 0.0)
        return jnp.where(j_of > 0, roll(x, 1, 1), far)

    def from_south(x):
        far = roll(roll(x, -nc, 0), (R - 1) * C, 1)
        far = jnp.where(dr < nr - 1, far, 0.0)
        return jnp.where(i_of < R - 1, roll(x, -C, 1), far)

    def from_north(x):
        far = roll(roll(x, nc, 0), -(R - 1) * C, 1)
        far = jnp.where(dr > 0, far, 0.0)
        return jnp.where(i_of > 0, roll(x, C, 1), far)

    ce = (jnp.where(valid, east, 0.0), jnp.where(valid, roll(east, -R * C, 1), 0.0))
    cs = (jnp.where(valid, south, 0.0), jnp.where(valid, roll(south, -R * C, 1), 0.0))
    cw = tuple(from_west(x) for x in ce)
    cn = tuple(from_north(x) for x in cs)
    mean = 1.0 / float(ndev * R * C)

    def times(a, b):
        return (a[0] * b[0] - a[1] * b[1], a[0] * b[1] + a[1] * b[0])

    def conj_times(a, b):
        return (a[0] * b[0] + a[1] * b[1], a[0] * b[1] - a[1] * b[0])

    now = (jnp.where(valid, f32(1.0), f32(0.0)), jnp.zeros((ndev, S), f32))
    square = jnp.zeros((ndev, S), f32)
    constant = 1.0
    for step in range(ITERS):
        terms = (
            times(ce, tuple(from_east(x) for x in now)),
            times(cs, tuple(from_south(x) for x in now)),
            conj_times(cw, tuple(from_west(x) for x in now)),
            conj_times(cn, tuple(from_north(x) for x in now)),
        )
        now = tuple(
            jnp.where(valid, terms[0][q] + terms[1][q] + terms[2][q] + terms[3][q], 0.0)
            for q in range(2)
        )
        square = eps_norm * square + (now[0] * now[0] + now[1] * now[1])
        constant = constant * eps_norm
    outs = now + tuple(from_east(x) for x in now) + tuple(from_south(x) for x in now)
    for q in range(6):
        fields[q] = outs[q]
    total = jnp.sum(jnp.sum(square, axis=0, keepdims=True), axis=1, keepdims=True)
    factor = 1.0 / jnp.sqrt(total * mean + constant)
    diagonal = lax.broadcasted_iota(jnp.int32, (R * C, S), 0) == lax.broadcasted_iota(
        jnp.int32, (R * C, S), 1
    )
    for q in range(6):
        row = fields[q, pl.ds(me, 1), :] * factor
        phase_out[q : q + 1, :] = row
        spot = jnp.where(diagonal, jnp.broadcast_to(row, (R * C, S)), 0.0)
        factors[q * R * C : (q + 1) * R * C, :] = jnp.broadcast_to(
            jnp.sum(spot, axis=1, keepdims=True), (R * C, S)
        )

    for other in others:
        gather_copy(other, (my_row, my_col)).wait_send()

    @pl.when(my_col > 0)
    def _():
        for k in range(R):
            east_copy(k, my_col - 1).wait_send()

    @pl.when(my_row > 0)
    def _():
        for k in range(2 * C):
            south_copy(k, my_row - 1).wait_send()


def blend_kernel(dims, aw, ew, sw, factors, phase, out, phases, ov, pad, out_sem, phase_sem):
    R, C, S, pair = dims
    lo = S // 2 - 8
    T = S - lo
    piece = pair * 2 * S

    def save(k):
        return pltpu.make_async_copy(
            ov.at[pl.ds(k * piece, piece)], out.at[pl.ds(k * piece, piece)], out_sem.at[k]
        )

    def at(ref, row):
        return ref[pl.ds(pl.multiple_of(row, 8), 8), :]

    def times(g, a):
        return g[0] * a[0] - g[1] * a[1], g[0] * a[1] + g[1] * a[0]

    def place(p):
        g, ge, gs = (
            [jnp.broadcast_to(factors[pl.ds((2 * k + part) * R * C + p, 1), :], (8, S)) for part in range(2)]
            for k in range(3)
        )
        base = p * 2 * S
        for q in range(0, S, 8):
            own = times(g, (at(aw, base + q), at(aw, base + S + q)))
            east = times(ge, (at(ew, base + q), at(ew, base + S + q)))
            sums = [own[part] + east[part] for part in range(2)]
            if q >= lo:
                down = p * 2 * T + q - lo
                south = times(gs, (at(sw, down), at(sw, down + T)))
                sums = [sums[part] + south[part] for part in range(2)]
            ov[pl.ds(pl.multiple_of(base + q, 8), 8), :] = sums[0]
            ov[pl.ds(pl.multiple_of(base + S + q, 8), 8), :] = sums[1]

    def step(k, carry):
        for n in range(pair):
            place(k * pair + n)
        save(k).start()
        return carry

    lax.fori_loop(0, R * C // pair, step, 0)

    row8 = lax.broadcasted_iota(jnp.int32, (R, S), 0)
    for part in range(2):
        line = jnp.broadcast_to(phase[part : part + 1, :], (R, S))
        plane = line
        for i in range(1, R):
            plane = jnp.where(row8 == i, pltpu.roll(line, S - i * C, 1), plane)
        pad[part] = plane[:, :C]
    send = pltpu.make_async_copy(pad, phases, phase_sem.at[0])
    send.start()
    for k in range(R * C // pair):
        save(k).wait()
    send.wait()


def local(nr, nc, patches, right_offset, right_width, down_offset, down_width):
    R, C, _, S, _ = patches.shape
    H, ndev = S // 2, nr * nc
    T = S - (H - 8)
    dims = (R, C, S, nr, nc)
    flat = patches.reshape(R * C * 2 * S, S)
    anyspec = pl.BlockSpec(memory_space=pl.ANY)
    vmem = pl.BlockSpec(memory_space=pltpu.VMEM)
    dma = pltpu.SemaphoreType.DMA
    tables = (right_offset, right_width, down_offset, down_width)
    parts = pl.pallas_call(
        functools.partial(sync_kernel, dims),
        out_shape=(
            pltpu.VMEM((R * C * 2 * S, S), f32),
            pltpu.VMEM((R * C * 2 * S, S), f32),
            pltpu.VMEM((R * C * 2 * T, S), f32),
            pltpu.VMEM((6 * R * C, S), f32),
            pltpu.VMEM((8, S), f32),
        ),
        in_specs=[pl.BlockSpec(memory_space=pltpu.HBM)] * 5,
        out_specs=(vmem,) * 5,
        scratch_shapes=[
            pltpu.VMEM((PAD + R * C * 2 * S, S), f32),
            pltpu.VMEM((R * S, S), f32),
            pltpu.VMEM((2 * PAD + 2 * C * H, S), f32),
            pltpu.VMEM((R * S, S), f32),
            pltpu.VMEM((4 * R * C, S), f32),
            pltpu.VMEM((2, S), f32),
            pltpu.VMEM((ndev, 2, S), f32),
            pltpu.VMEM((6, ndev, S), f32),
        ] + [pltpu.SMEM((R, C), jnp.int32)] * 4 + [
            dma((R,)), dma((R,)),
            dma((R,)), dma((R,)),
            dma((2 * C,)), dma((2 * C,)),
            dma((ndev,)), dma((ndev,)),
            dma((4,)),
            pltpu.SemaphoreType.REGULAR((n_rounds(nr) + n_rounds(nc),)),
        ],
        compiler_params=pltpu.CompilerParams(
            collective_id=0, has_side_effects=True, vmem_limit_bytes=24 << 20
        ),
        name="sync_patches",
    )(*(pltpu.with_memory_space_constraint(x, pltpu.HBM) for x in (flat, *tables)))
    pair = 2
    blended, phases = pl.pallas_call(
        functools.partial(blend_kernel, (R, C, S, pair)),
        out_shape=(
            jax.ShapeDtypeStruct((R * C * 2 * S, S), f32),
            jax.ShapeDtypeStruct((2, R, C), f32),
        ),
        in_specs=[vmem] * 5,
        out_specs=(anyspec, anyspec),
        scratch_shapes=[
            pltpu.VMEM((R * C * 2 * S, S), f32),
            pltpu.VMEM((2, R, C), f32),
            dma((R * C // pair,)),
            dma((1,)),
        ],
        compiler_params=pltpu.CompilerParams(vmem_limit_bytes=24 << 20),
        name="blend_patches",
    )(*parts)
    return blended.reshape(patches.shape), phases


def solution(mesh):
    return jax.shard_map(
        functools.partial(local, mesh.shape["row"], mesh.shape["col"]),
        mesh=mesh,
        in_specs=(P("row", "col", None, None, None),) + (P("row", "col"),) * 4,
        out_specs=(P("row", "col", None, None, None), P(None, "row", "col")),
        check_vma=False,
    )
```

```python
import functools

import jax
import jax.numpy as jnp
from jax import lax
from jax.experimental import pallas as pl
from jax.experimental.pallas import tpu as pltpu
from jax.sharding import PartitionSpec as P

ITERS = 2
PAD = 64
eps_norm = 1.0
highest = lax.Precision.HIGHEST
MESH = pl.DeviceIdType.MESH
f32 = jnp.float32


def fold_rows(x):
    return jnp.sum(x, axis=0, keepdims=True)


def doubling(pos, n, at):
    if n == 1:
        return []
    rounds = [[at(-1) + (pos > 0, pos < n - 1)]]
    known = 1
    while known < n - 1:
        rounds.append([
            at(-known) + (pos >= known, pos < n - known),
            at(known) + (pos < n - known, pos >= known),
        ])
        known *= 2
    return rounds


def groups(n, sizes):
    runs, first = [], 0
    while first < n:
        size = sizes[min(len(runs), len(sizes) - 1)]
        runs.append(range(first, min(n, first + size)))
        first += size
    return runs


def load_groups(n):
    return groups(n, (1, 1, 2, 4))


def arrive_groups(n):
    tail = min(n, 4)
    return groups(n - tail, (4,)) + [range(n - tail + k, n - tail + k + 1) for k in range(tail)]


def n_rounds(n):
    return len(doubling(0, n, lambda k: (0, 0)))


def sync_kernel(
    dims, patches, ro_in, rw_in, do_in, dw_in, aw, ew, sw, factors, phase_out,
    pv, east_recv, south_recv,
    epack, acc, send_buf, recv, fields, table,
    col_sem, rest_sem, e_send, e_recv, s_send, s_recv, g_send, g_recv, table_sem, round_sem,
):
    R, C, S, nr, nc = dims
    H, ndev = S // 2, nr * nc
    lo = H - 8
    T = S - lo
    my_row, my_col = lax.axis_index("row"), lax.axis_index("col")
    me = my_row * nc + my_col
    last_col, last_row = my_col == nc - 1, my_row == nr - 1

    low = my_col < nc // 2
    turn_rows = [lax.rem(my_row + k, nr) for k in range(nr)]
    turn_cols = [lax.rem(my_col + jnp.where(low, nc - k, k), nc) for k in range(nc)]
    others = [
        (turn_rows[a], turn_cols[b])
        for b in [*range(1, nc), 0]
        for a in [*range(1, nr), 0]
        if a or b
    ]
    barrier = pltpu.get_barrier_semaphore()

    def signal(sem, row, col, there):
        @pl.when(there)
        def _():
            pl.semaphore_signal(sem, inc=1, device_id=(row, col), device_id_type=MESH)

    def await_all(sem, *due):
        amount = sum(one.astype(jnp.int32) for one in due)

        @pl.when(amount > 0)
        def _():
            pl.semaphore_wait(sem, amount)

    steps = doubling(my_row, nr, lambda k: (my_row + k, my_col))
    steps += doubling(my_col, nc, lambda k: (my_row, my_col + k))

    def tell(k):
        for row, col, there, _ in steps[k]:
            signal(round_sem.at[k], row, col, there)

    def spread(k):
        if k < len(steps):
            await_all(round_sem.at[k], *(here for _, _, _, here in steps[k]))
            if k + 1 < len(steps):
                tell(k + 1)

    load_sem = {i: g for g, run in enumerate(load_groups(R)) for i in run}
    cols = [
        pltpu.make_async_copy(
            patches.at[pl.ds(i * C * 2 * S, 2 * S)],
            pv.at[pl.ds(PAD + i * C * 2 * S, 2 * S)],
            col_sem.at[load_sem[i]],
        )
        for i in range(R)
    ]
    rests = [
        pltpu.make_async_copy(
            patches.at[pl.ds((i * C + 1) * 2 * S, (C - 1) * 2 * S)],
            pv.at[pl.ds(PAD + (i * C + 1) * 2 * S, (C - 1) * 2 * S)],
            rest_sem.at[0],
        )
        for i in range(R)
    ]
    tables = [
        pltpu.make_async_copy(here, table.at[k], table_sem.at[0])
        for k, here in enumerate((ro_in, rw_in, do_in, dw_in))
    ]
    ro, rw, do, dw = (table.at[k] for k in range(4))

    def whole(src, dst, sem):
        return pltpu.make_async_copy(src, dst, sem)

    for copy in cols:
        copy.start()
    signal(barrier, my_row, my_col + 1, my_col < nc - 1)
    signal(barrier, my_row + 1, my_col, my_row < nr - 1)
    lane = lax.broadcasted_iota(jnp.int32, (S, S), 1)

    def load(g):
        size = len(load_groups(R)[g]) * 2 * S
        whole(patches.at[pl.ds(0, size)], pv.at[pl.ds(PAD, size)], col_sem.at[g]).wait()

    def pack(i):
        base = PAD + i * C * 2 * S
        re = pv[pl.ds(base, S), :]
        im = pv[pl.ds(base + S, S), :]
        epack[pl.ds(i * S, S), :] = jnp.where(lane < H, re, pltpu.roll(im, H, 1))

    def south_copy(k, row):
        return pltpu.make_async_remote_copy(
            src_ref=patches.at[pl.ds(k * S, H)],
            dst_ref=south_recv.at[pl.ds(PAD + k * H, H)],
            send_sem=s_send.at[0],
            recv_sem=s_recv.at[0],
            device_id=(row, my_col),
            device_id_type=MESH,
        )

    def all_south(row):
        return pltpu.make_async_remote_copy(
            src_ref=patches.at[pl.ds(0, 2 * C * H)],
            dst_ref=south_recv.at[pl.ds(PAD, 2 * C * H)],
            send_sem=s_send.at[0],
            recv_sem=s_recv.at[0],
            device_id=(row, my_col),
            device_id_type=MESH,
        )

    arrive_sem = {i: g for g, run in enumerate(arrive_groups(R)) for i in run}

    def east_run(first, n, sem, col):
        return pltpu.make_async_remote_copy(
            src_ref=epack.at[pl.ds(first * S, n * S)],
            dst_ref=east_recv.at[pl.ds(first * S, n * S)],
            send_sem=e_send.at[0],
            recv_sem=e_recv.at[sem],
            device_id=(my_row, col),
            device_id_type=MESH,
        )

    def east_copy(k, col):
        return east_run(k, 1, arrive_sem[k], col)

    def send_east(i):
        @pl.when(my_col > 0)
        def _():
            east_copy(i, my_col - 1).start()

    load(0)
    for copy in tables:
        copy.start()
    for copy in rests:
        copy.start()
    pack(0)
    await_all(barrier, my_row > 0, my_col > 0)
    send_east(0)
    for g, run in enumerate(load_groups(R)):
        if g:
            load(g)
            for i in run:
                pack(i)
                send_east(i)
        if g == 1 or len(load_groups(R)) == 1:

            @pl.when(my_row > 0)
            def _():
                for k in range(2 * C):
                    south_copy(k, my_row - 1).start()

            if steps:
                tell(0)
    acc[...] = jnp.zeros_like(acc)
    whole(table, table, table_sem.at[0]).wait()
    size = R * (C - 1) * 2 * S
    whole(patches.at[pl.ds(0, size)], pv.at[pl.ds(PAD, size)], rest_sem.at[0]).wait()

    lane1 = lax.broadcasted_iota(jnp.int32, (1, S), 1)
    row8 = lax.broadcasted_iota(jnp.int32, (8, S), 0)

    def at(ref, row):
        return ref[pl.ds(pl.multiple_of(row, 8), 8), :]

    def put_at(ref, row, value):
        ref[pl.ds(pl.multiple_of(row, 8), 8), :] = value

    def scaled(re, im, width):
        scale = 1.0 / jnp.sqrt(jnp.full((1, S), S * width, jnp.int32).astype(f32))
        return fold_rows(re) * scale, fold_rows(im) * scale

    def put(plane, p, re, im, width):
        re, im = scaled(re, im, width)
        acc[pl.ds(plane * R * C + p, 1), :] = re
        acc[pl.ds((plane + 1) * R * C + p, 1), :] = im

    def gathered(pieces):
        re, im = None, None
        for a_re, a_im, b_re, b_im in pieces:
            u, v = a_re * b_re + a_im * b_im, a_re * b_im - a_im * b_re
            re, im = (u, v) if re is None else (re + u, im + v)
        return re, im

    def weights(i, j, within):
        o, w = ro[i, j], rw[i, j]
        keep = (lane1 >= o) & (lane1 < o + w)
        live = keep if j < C - 1 else keep & jnp.logical_not(last_col)
        half = jnp.where(live, f32(0.5), f32(1.0))
        third = jnp.where(live, f32(1.0 / 3.0), f32(0.5))
        down = jnp.logical_not((i == R - 1) & last_row)
        third = jnp.where(jnp.full((1, S), down), third, half)
        if within:
            half, third = jnp.where(keep, half, 0.0), jnp.where(keep, third, 0.0)
        return jnp.broadcast_to(half, (8, S)), jnp.broadcast_to(third, (8, S))

    def reached(i, j, q):
        o, w = do[i, j], dw[i, j]
        return row8 >= o - q if q < S - 8 else row8 < o + w - q

    def weight_at(i, j, q, half, third):
        return half if q < lo else jnp.where(reached(i, j, q), third, half)

    def rows_of(p):
        return PAD + p * 2 * S

    def east_of(i, j):
        base = rows_of(i * C + j + 1)

        def load(q, o):
            return pltpu.roll(at(pv, base + q), o, 1), pltpu.roll(at(pv, base + S + q), o, 1)

        return load

    def east_rim(i):
        def load(q, o):
            both = at(east_recv, i * S + q)
            return pltpu.roll(both, o, 1), pltpu.roll(both, lax.rem(o + H, S), 1)

        return load

    def place_east(i, j, q, b, half, third):
        to = (i * C + j) * 2 * S + q
        weight = weight_at(i, j, q, half, third)
        put_at(ew, to, b[0] * weight)
        put_at(ew, to + S, b[1] * weight)

    def east_sums(i, j, load, place):
        p = i * C + j
        o, w = ro[i, j], rw[i, j]
        base = rows_of(p)
        half, third = weights(i, j, True)

        def piece(q):
            b = load(q, o)
            if place:
                place_east(i, j, q, b, half, third)
            return (at(pv, base + q), at(pv, base + S + q)) + b

        re, im = gathered(piece(q) for q in range(0, S, 8))
        keep = (lane1 >= o) & (lane1 < o + w)
        return p, jnp.where(keep, re, 0.0), jnp.where(keep, im, 0.0), w

    def east_inner(i, carry):
        for j in range(C - 1):
            put(0, *east_sums(i, j, east_of(i, j), True))
        return carry

    def south_store(i, j, ref, start, gap):
        p = i * C + j
        o, w = do[i, j], dw[i, j]
        base = rows_of(p)
        _, third = weights(i, j, False)

        def piece(q):
            keep = reached(i, j, q)
            b_re = jnp.where(keep, ref[pl.ds(start + (q - o), 8), :], 0.0)
            b_im = jnp.where(keep, ref[pl.ds(start + gap + (q - o), 8), :], 0.0)
            to = p * 2 * T + q - lo
            put_at(sw, to, b_re * third)
            put_at(sw, to + T, b_im * third)
            return at(pv, base + q), at(pv, base + S + q), b_re, b_im

        re, im = gathered(piece(q) for q in range(lo, S, 8))
        put(2, p, re, im, w)

    def south_inner(i, carry):
        for j in range(C):
            south_store(i, j, pv, rows_of((i + 1) * C + j), S)
        return carry

    spread(0)
    lax.fori_loop(0, R // 2, east_inner, 0)
    spread(1)
    lax.fori_loop(R // 2, R, east_inner, 0)
    spread(2)
    lax.fori_loop(0, R // 2, south_inner, 0)
    spread(3)
    lax.fori_loop(R // 2, R - 1, south_inner, 0)
    spread(4)

    @pl.when(my_row < nr - 1)
    def _():
        all_south(my_row).wait_recv()

    @pl.when(last_row)
    def _():
        south_recv[...] = jnp.zeros_like(south_recv)

    for j in range(C):
        south_store(R - 1, j, south_recv, PAD + j * 2 * H, H)

    for k in range(5, len(steps)):
        spread(k)

    @pl.when(last_col)
    def _():
        east_recv[...] = jnp.zeros_like(east_recv)

    def east_arrive(g):
        run = arrive_groups(R)[g]

        @pl.when(my_col < nc - 1)
        def _():
            east_run(run[0], len(run), g, my_col).wait_recv()

        return run

    last = len(arrive_groups(R)) - 1
    for g in range(last):
        for i in east_arrive(g):
            put(0, *east_sums(i, C - 1, east_rim(i), False))

    sums = lax.dot_general(
        jnp.ones((8, S), f32), acc[...], (((1,), (1,)), ((), ())),
        precision=highest, preferred_element_type=f32,
    )
    east_row = sums[0:1, :S]
    for i in east_arrive(last):
        p, re, im, width = east_sums(i, C - 1, east_rim(i), False)
        re, im = (jnp.sum(x, axis=1, keepdims=True) for x in scaled(re, im, width))
        east_row = jnp.where(lane1 == p, re, jnp.where(lane1 == R * C + p, im, east_row))
    mine = jnp.concatenate([east_row, sums[0:1, S:]], axis=0)
    send_buf[...] = mine
    recv[me] = mine

    def index(d):
        return d[0] * nc + d[1]

    def gather_copy(target, source):
        return pltpu.make_async_remote_copy(
            src_ref=send_buf,
            dst_ref=recv.at[index(source)],
            send_sem=g_send.at[0],
            recv_sem=g_recv.at[0],
            device_id=target,
            device_id_type=MESH,
        )

    def all_gathered():
        return pltpu.make_async_remote_copy(
            src_ref=recv.at[pl.ds(0, ndev - 1)],
            dst_ref=recv.at[pl.ds(0, ndev - 1)],
            send_sem=g_send.at[0],
            recv_sem=g_recv.at[0],
            device_id=others[0],
            device_id_type=MESH,
        )

    for other in others:
        gather_copy(other, (my_row, my_col)).start()

    def weigh(i, carry):
        for j in range(C):
            half, third = weights(i, j, False)
            base, to = rows_of(i * C + j), (i * C + j) * 2 * S
            for q in range(0, S, 8):
                weight = weight_at(i, j, q, half, third)
                put_at(aw, to + q, at(pv, base + q) * weight)
                put_at(aw, to + S + q, at(pv, base + S + q) * weight)
        half, third = weights(i, C - 1, True)
        load, o = east_rim(i), ro[i, C - 1]
        for q in range(0, S, 8):
            place_east(i, C - 1, q, load(q, o), half, third)
        return carry

    lax.fori_loop(0, R, weigh, 0)

    all_gathered().wait_recv()

    got = recv[...]
    east, south = got[:, 0, :], got[:, 1, :]
    field = lax.broadcasted_iota(jnp.int32, (ndev, S), 0)
    slot = lax.broadcasted_iota(jnp.int32, (ndev, S), 1)
    valid = slot < R * C
    j_of, i_of = slot % C, (slot // C) % R
    dc, dr = field % nc, field // nc

    def roll(x, by, axis):
        return pltpu.roll(x, by % x.shape[axis], axis)

    def from_east(x):
        far = roll(roll(x, -1, 0), C - 1, 1)
        far = jnp.where(dc < nc - 1, far, 0.0)
        return jnp.where(j_of < C - 1, roll(x, -1, 1), far)

    def from_west(x):
        far = roll(roll(x, 1, 0), 1 - C, 1)
        far = jnp.where(dc > 0, far, 0.0)
        return jnp.where(j_of > 0, roll(x, 1, 1), far)

    def from_south(x):
        far = roll(roll(x, -nc, 0), (R - 1) * C, 1)
        far = jnp.where(dr < nr - 1, far, 0.0)
        return jnp.where(i_of < R - 1, roll(x, -C, 1), far)

    def from_north(x):
        far = roll(roll(x, nc, 0), -(R - 1) * C, 1)
        far = jnp.where(dr > 0, far, 0.0)
        return jnp.where(i_of > 0, roll(x, C, 1), far)

    ce = (jnp.where(valid, east, 0.0), jnp.where(valid, roll(east, -R * C, 1), 0.0))
    cs = (jnp.where(valid, south, 0.0), jnp.where(valid, roll(south, -R * C, 1), 0.0))
    cw = tuple(from_west(x) for x in ce)
    cn = tuple(from_north(x) for x in cs)
    mean = 1.0 / float(ndev * R * C)

    def times(a, b):
        return (a[0] * b[0] - a[1] * b[1], a[0] * b[1] + a[1] * b[0])

    def conj_times(a, b):
        return (a[0] * b[0] + a[1] * b[1], a[0] * b[1] - a[1] * b[0])

    now = (ce[0] + cs[0] + cw[0] + cn[0], ce[1] + cs[1] - cw[1] - cn[1])
    now = tuple(jnp.where(valid, x, 0.0) for x in now)
    square = now[0] * now[0] + now[1] * now[1]
    constant = eps_norm
    for step in range(1, ITERS):
        terms = (
            times(ce, tuple(from_east(x) for x in now)),
            times(cs, tuple(from_south(x) for x in now)),
            conj_times(cw, tuple(from_west(x) for x in now)),
            conj_times(cn, tuple(from_north(x) for x in now)),
        )
        now = tuple(
            jnp.where(valid, terms[0][q] + terms[1][q] + terms[2][q] + terms[3][q], 0.0)
            for q in range(2)
        )
        square = eps_norm * square + (now[0] * now[0] + now[1] * now[1])
        constant = constant * eps_norm
    outs = now + tuple(from_east(x) for x in now) + tuple(from_south(x) for x in now)
    for q in range(6):
        fields[q] = outs[q]
    total = jnp.sum(jnp.sum(square, axis=0, keepdims=True), axis=1, keepdims=True)
    factor = 1.0 / jnp.sqrt(total * mean + constant)
    diagonal = lax.broadcasted_iota(jnp.int32, (R * C, S), 0) == lax.broadcasted_iota(
        jnp.int32, (R * C, S), 1
    )
    for q in range(6):
        row = fields[q, pl.ds(me, 1), :] * factor
        phase_out[q : q + 1, :] = row
        spot = jnp.where(diagonal, jnp.broadcast_to(row, (R * C, S)), 0.0)
        factors[q * R * C : (q + 1) * R * C, :] = jnp.broadcast_to(
            jnp.sum(spot, axis=1, keepdims=True), (R * C, S)
        )

    all_gathered().wait_send()

    @pl.when(my_col > 0)
    def _():
        east_run(0, R, 0, my_col - 1).wait_send()

    @pl.when(my_row > 0)
    def _():
        all_south(my_row - 1).wait_send()


def blend_kernel(dims, aw, ew, sw, factors, phase, out, phases, ov, pad, out_sem, phase_sem):
    R, C, S, pair = dims
    lo = S // 2 - 8
    T = S - lo
    piece = pair * 2 * S

    def save(k):
        return pltpu.make_async_copy(
            ov.at[pl.ds(k * piece, piece)], out.at[pl.ds(k * piece, piece)], out_sem.at[0]
        )

    def at(ref, row):
        return ref[pl.ds(pl.multiple_of(row, 8), 8), :]

    def times(g, a):
        return g[0] * a[0] - g[1] * a[1], g[0] * a[1] + g[1] * a[0]

    def place(p):
        g, ge, gs = (
            [jnp.broadcast_to(factors[pl.ds((2 * k + part) * R * C + p, 1), :], (8, S)) for part in range(2)]
            for k in range(3)
        )
        base = p * 2 * S
        for q in range(0, S, 8):
            own = times(g, (at(aw, base + q), at(aw, base + S + q)))
            east = times(ge, (at(ew, base + q), at(ew, base + S + q)))
            sums = [own[part] + east[part] for part in range(2)]
            if q >= lo:
                down = p * 2 * T + q - lo
                south = times(gs, (at(sw, down), at(sw, down + T)))
                sums = [sums[part] + south[part] for part in range(2)]
            ov[pl.ds(pl.multiple_of(base + q, 8), 8), :] = sums[0]
            ov[pl.ds(pl.multiple_of(base + S + q, 8), 8), :] = sums[1]

    def step(k, carry):
        for n in range(pair):
            place(k * pair + n)
        save(k).start()
        return carry

    lax.fori_loop(0, R * C // pair, step, 0)

    row8 = lax.broadcasted_iota(jnp.int32, (R, S), 0)
    for part in range(2):
        line = jnp.broadcast_to(phase[part : part + 1, :], (R, S))
        plane = line
        for i in range(1, R):
            plane = jnp.where(row8 == i, pltpu.roll(line, S - i * C, 1), plane)
        pad[part] = plane[:, :C]
    send = pltpu.make_async_copy(pad, phases, phase_sem.at[0])
    send.start()
    send.wait()
    pltpu.make_async_copy(ov, out, out_sem.at[0]).wait()


def local(nr, nc, patches, right_offset, right_width, down_offset, down_width):
    R, C, _, S, _ = patches.shape
    H, ndev = S // 2, nr * nc
    T = S - (H - 8)
    dims = (R, C, S, nr, nc)
    flat = patches.reshape(R * C * 2 * S, S)
    anyspec = pl.BlockSpec(memory_space=pl.ANY)
    vmem = pl.BlockSpec(memory_space=pltpu.VMEM)
    dma = pltpu.SemaphoreType.DMA
    tables = (right_offset, right_width, down_offset, down_width)
    parts = pl.pallas_call(
        functools.partial(sync_kernel, dims),
        out_shape=(
            pltpu.VMEM((R * C * 2 * S, S), f32),
            pltpu.VMEM((R * C * 2 * S, S), f32),
            pltpu.VMEM((R * C * 2 * T, S), f32),
            pltpu.VMEM((6 * R * C, S), f32),
            pltpu.VMEM((8, S), f32),
        ),
        in_specs=[pl.BlockSpec(memory_space=pltpu.HBM)] * 5,
        out_specs=(vmem,) * 5,
        scratch_shapes=[
            pltpu.VMEM((PAD + R * C * 2 * S, S), f32),
            pltpu.VMEM((R * S, S), f32),
            pltpu.VMEM((2 * PAD + 2 * C * H, S), f32),
            pltpu.VMEM((R * S, S), f32),
            pltpu.VMEM((4 * R * C, S), f32),
            pltpu.VMEM((2, S), f32),
            pltpu.VMEM((ndev, 2, S), f32),
            pltpu.VMEM((6, ndev, S), f32),
            pltpu.SMEM((4, R, C), jnp.int32),
            dma((len(load_groups(R)),)), dma((1,)),
            dma((1,)), dma((len(arrive_groups(R)),)),
            dma((1,)), dma((1,)),
            dma((1,)), dma((1,)),
            dma((1,)),
            pltpu.SemaphoreType.REGULAR((n_rounds(nr) + n_rounds(nc),)),
        ],
        compiler_params=pltpu.CompilerParams(
            collective_id=0, has_side_effects=True, vmem_limit_bytes=24 << 20
        ),
        name="sync_patches",
    )(*(pltpu.with_memory_space_constraint(x, pltpu.HBM) for x in (flat, *tables)))
    pair = 2
    blended, phases = pl.pallas_call(
        functools.partial(blend_kernel, (R, C, S, pair)),
        out_shape=(
            jax.ShapeDtypeStruct((R * C * 2 * S, S), f32),
            jax.ShapeDtypeStruct((2, R, C), f32),
        ),
        in_specs=[vmem] * 5,
        out_specs=(anyspec, anyspec),
        scratch_shapes=[
            pltpu.VMEM((R * C * 2 * S, S), f32),
            pltpu.VMEM((2, R, C), f32),
            dma((1,)),
            dma((1,)),
        ],
        compiler_params=pltpu.CompilerParams(vmem_limit_bytes=24 << 20),
        name="blend_patches",
    )(*parts)
    return blended.reshape(patches.shape), phases


def solution(mesh):
    return jax.shard_map(
        functools.partial(local, mesh.shape["row"], mesh.shape["col"]),
        mesh=mesh,
        in_specs=(P("row", "col", None, None, None),) + (P("row", "col"),) * 4,
        out_specs=(P("row", "col", None, None, None), P(None, "row", "col")),
        check_vma=False,
    )
```

```python
import functools

import jax
import jax.numpy as jnp
from jax import lax
from jax.experimental import pallas as pl
from jax.experimental.pallas import tpu as pltpu
from jax.sharding import PartitionSpec as P

ITERS = 2
PAD = 64
eps_norm = 1.0
highest = lax.Precision.HIGHEST
MESH = pl.DeviceIdType.MESH
f32 = jnp.float32


def fold_rows(x):
    return jnp.sum(x, axis=0, keepdims=True)


def doubling(pos, n, at):
    if n == 1:
        return []
    rounds = [[at(-1) + (pos > 0, pos < n - 1)]]
    known = 1
    while known < n - 1:
        rounds.append([
            at(-known) + (pos >= known, pos < n - known),
            at(known) + (pos < n - known, pos >= known),
        ])
        known *= 2
    return rounds


def groups(n, sizes):
    runs, first = [], 0
    while first < n:
        size = sizes[min(len(runs), len(sizes) - 1)]
        runs.append(range(first, min(n, first + size)))
        first += size
    return runs


def load_groups(n):
    return groups(n, (1, 1, 2, 4))


def arrive_groups(n):
    tail = min(n, 4)
    return groups(n - tail, (4,)) + [range(n - tail + k, n - tail + k + 1) for k in range(tail)]


def n_rounds(n):
    return len(doubling(0, n, lambda k: (0, 0)))


def sync_kernel(
    dims, patches, ro_in, rw_in, do_in, dw_in, aw, ew, sw, factors, phase_out,
    pv, east_recv, south_recv,
    epack, acc, send_buf, recv, fields, table, relay_buf, strips, turned, late,
    col_sem, rest_sem, e_send, e_recv, s_send, s_recv, g_send, g_recv, table_sem, round_sem,
    relay_recv, relay_send, turn_recv, turn_send, pair_sem,
):
    R, C, S, nr, nc = dims
    H, ndev = S // 2, nr * nc
    lo = H - 8
    T = S - lo
    my_row, my_col = lax.axis_index("row"), lax.axis_index("col")
    me = my_row * nc + my_col
    last_col, last_row = my_col == nc - 1, my_row == nr - 1
    even = lax.rem(my_col, 2) == 0
    opens = even & (my_col >= 2) & (my_col < nc - 1)
    closes = jnp.logical_not(even) & (my_col >= 3)
    n_relay, n_turn = R // 2, min(2, R)

    def relayed(c):
        return jnp.clip(c - 2, 0, n_relay)

    def turned_of(c):
        return jnp.where(c == nc - 2, n_turn, 1)

    def sent_around(i):
        return opens & (i >= R - relayed(my_col))

    def turned_here(i):
        return opens & (i >= R - turned_of(my_col))

    low = my_col < nc // 2
    turn_rows = [lax.rem(my_row + k, nr) for k in range(nr)]
    turn_cols = [lax.rem(my_col + jnp.where(low, nc - k, k), nc) for k in range(nc)]
    others = [
        (turn_rows[a], turn_cols[b])
        for b in [*range(1, nc), 0]
        for a in [*range(1, nr), 0]
        if a or b
    ]
    barrier = pltpu.get_barrier_semaphore()

    def signal(sem, row, col, there):
        @pl.when(there)
        def _():
            pl.semaphore_signal(sem, inc=1, device_id=(row, col), device_id_type=MESH)

    def await_all(sem, *due):
        amount = sum(one.astype(jnp.int32) for one in due)

        @pl.when(amount > 0)
        def _():
            pl.semaphore_wait(sem, amount)

    steps = doubling(my_row, nr, lambda k: (my_row + k, my_col))
    steps += doubling(my_col, nc, lambda k: (my_row, my_col + k))

    def tell(k):
        for row, col, there, _ in steps[k]:
            signal(round_sem.at[k], row, col, there)

    def spread(k):
        if k < len(steps):
            await_all(round_sem.at[k], *(here for _, _, _, here in steps[k]))
            if k + 1 < len(steps):
                tell(k + 1)

    load_sem = {i: g for g, run in enumerate(load_groups(R)) for i in run}
    cols = [
        pltpu.make_async_copy(
            patches.at[pl.ds(i * C * 2 * S, 2 * S)],
            pv.at[pl.ds(PAD + i * C * 2 * S, 2 * S)],
            col_sem.at[load_sem[i]],
        )
        for i in range(R)
    ]
    rests = [
        pltpu.make_async_copy(
            patches.at[pl.ds((i * C + 1) * 2 * S, (C - 1) * 2 * S)],
            pv.at[pl.ds(PAD + (i * C + 1) * 2 * S, (C - 1) * 2 * S)],
            rest_sem.at[0],
        )
        for i in range(R)
    ]
    tables = [
        pltpu.make_async_copy(here, table.at[k], table_sem.at[0])
        for k, here in enumerate((ro_in, rw_in, do_in, dw_in))
    ]
    ro, rw, do, dw = (table.at[k] for k in range(4))

    def whole(src, dst, sem):
        return pltpu.make_async_copy(src, dst, sem)

    for copy in cols:
        copy.start()
    signal(barrier, my_row, my_col + 1, my_col < nc - 1)
    signal(barrier, my_row + 1, my_col, my_row < nr - 1)
    lane = lax.broadcasted_iota(jnp.int32, (S, S), 1)

    def load(g):
        size = len(load_groups(R)[g]) * 2 * S
        whole(patches.at[pl.ds(0, size)], pv.at[pl.ds(PAD, size)], col_sem.at[g]).wait()

    def pack(i):
        base = PAD + i * C * 2 * S
        re = pv[pl.ds(base, S), :]
        im = pv[pl.ds(base + S, S), :]
        epack[pl.ds(i * S, S), :] = jnp.where(lane < H, re, pltpu.roll(im, H, 1))

    def south_copy(k, row):
        return pltpu.make_async_remote_copy(
            src_ref=patches.at[pl.ds(k * S, H)],
            dst_ref=south_recv.at[pl.ds(PAD + k * H, H)],
            send_sem=s_send.at[0],
            recv_sem=s_recv.at[0],
            device_id=(row, my_col),
            device_id_type=MESH,
        )

    def all_south(row):
        return pltpu.make_async_remote_copy(
            src_ref=patches.at[pl.ds(0, 2 * C * H)],
            dst_ref=south_recv.at[pl.ds(PAD, 2 * C * H)],
            send_sem=s_send.at[0],
            recv_sem=s_recv.at[0],
            device_id=(row, my_col),
            device_id_type=MESH,
        )

    arrive_sem = {i: g for g, run in enumerate(arrive_groups(R)) for i in run}

    def east_run(first, n, sem, col):
        return pltpu.make_async_remote_copy(
            src_ref=epack.at[pl.ds(first * S, n * S)],
            dst_ref=east_recv.at[pl.ds(first * S, n * S)],
            send_sem=e_send.at[0],
            recv_sem=e_recv.at[sem],
            device_id=(my_row, col),
            device_id_type=MESH,
        )

    def east_copy(k, col):
        return east_run(k, 1, arrive_sem[k], col)

    def send_east(i):
        @pl.when((my_col > 0) & jnp.logical_not(sent_around(i)) if i >= R - n_relay else my_col > 0)
        def _():
            east_copy(i, my_col - 1).start()

    def relay_copy(i, col):
        k = i - (R - n_relay)
        return pltpu.make_async_remote_copy(
            src_ref=epack.at[pl.ds(i * S, S)],
            dst_ref=relay_buf.at[pl.ds(k * S, S)],
            send_sem=e_send.at[0],
            recv_sem=relay_recv.at[k],
            device_id=(my_row, col),
            device_id_type=MESH,
        )

    def forward_copy(i, col):
        k = i - (R - n_relay)
        return pltpu.make_async_remote_copy(
            src_ref=relay_buf.at[pl.ds(k * S, S)],
            dst_ref=east_recv.at[pl.ds(i * S, S)],
            send_sem=relay_send.at[k],
            recv_sem=e_recv.at[arrive_sem[i]],
            device_id=(my_row, col),
            device_id_type=MESH,
        )

    def forwards(i):
        return closes & (i >= R - relayed(my_col - 1))

    def forward(i):
        if i < R:

            @pl.when(forwards(i))
            def _():
                relay_copy(i, my_col).wait_recv()
                forward_copy(i, my_col - 2).start()

    def turn_copy(i, col):
        k = i - (R - n_turn)
        return pltpu.make_async_remote_copy(
            src_ref=strips.at[pl.ds(k * S, S)],
            dst_ref=turned.at[pl.ds(k * S, S)],
            send_sem=turn_send.at[k],
            recv_sem=turn_recv.at[k],
            device_id=(my_row, col),
            device_id_type=MESH,
        )

    load(0)
    for copy in tables:
        copy.start()
    for copy in rests:
        copy.start()
    pack(0)
    await_all(barrier, my_row > 0, my_col > 0)
    send_east(0)
    signal(pair_sem.at[0], my_row, my_col - 1, closes)
    for g, run in enumerate(load_groups(R)):
        if g:
            load(g)
            for i in run:
                pack(i)
                send_east(i)
        if g == 1 or len(load_groups(R)) == 1:

            @pl.when(my_row > 0)
            def _():
                for k in range(2 * C):
                    south_copy(k, my_row - 1).start()

            if steps:
                tell(0)
    acc[...] = jnp.zeros_like(acc)
    late[...] = jnp.zeros_like(late)
    await_all(pair_sem.at[0], opens)
    for i in range(R - n_relay, R):

        @pl.when(sent_around(i))
        def _():
            relay_copy(i, my_col + 1).start()

    spread(0)
    whole(table, table, table_sem.at[0]).wait()
    size = R * (C - 1) * 2 * S
    whole(patches.at[pl.ds(0, size)], pv.at[pl.ds(PAD, size)], rest_sem.at[0]).wait()

    lane1 = lax.broadcasted_iota(jnp.int32, (1, S), 1)
    row8 = lax.broadcasted_iota(jnp.int32, (8, S), 0)

    for i in range(R - n_turn, R):

        @pl.when(turned_here(i))
        def _():
            o, w = ro[i, C - 1], rw[i, C - 1]
            base = PAD + (i * C + C - 1) * 2 * S
            scale = 1.0 / jnp.sqrt(jnp.full((1, S), S * w, jnp.int32).astype(f32))
            weight = jnp.where((lane1 & (H - 1)) < w, scale, 0.0)
            re = pltpu.roll(pv[pl.ds(base, S), :], S - o, 1)
            im = pltpu.roll(pv[pl.ds(base + S, S), :], lax.rem(S + H - o, S), 1)
            strips[pl.ds((i - R + n_turn) * S, S), :] = jnp.where(lane < H, re, im) * weight
            turn_copy(i, my_col + 1).start()

    def at(ref, row):
        return ref[pl.ds(pl.multiple_of(row, 8), 8), :]

    def put_at(ref, row, value):
        ref[pl.ds(pl.multiple_of(row, 8), 8), :] = value

    def scaled(re, im, width):
        scale = 1.0 / jnp.sqrt(jnp.full((1, S), S * width, jnp.int32).astype(f32))
        return fold_rows(re) * scale, fold_rows(im) * scale

    def put(plane, p, re, im, width):
        re, im = scaled(re, im, width)
        acc[pl.ds(plane * R * C + p, 1), :] = re
        acc[pl.ds((plane + 1) * R * C + p, 1), :] = im

    def gathered(pieces):
        re, im = None, None
        for a_re, a_im, b_re, b_im in pieces:
            u, v = a_re * b_re + a_im * b_im, a_re * b_im - a_im * b_re
            re, im = (u, v) if re is None else (re + u, im + v)
        return re, im

    def weights(i, j, within):
        o, w = ro[i, j], rw[i, j]
        keep = (lane1 >= o) & (lane1 < o + w)
        live = keep if j < C - 1 else keep & jnp.logical_not(last_col)
        half = jnp.where(live, f32(0.5), f32(1.0))
        third = jnp.where(live, f32(1.0 / 3.0), f32(0.5))
        down = jnp.logical_not((i == R - 1) & last_row)
        third = jnp.where(jnp.full((1, S), down), third, half)
        if within:
            half, third = jnp.where(keep, half, 0.0), jnp.where(keep, third, 0.0)
        return jnp.broadcast_to(half, (8, S)), jnp.broadcast_to(third, (8, S))

    def reached(i, j, q):
        o, w = do[i, j], dw[i, j]
        return row8 >= o - q if q < S - 8 else row8 < o + w - q

    def weight_at(i, j, q, half, third):
        return half if q < lo else jnp.where(reached(i, j, q), third, half)

    def rows_of(p):
        return PAD + p * 2 * S

    def east_of(i, j):
        base = rows_of(i * C + j + 1)

        def load(q, o):
            return pltpu.roll(at(pv, base + q), o, 1), pltpu.roll(at(pv, base + S + q), o, 1)

        return load

    def east_rim(i):
        def load(q, o):
            both = at(east_recv, i * S + q)
            return pltpu.roll(both, o, 1), pltpu.roll(both, lax.rem(o + H, S), 1)

        return load

    def place_east(i, j, q, b, half, third):
        to = (i * C + j) * 2 * S + q
        weight = weight_at(i, j, q, half, third)
        put_at(ew, to, b[0] * weight)
        put_at(ew, to + S, b[1] * weight)

    def east_sums(i, j, load, place):
        p = i * C + j
        o, w = ro[i, j], rw[i, j]
        base = rows_of(p)
        half, third = weights(i, j, True)

        def piece(q):
            b = load(q, o)
            if place:
                place_east(i, j, q, b, half, third)
            return (at(pv, base + q), at(pv, base + S + q)) + b

        re, im = gathered(piece(q) for q in range(0, S, 8))
        keep = (lane1 >= o) & (lane1 < o + w)
        return p, jnp.where(keep, re, 0.0), jnp.where(keep, im, 0.0), w

    def east_inner(i, carry):
        for j in range(C - 1):
            put(0, *east_sums(i, j, east_of(i, j), True))
        return carry

    def south_store(i, j, ref, start, gap):
        p = i * C + j
        o, w = do[i, j], dw[i, j]
        base = rows_of(p)
        _, third = weights(i, j, False)

        def piece(q):
            keep = reached(i, j, q)
            b_re = jnp.where(keep, ref[pl.ds(start + (q - o), 8), :], 0.0)
            b_im = jnp.where(keep, ref[pl.ds(start + gap + (q - o), 8), :], 0.0)
            to = p * 2 * T + q - lo
            put_at(sw, to, b_re * third)
            put_at(sw, to + T, b_im * third)
            return at(pv, base + q), at(pv, base + S + q), b_re, b_im

        re, im = gathered(piece(q) for q in range(lo, S, 8))
        put(2, p, re, im, w)

    def south_inner(i, carry):
        for j in range(C):
            south_store(i, j, pv, rows_of((i + 1) * C + j), S)
        return carry

    spread(1)
    lax.fori_loop(0, R // 2, east_inner, 0)
    spread(2)
    forward(R - n_relay)
    lax.fori_loop(R // 2, R, east_inner, 0)
    spread(3)
    forward(R - n_relay + 1)
    lax.fori_loop(0, R // 2, south_inner, 0)
    spread(4)
    forward(R - n_relay + 2)
    lax.fori_loop(R // 2, R - 1, south_inner, 0)
    spread(5)
    for i in range(R - n_relay + 3, R):
        forward(i)

    @pl.when(my_row < nr - 1)
    def _():
        all_south(my_row).wait_recv()

    @pl.when(last_row)
    def _():
        south_recv[...] = jnp.zeros_like(south_recv)

    for j in range(C):
        south_store(R - 1, j, south_recv, PAD + j * 2 * H, H)

    for k in range(6, len(steps)):
        spread(k)

    @pl.when(last_col)
    def _():
        east_recv[...] = jnp.zeros_like(east_recv)

    def east_wait(g):
        run = arrive_groups(R)[g]
        east_run(run[0], len(run), g, my_col).wait_recv()

    def rim_row(i):
        return 2 * (i - (R - n_late))

    n_late = min(3, R)
    for g, run in enumerate(arrive_groups(R)):
        if len(run) > 1 or run[0] < R - n_late:

            @pl.when(jnp.logical_not(last_col))
            def _():
                east_wait(g)

            for i in run:
                put(0, *east_sums(i, C - 1, east_rim(i), False))
    sums = lax.dot_general(
        jnp.ones((8, S), f32), acc[...], (((1,), (1,)), ((), ())),
        precision=highest, preferred_element_type=f32,
    )

    def rim(i):
        @pl.when(jnp.logical_not(last_col) & jnp.logical_not(turned_here(i)))
        def _():
            east_wait(arrive_sem[i])
            _, re, im, width = east_sums(i, C - 1, east_rim(i), False)
            re, im = scaled(re, im, width)
            late[rim_row(i) : rim_row(i) + 1, :] = re
            late[rim_row(i) + 1 : rim_row(i) + 2, :] = im

    def turn_row(i):
        return 2 * n_late + 2 * (i - (R - n_turn))

    def turn(i):
        @pl.when(closes & (i >= R - turned_of(my_col - 1)))
        def _():
            turn_copy(i, my_col).wait_recv()
            re, im = None, None
            for q in range(0, S, 8):
                a = at(turned, (i - R + n_turn) * S + q)
                b = at(epack, i * S + q)
                u, v = a * b, a * pltpu.roll(b, H, 1)
                re, im = (u, v) if re is None else (re + u, im + v)
            im = jnp.where(lane1 < H, im, -im)
            late[turn_row(i) : turn_row(i) + 1, :] = fold_rows(re)
            late[turn_row(i) + 1 : turn_row(i) + 2, :] = fold_rows(im)

    for i in range(R - n_late, R):
        if i == R - 1:
            for k in range(R - n_turn, R):
                turn(k)
        rim(i)
    tails = jnp.sum(late[...], axis=1, keepdims=True)

    def spot(i, part, row):
        return jnp.where(lane1 == part * R * C + i * C + C - 1, tails[row : row + 1, :], 0.0)

    east_row, turn_line = sums[0:1, :S], jnp.zeros((1, S), f32)
    for part in range(2):
        for i in range(R - n_late, R):
            east_row = east_row + spot(i, part, rim_row(i) + part)
        for i in range(R - n_turn, R):
            turn_line = turn_line + spot(i, part, turn_row(i) + part)
    mine = jnp.concatenate([east_row, sums[0:1, S:], turn_line], axis=0)
    send_buf[...] = mine
    recv[me] = mine

    def index(d):
        return d[0] * nc + d[1]

    def gather_copy(target, source):
        return pltpu.make_async_remote_copy(
            src_ref=send_buf,
            dst_ref=recv.at[index(source)],
            send_sem=g_send.at[0],
            recv_sem=g_recv.at[0],
            device_id=target,
            device_id_type=MESH,
        )

    def all_gathered():
        return pltpu.make_async_remote_copy(
            src_ref=recv.at[pl.ds(0, ndev - 1)],
            dst_ref=recv.at[pl.ds(0, ndev - 1)],
            send_sem=g_send.at[0],
            recv_sem=g_recv.at[0],
            device_id=others[0],
            device_id_type=MESH,
        )

    for other in others:
        gather_copy(other, (my_row, my_col)).start()

    def weigh(i, carry):
        for j in range(C):
            half, third = weights(i, j, False)
            base, to = rows_of(i * C + j), (i * C + j) * 2 * S
            for q in range(0, S, 8):
                weight = weight_at(i, j, q, half, third)
                put_at(aw, to + q, at(pv, base + q) * weight)
                put_at(aw, to + S + q, at(pv, base + S + q) * weight)
        return carry

    def weigh_rim(i, carry):
        half, third = weights(i, C - 1, True)
        load, o = east_rim(i), ro[i, C - 1]
        for q in range(0, S, 8):
            place_east(i, C - 1, q, load(q, o), half, third)
        return carry

    lax.fori_loop(0, R, weigh, 0)
    for i in range(R - n_turn, R):

        @pl.when(turned_here(i))
        def _():
            east_wait(arrive_sem[i])

    lax.fori_loop(0, R, weigh_rim, 0)

    all_gathered().wait_recv()

    got = recv[...]
    east, south = got[:, 0, :] + pltpu.roll(got[:, 2, :], ndev - 1, 0), got[:, 1, :]
    field = lax.broadcasted_iota(jnp.int32, (ndev, S), 0)
    slot = lax.broadcasted_iota(jnp.int32, (ndev, S), 1)
    valid = slot < R * C
    j_of, i_of = slot % C, (slot // C) % R
    dc, dr = field % nc, field // nc

    def roll(x, by, axis):
        return pltpu.roll(x, by % x.shape[axis], axis)

    def from_east(x):
        far = roll(roll(x, -1, 0), C - 1, 1)
        far = jnp.where(dc < nc - 1, far, 0.0)
        return jnp.where(j_of < C - 1, roll(x, -1, 1), far)

    def from_west(x):
        far = roll(roll(x, 1, 0), 1 - C, 1)
        far = jnp.where(dc > 0, far, 0.0)
        return jnp.where(j_of > 0, roll(x, 1, 1), far)

    def from_south(x):
        far = roll(roll(x, -nc, 0), (R - 1) * C, 1)
        far = jnp.where(dr < nr - 1, far, 0.0)
        return jnp.where(i_of < R - 1, roll(x, -C, 1), far)

    def from_north(x):
        far = roll(roll(x, nc, 0), -(R - 1) * C, 1)
        far = jnp.where(dr > 0, far, 0.0)
        return jnp.where(i_of > 0, roll(x, C, 1), far)

    ce = (jnp.where(valid, east, 0.0), jnp.where(valid, roll(east, -R * C, 1), 0.0))
    cs = (jnp.where(valid, south, 0.0), jnp.where(valid, roll(south, -R * C, 1), 0.0))
    cw = tuple(from_west(x) for x in ce)
    cn = tuple(from_north(x) for x in cs)
    mean = 1.0 / float(ndev * R * C)

    def times(a, b):
        return (a[0] * b[0] - a[1] * b[1], a[0] * b[1] + a[1] * b[0])

    def conj_times(a, b):
        return (a[0] * b[0] + a[1] * b[1], a[0] * b[1] - a[1] * b[0])

    now = (ce[0] + cs[0] + cw[0] + cn[0], ce[1] + cs[1] - cw[1] - cn[1])
    now = tuple(jnp.where(valid, x, 0.0) for x in now)
    square = now[0] * now[0] + now[1] * now[1]
    constant = eps_norm
    for step in range(1, ITERS):
        terms = (
            times(ce, tuple(from_east(x) for x in now)),
            times(cs, tuple(from_south(x) for x in now)),
            conj_times(cw, tuple(from_west(x) for x in now)),
            conj_times(cn, tuple(from_north(x) for x in now)),
        )
        now = tuple(
            jnp.where(valid, terms[0][q] + terms[1][q] + terms[2][q] + terms[3][q], 0.0)
            for q in range(2)
        )
        square = eps_norm * square + (now[0] * now[0] + now[1] * now[1])
        constant = constant * eps_norm
    outs = now + tuple(from_east(x) for x in now) + tuple(from_south(x) for x in now)
    for q in range(6):
        fields[q] = outs[q]
    total = jnp.sum(jnp.sum(square, axis=0, keepdims=True), axis=1, keepdims=True)
    factor = 1.0 / jnp.sqrt(total * mean + constant)
    diagonal = lax.broadcasted_iota(jnp.int32, (R * C, S), 0) == lax.broadcasted_iota(
        jnp.int32, (R * C, S), 1
    )
    for q in range(6):
        row = fields[q, pl.ds(me, 1), :] * factor
        phase_out[q : q + 1, :] = row
        spot = jnp.where(diagonal, jnp.broadcast_to(row, (R * C, S)), 0.0)
        factors[q * R * C : (q + 1) * R * C, :] = jnp.broadcast_to(
            jnp.sum(spot, axis=1, keepdims=True), (R * C, S)
        )

    all_gathered().wait_send()

    @pl.when(my_col > 0)
    def _():
        east_run(0, R, 0, my_col - 1).wait_send()

    for i in range(R - n_relay, R):

        @pl.when(forwards(i))
        def _():
            forward_copy(i, my_col - 2).wait_send()

    for i in range(R - n_turn, R):

        @pl.when(turned_here(i))
        def _():
            turn_copy(i, my_col + 1).wait_send()

    @pl.when(my_row > 0)
    def _():
        all_south(my_row - 1).wait_send()


def blend_kernel(dims, aw, ew, sw, factors, phase, out, phases, ov, pad, out_sem, phase_sem):
    R, C, S, pair = dims
    lo = S // 2 - 8
    T = S - lo
    piece = pair * 2 * S

    def save(k):
        return pltpu.make_async_copy(
            ov.at[pl.ds(k * piece, piece)], out.at[pl.ds(k * piece, piece)], out_sem.at[0]
        )

    def at(ref, row):
        return ref[pl.ds(pl.multiple_of(row, 8), 8), :]

    def times(g, a):
        return g[0] * a[0] - g[1] * a[1], g[0] * a[1] + g[1] * a[0]

    def place(p):
        g, ge, gs = (
            [jnp.broadcast_to(factors[pl.ds((2 * k + part) * R * C + p, 1), :], (8, S)) for part in range(2)]
            for k in range(3)
        )
        base = p * 2 * S
        for q in range(0, S, 8):
            own = times(g, (at(aw, base + q), at(aw, base + S + q)))
            east = times(ge, (at(ew, base + q), at(ew, base + S + q)))
            sums = [own[part] + east[part] for part in range(2)]
            if q >= lo:
                down = p * 2 * T + q - lo
                south = times(gs, (at(sw, down), at(sw, down + T)))
                sums = [sums[part] + south[part] for part in range(2)]
            ov[pl.ds(pl.multiple_of(base + q, 8), 8), :] = sums[0]
            ov[pl.ds(pl.multiple_of(base + S + q, 8), 8), :] = sums[1]

    def step(k, carry):
        for n in range(pair):
            place(k * pair + n)
        save(k).start()
        return carry

    lax.fori_loop(0, R * C // pair, step, 0)

    row8 = lax.broadcasted_iota(jnp.int32, (R, S), 0)
    for part in range(2):
        line = jnp.broadcast_to(phase[part : part + 1, :], (R, S))
        plane = line
        for i in range(1, R):
            plane = jnp.where(row8 == i, pltpu.roll(line, S - i * C, 1), plane)
        pad[part] = plane[:, :C]
    send = pltpu.make_async_copy(pad, phases, phase_sem.at[0])
    send.start()
    send.wait()
    pltpu.make_async_copy(ov, out, out_sem.at[0]).wait()


def local(nr, nc, patches, right_offset, right_width, down_offset, down_width):
    R, C, _, S, _ = patches.shape
    H, ndev = S // 2, nr * nc
    T = S - (H - 8)
    dims = (R, C, S, nr, nc)
    flat = patches.reshape(R * C * 2 * S, S)
    anyspec = pl.BlockSpec(memory_space=pl.ANY)
    vmem = pl.BlockSpec(memory_space=pltpu.VMEM)
    dma = pltpu.SemaphoreType.DMA
    tables = (right_offset, right_width, down_offset, down_width)
    parts = pl.pallas_call(
        functools.partial(sync_kernel, dims),
        out_shape=(
            pltpu.VMEM((R * C * 2 * S, S), f32),
            pltpu.VMEM((R * C * 2 * S, S), f32),
            pltpu.VMEM((R * C * 2 * T, S), f32),
            pltpu.VMEM((6 * R * C, S), f32),
            pltpu.VMEM((8, S), f32),
        ),
        in_specs=[pl.BlockSpec(memory_space=pltpu.HBM)] * 5,
        out_specs=(vmem,) * 5,
        scratch_shapes=[
            pltpu.VMEM((PAD + R * C * 2 * S, S), f32),
            pltpu.VMEM((R * S, S), f32),
            pltpu.VMEM((2 * PAD + 2 * C * H, S), f32),
            pltpu.VMEM((R * S, S), f32),
            pltpu.VMEM((4 * R * C, S), f32),
            pltpu.VMEM((3, S), f32),
            pltpu.VMEM((ndev, 3, S), f32),
            pltpu.VMEM((6, ndev, S), f32),
            pltpu.SMEM((4, R, C), jnp.int32),
            pltpu.VMEM((R // 2 * S, S), f32),
            pltpu.VMEM((min(2, R) * S, S), f32),
            pltpu.VMEM((min(2, R) * S, S), f32),
            pltpu.VMEM((16, S), f32),
            dma((len(load_groups(R)),)), dma((1,)),
            dma((1,)), dma((len(arrive_groups(R)),)),
            dma((1,)), dma((1,)),
            dma((1,)), dma((1,)),
            dma((1,)),
            pltpu.SemaphoreType.REGULAR((n_rounds(nr) + n_rounds(nc),)),
            dma((R // 2,)), dma((R // 2,)),
            dma((min(2, R),)), dma((min(2, R),)),
            pltpu.SemaphoreType.REGULAR((1,)),
        ],
        compiler_params=pltpu.CompilerParams(
            collective_id=0, has_side_effects=True, vmem_limit_bytes=24 << 20
        ),
        name="sync_patches",
    )(*(pltpu.with_memory_space_constraint(x, pltpu.HBM) for x in (flat, *tables)))
    pair = 2
    blended, phases = pl.pallas_call(
        functools.partial(blend_kernel, (R, C, S, pair)),
        out_shape=(
            jax.ShapeDtypeStruct((R * C * 2 * S, S), f32),
            jax.ShapeDtypeStruct((2, R, C), f32),
        ),
        in_specs=[vmem] * 5,
        out_specs=(anyspec, anyspec),
        scratch_shapes=[
            pltpu.VMEM((R * C * 2 * S, S), f32),
            pltpu.VMEM((2, R, C), f32),
            dma((1,)),
            dma((1,)),
        ],
        compiler_params=pltpu.CompilerParams(vmem_limit_bytes=24 << 20),
        name="blend_patches",
    )(*parts)
    return blended.reshape(patches.shape), phases


def solution(mesh):
    return jax.shard_map(
        functools.partial(local, mesh.shape["row"], mesh.shape["col"]),
        mesh=mesh,
        in_specs=(P("row", "col", None, None, None),) + (P("row", "col"),) * 4,
        out_specs=(P("row", "col", None, None, None), P(None, "row", "col")),
        check_vma=False,
    )
```

```python
import functools

import jax
import jax.numpy as jnp
from jax import lax
from jax.experimental import pallas as pl
from jax.experimental.pallas import tpu as pltpu
from jax.sharding import PartitionSpec as P

ITERS = 2
PAD = 64
eps_norm = 1.0
highest = lax.Precision.HIGHEST
MESH = pl.DeviceIdType.MESH
f32 = jnp.float32


def fold_rows(x):
    return jnp.sum(x, axis=0, keepdims=True)


def doubling(pos, n, at):
    if n == 1:
        return []
    rounds = [[at(-1) + (pos > 0, pos < n - 1)]]
    known = 1
    while known < n - 1:
        rounds.append([
            at(-known) + (pos >= known, pos < n - known),
            at(known) + (pos < n - known, pos >= known),
        ])
        known *= 2
    return rounds


def groups(n, sizes):
    runs, first = [], 0
    while first < n:
        size = sizes[min(len(runs), len(sizes) - 1)]
        runs.append(range(first, min(n, first + size)))
        first += size
    return runs


def n_relays(n):
    return min(3, n // 2)


def load_groups(n):
    return groups(n, (1, 1, 2, 4))


def arrive_groups(n):
    tail = min(n, 4)
    return groups(n - tail, (4,)) + [range(n - tail + k, n - tail + k + 1) for k in range(tail)]


def n_rounds(n):
    return len(doubling(0, n, lambda k: (0, 0)))


def sync_kernel(
    dims, patches, ro_in, rw_in, do_in, dw_in, aw, ew, sw, factors, phase_out,
    pv, east_recv, south_recv,
    epack, acc, send_buf, recv, fields, table, relay_buf, strips, turned, late,
    col_sem, rest_sem, e_send, e_recv, s_send, s_recv, g_send, g_recv, table_sem, round_sem,
    relay_recv, relay_send, turn_recv, turn_send, pair_sem,
):
    R, C, S, nr, nc = dims
    H, ndev = S // 2, nr * nc
    lo = H - 8
    T = S - lo
    my_row, my_col = lax.axis_index("row"), lax.axis_index("col")
    me = my_row * nc + my_col
    last_col, last_row = my_col == nc - 1, my_row == nr - 1
    even = lax.rem(my_col, 2) == 0
    opens = even & (my_col >= max(2, nc - 4)) & (my_col < nc - 1)
    closes = jnp.logical_not(even) & (my_col >= max(3, nc - 3))
    n_relay, n_turn = n_relays(R), min(2, R)

    def relayed(c):
        return jnp.where(c == nc - 2, n_relay, 0)

    def turned_of(c):
        return jnp.where(c == nc - 2, n_turn, 1)

    def sent_around(i):
        return opens & (i >= R - relayed(my_col))

    def turned_here(i):
        return opens & (i >= R - turned_of(my_col))

    low = my_col < nc // 2
    turn_rows = [lax.rem(my_row + k, nr) for k in range(nr)]
    turn_cols = [lax.rem(my_col + jnp.where(low, nc - k, k), nc) for k in range(nc)]
    others = [
        (turn_rows[a], turn_cols[b])
        for b in [*range(1, nc), 0]
        for a in [*range(1, nr), 0]
        if a or b
    ]
    barrier = pltpu.get_barrier_semaphore()

    def signal(sem, row, col, there):
        @pl.when(there)
        def _():
            pl.semaphore_signal(sem, inc=1, device_id=(row, col), device_id_type=MESH)

    def await_all(sem, *due):
        amount = sum(one.astype(jnp.int32) for one in due)

        @pl.when(amount > 0)
        def _():
            pl.semaphore_wait(sem, amount)

    steps = doubling(my_row, nr, lambda k: (my_row + k, my_col))
    steps += doubling(my_col, nc, lambda k: (my_row, my_col + k))

    def tell(k):
        for row, col, there, _ in steps[k]:
            signal(round_sem.at[k], row, col, there)

    def spread(k):
        if k < len(steps):
            await_all(round_sem.at[k], *(here for _, _, _, here in steps[k]))
            if k + 1 < len(steps):
                tell(k + 1)

    load_sem = {i: g for g, run in enumerate(load_groups(R)) for i in run}
    cols = [
        pltpu.make_async_copy(
            patches.at[pl.ds(i * C * 2 * S, 2 * S)],
            pv.at[pl.ds(PAD + i * C * 2 * S, 2 * S)],
            col_sem.at[load_sem[i]],
        )
        for i in range(R)
    ]
    rests = [
        pltpu.make_async_copy(
            patches.at[pl.ds((i * C + 1) * 2 * S, (C - 1) * 2 * S)],
            pv.at[pl.ds(PAD + (i * C + 1) * 2 * S, (C - 1) * 2 * S)],
            rest_sem.at[0],
        )
        for i in range(R)
    ]
    tables = [
        pltpu.make_async_copy(here, table.at[k], table_sem.at[0])
        for k, here in enumerate((ro_in, rw_in, do_in, dw_in))
    ]
    ro, rw, do, dw = (table.at[k] for k in range(4))

    def whole(src, dst, sem):
        return pltpu.make_async_copy(src, dst, sem)

    for copy in cols:
        copy.start()
    signal(barrier, my_row, my_col + 1, my_col < nc - 1)
    signal(barrier, my_row + 1, my_col, my_row < nr - 1)
    lane = lax.broadcasted_iota(jnp.int32, (S, S), 1)

    def load(g):
        size = len(load_groups(R)[g]) * 2 * S
        whole(patches.at[pl.ds(0, size)], pv.at[pl.ds(PAD, size)], col_sem.at[g]).wait()

    def pack(i):
        base = PAD + i * C * 2 * S
        re = pv[pl.ds(base, S), :]
        im = pv[pl.ds(base + S, S), :]
        epack[pl.ds(i * S, S), :] = jnp.where(lane < H, re, pltpu.roll(im, H, 1))

    def south_copy(k, row):
        return pltpu.make_async_remote_copy(
            src_ref=patches.at[pl.ds(k * S, H)],
            dst_ref=south_recv.at[pl.ds(PAD + k * H, H)],
            send_sem=s_send.at[0],
            recv_sem=s_recv.at[0],
            device_id=(row, my_col),
            device_id_type=MESH,
        )

    def all_south(row):
        return pltpu.make_async_remote_copy(
            src_ref=patches.at[pl.ds(0, 2 * C * H)],
            dst_ref=south_recv.at[pl.ds(PAD, 2 * C * H)],
            send_sem=s_send.at[0],
            recv_sem=s_recv.at[0],
            device_id=(row, my_col),
            device_id_type=MESH,
        )

    arrive_sem = {i: g for g, run in enumerate(arrive_groups(R)) for i in run}

    def east_run(first, n, sem, col):
        return pltpu.make_async_remote_copy(
            src_ref=epack.at[pl.ds(first * S, n * S)],
            dst_ref=east_recv.at[pl.ds(first * S, n * S)],
            send_sem=e_send.at[0],
            recv_sem=e_recv.at[sem],
            device_id=(my_row, col),
            device_id_type=MESH,
        )

    def east_copy(k, col):
        return east_run(k, 1, arrive_sem[k], col)

    def send_east(i):
        @pl.when((my_col > 0) & jnp.logical_not(sent_around(i)) if i >= R - n_relay else my_col > 0)
        def _():
            east_copy(i, my_col - 1).start()

    def relay_copy(i, col):
        k = i - (R - n_relay)
        return pltpu.make_async_remote_copy(
            src_ref=epack.at[pl.ds(i * S, S)],
            dst_ref=relay_buf.at[pl.ds(k * S, S)],
            send_sem=e_send.at[0],
            recv_sem=relay_recv.at[k],
            device_id=(my_row, col),
            device_id_type=MESH,
        )

    def forward_copy(i, col):
        k = i - (R - n_relay)
        return pltpu.make_async_remote_copy(
            src_ref=relay_buf.at[pl.ds(k * S, S)],
            dst_ref=east_recv.at[pl.ds(i * S, S)],
            send_sem=relay_send.at[k],
            recv_sem=e_recv.at[arrive_sem[i]],
            device_id=(my_row, col),
            device_id_type=MESH,
        )

    def forwards(i):
        return closes & (i >= R - relayed(my_col - 1))

    def forward(i):
        if i < R:

            @pl.when(forwards(i))
            def _():
                relay_copy(i, my_col).wait_recv()
                forward_copy(i, my_col - 2).start()

    def turn_copy(i, col):
        k = i - (R - n_turn)
        return pltpu.make_async_remote_copy(
            src_ref=strips.at[pl.ds(k * S, S)],
            dst_ref=turned.at[pl.ds(k * S, S)],
            send_sem=turn_send.at[k],
            recv_sem=turn_recv.at[k],
            device_id=(my_row, col),
            device_id_type=MESH,
        )

    @pl.when(closes)
    def _():
        await_all(barrier, my_row > 0, my_col > 0)
        signal(pair_sem.at[0], my_row, my_col - 1, closes)

    load(0)
    for copy in tables:
        copy.start()
    for copy in rests:
        copy.start()
    pack(0)

    @pl.when(jnp.logical_not(closes))
    def _():
        await_all(barrier, my_row > 0, my_col > 0)

    send_east(0)
    for g, run in enumerate(load_groups(R)):
        if g:
            load(g)
            for i in run:
                pack(i)
                send_east(i)
        if g == 1 or len(load_groups(R)) == 1:

            @pl.when(my_row > 0)
            def _():
                for k in range(2 * C):
                    south_copy(k, my_row - 1).start()

            if steps:
                tell(0)
    acc[...] = jnp.zeros_like(acc)
    late[...] = jnp.zeros_like(late)
    await_all(pair_sem.at[0], opens)
    for i in range(R - n_relay, R):

        @pl.when(sent_around(i))
        def _():
            relay_copy(i, my_col + 1).start()

    spread(0)
    whole(table, table, table_sem.at[0]).wait()
    size = R * (C - 1) * 2 * S
    whole(patches.at[pl.ds(0, size)], pv.at[pl.ds(PAD, size)], rest_sem.at[0]).wait()

    lane1 = lax.broadcasted_iota(jnp.int32, (1, S), 1)
    row8 = lax.broadcasted_iota(jnp.int32, (8, S), 0)

    for i in range(R - n_turn, R):

        @pl.when(turned_here(i))
        def _():
            o, w = ro[i, C - 1], rw[i, C - 1]
            base = PAD + (i * C + C - 1) * 2 * S
            scale = 1.0 / jnp.sqrt(jnp.full((1, S), S * w, jnp.int32).astype(f32))
            weight = jnp.where((lane1 & (H - 1)) < w, scale, 0.0)
            re = pltpu.roll(pv[pl.ds(base, S), :], S - o, 1)
            im = pltpu.roll(pv[pl.ds(base + S, S), :], lax.rem(S + H - o, S), 1)
            strips[pl.ds((i - R + n_turn) * S, S), :] = jnp.where(lane < H, re, im) * weight
            turn_copy(i, my_col + 1).start()

    def at(ref, row):
        return ref[pl.ds(pl.multiple_of(row, 8), 8), :]

    def put_at(ref, row, value):
        ref[pl.ds(pl.multiple_of(row, 8), 8), :] = value

    def scaled(re, im, width):
        scale = 1.0 / jnp.sqrt(jnp.full((1, S), S * width, jnp.int32).astype(f32))
        return fold_rows(re) * scale, fold_rows(im) * scale

    def put(plane, p, re, im, width):
        re, im = scaled(re, im, width)
        acc[pl.ds(plane * R * C + p, 1), :] = re
        acc[pl.ds((plane + 1) * R * C + p, 1), :] = im

    def gathered(pieces):
        re, im = None, None
        for a_re, a_im, b_re, b_im in pieces:
            u, v = a_re * b_re + a_im * b_im, a_re * b_im - a_im * b_re
            re, im = (u, v) if re is None else (re + u, im + v)
        return re, im

    def weights(i, j, within):
        o, w = ro[i, j], rw[i, j]
        keep = (lane1 >= o) & (lane1 < o + w)
        live = keep if j < C - 1 else keep & jnp.logical_not(last_col)
        half = jnp.where(live, f32(0.5), f32(1.0))
        third = jnp.where(live, f32(1.0 / 3.0), f32(0.5))
        down = jnp.logical_not((i == R - 1) & last_row)
        third = jnp.where(jnp.full((1, S), down), third, half)
        if within:
            half, third = jnp.where(keep, half, 0.0), jnp.where(keep, third, 0.0)
        return jnp.broadcast_to(half, (8, S)), jnp.broadcast_to(third, (8, S))

    def reached(i, j, q):
        o, w = do[i, j], dw[i, j]
        return row8 >= o - q if q < S - 8 else row8 < o + w - q

    def weight_at(i, j, q, half, third):
        return half if q < lo else jnp.where(reached(i, j, q), third, half)

    def rows_of(p):
        return PAD + p * 2 * S

    def east_of(i, j):
        base = rows_of(i * C + j + 1)

        def load(q, o):
            return pltpu.roll(at(pv, base + q), o, 1), pltpu.roll(at(pv, base + S + q), o, 1)

        return load

    def east_rim(i):
        def load(q, o):
            both = at(east_recv, i * S + q)
            return pltpu.roll(both, o, 1), pltpu.roll(both, lax.rem(o + H, S), 1)

        return load

    def place_east(i, j, q, b, half, third):
        to = (i * C + j) * 2 * S + q
        weight = weight_at(i, j, q, half, third)
        put_at(ew, to, b[0] * weight)
        put_at(ew, to + S, b[1] * weight)

    def east_sums(i, j, load, place):
        p = i * C + j
        o, w = ro[i, j], rw[i, j]
        base = rows_of(p)
        half, third = weights(i, j, True)

        def piece(q):
            b = load(q, o)
            if place:
                place_east(i, j, q, b, half, third)
            return (at(pv, base + q), at(pv, base + S + q)) + b

        re, im = gathered(piece(q) for q in range(0, S, 8))
        keep = (lane1 >= o) & (lane1 < o + w)
        return p, jnp.where(keep, re, 0.0), jnp.where(keep, im, 0.0), w

    def east_inner(i, carry):
        for j in range(C - 1):
            put(0, *east_sums(i, j, east_of(i, j), True))
        return carry

    def south_store(i, j, ref, start, gap):
        p = i * C + j
        o, w = do[i, j], dw[i, j]
        base = rows_of(p)
        _, third = weights(i, j, False)

        def piece(q):
            keep = reached(i, j, q)
            b_re = jnp.where(keep, ref[pl.ds(start + (q - o), 8), :], 0.0)
            b_im = jnp.where(keep, ref[pl.ds(start + gap + (q - o), 8), :], 0.0)
            to = p * 2 * T + q - lo
            put_at(sw, to, b_re * third)
            put_at(sw, to + T, b_im * third)
            return at(pv, base + q), at(pv, base + S + q), b_re, b_im

        re, im = gathered(piece(q) for q in range(lo, S, 8))
        put(2, p, re, im, w)

    def south_inner(i, carry):
        for j in range(C):
            south_store(i, j, pv, rows_of((i + 1) * C + j), S)
        return carry

    spread(1)
    lax.fori_loop(0, R // 2, east_inner, 0)
    spread(2)
    forward(R - n_relay)
    lax.fori_loop(R // 2, R, east_inner, 0)
    spread(3)
    forward(R - n_relay + 1)
    lax.fori_loop(0, R // 2, south_inner, 0)
    spread(4)
    forward(R - n_relay + 2)
    lax.fori_loop(R // 2, R - 1, south_inner, 0)
    spread(5)

    @pl.when(my_row < nr - 1)
    def _():
        all_south(my_row).wait_recv()

    @pl.when(last_row)
    def _():
        south_recv[...] = jnp.zeros_like(south_recv)

    for j in range(C):
        south_store(R - 1, j, south_recv, PAD + j * 2 * H, H)

    for k in range(6, len(steps)):
        spread(k)

    @pl.when(last_col)
    def _():
        east_recv[...] = jnp.zeros_like(east_recv)

    def east_wait(g):
        run = arrive_groups(R)[g]
        east_run(run[0], len(run), g, my_col).wait_recv()

    def rim_row(i):
        return 2 * (i - (R - n_late))

    n_late = min(3, R)
    for g, run in enumerate(arrive_groups(R)):
        if len(run) > 1 or run[0] < R - n_late:

            @pl.when(jnp.logical_not(last_col))
            def _():
                east_wait(g)

            for i in run:
                put(0, *east_sums(i, C - 1, east_rim(i), False))
    sums = lax.dot_general(
        jnp.ones((8, S), f32), acc[...], (((1,), (1,)), ((), ())),
        precision=highest, preferred_element_type=f32,
    )

    def rim(i):
        @pl.when(jnp.logical_not(last_col) & jnp.logical_not(turned_here(i)))
        def _():
            east_wait(arrive_sem[i])
            _, re, im, width = east_sums(i, C - 1, east_rim(i), False)
            re, im = scaled(re, im, width)
            late[rim_row(i) : rim_row(i) + 1, :] = re
            late[rim_row(i) + 1 : rim_row(i) + 2, :] = im

    def turn_row(i):
        return 2 * n_late + 2 * (i - (R - n_turn))

    def turn(i):
        @pl.when(closes & (i >= R - turned_of(my_col - 1)))
        def _():
            turn_copy(i, my_col).wait_recv()
            re, im = None, None
            for q in range(0, S, 8):
                a = at(turned, (i - R + n_turn) * S + q)
                b = at(epack, i * S + q)
                u, v = a * b, a * pltpu.roll(b, H, 1)
                re, im = (u, v) if re is None else (re + u, im + v)
            im = jnp.where(lane1 < H, im, -im)
            late[turn_row(i) : turn_row(i) + 1, :] = fold_rows(re)
            late[turn_row(i) + 1 : turn_row(i) + 2, :] = fold_rows(im)

    for i in range(R - n_late, R):
        if i == R - 1:
            for k in range(R - n_turn, R):
                turn(k)
        rim(i)
    tails = jnp.sum(late[...], axis=1, keepdims=True)

    def spot(i, part, row):
        return jnp.where(lane1 == part * R * C + i * C + C - 1, tails[row : row + 1, :], 0.0)

    east_row, turn_line = sums[0:1, :S], jnp.zeros((1, S), f32)
    for part in range(2):
        for i in range(R - n_late, R):
            east_row = east_row + spot(i, part, rim_row(i) + part)
        for i in range(R - n_turn, R):
            turn_line = turn_line + spot(i, part, turn_row(i) + part)
    mine = jnp.concatenate([east_row, sums[0:1, S:], turn_line], axis=0)
    send_buf[...] = mine
    recv[me] = mine

    def index(d):
        return d[0] * nc + d[1]

    def gather_copy(target, source):
        return pltpu.make_async_remote_copy(
            src_ref=send_buf,
            dst_ref=recv.at[index(source)],
            send_sem=g_send.at[0],
            recv_sem=g_recv.at[0],
            device_id=target,
            device_id_type=MESH,
        )

    def all_gathered():
        return pltpu.make_async_remote_copy(
            src_ref=recv.at[pl.ds(0, ndev - 1)],
            dst_ref=recv.at[pl.ds(0, ndev - 1)],
            send_sem=g_send.at[0],
            recv_sem=g_recv.at[0],
            device_id=others[0],
            device_id_type=MESH,
        )

    for other in others:
        gather_copy(other, (my_row, my_col)).start()

    def weigh(i, carry):
        for j in range(C):
            half, third = weights(i, j, False)
            base, to = rows_of(i * C + j), (i * C + j) * 2 * S
            for q in range(0, S, 8):
                weight = weight_at(i, j, q, half, third)
                put_at(aw, to + q, at(pv, base + q) * weight)
                put_at(aw, to + S + q, at(pv, base + S + q) * weight)
        return carry

    def weigh_rim(i, carry):
        half, third = weights(i, C - 1, True)
        load, o = east_rim(i), ro[i, C - 1]
        for q in range(0, S, 8):
            place_east(i, C - 1, q, load(q, o), half, third)
        return carry

    lax.fori_loop(0, R, weigh, 0)
    for i in range(R - n_turn, R):

        @pl.when(turned_here(i))
        def _():
            east_wait(arrive_sem[i])

    lax.fori_loop(0, R, weigh_rim, 0)

    all_gathered().wait_recv()

    got = recv[...]
    east, south = got[:, 0, :] + pltpu.roll(got[:, 2, :], ndev - 1, 0), got[:, 1, :]
    field = lax.broadcasted_iota(jnp.int32, (ndev, S), 0)
    slot = lax.broadcasted_iota(jnp.int32, (ndev, S), 1)
    valid = slot < R * C
    j_of, i_of = slot % C, (slot // C) % R
    dc, dr = field % nc, field // nc

    def roll(x, by, axis):
        return pltpu.roll(x, by % x.shape[axis], axis)

    def from_east(x):
        far = roll(roll(x, -1, 0), C - 1, 1)
        far = jnp.where(dc < nc - 1, far, 0.0)
        return jnp.where(j_of < C - 1, roll(x, -1, 1), far)

    def from_west(x):
        far = roll(roll(x, 1, 0), 1 - C, 1)
        far = jnp.where(dc > 0, far, 0.0)
        return jnp.where(j_of > 0, roll(x, 1, 1), far)

    def from_south(x):
        far = roll(roll(x, -nc, 0), (R - 1) * C, 1)
        far = jnp.where(dr < nr - 1, far, 0.0)
        return jnp.where(i_of < R - 1, roll(x, -C, 1), far)

    def from_north(x):
        far = roll(roll(x, nc, 0), -(R - 1) * C, 1)
        far = jnp.where(dr > 0, far, 0.0)
        return jnp.where(i_of > 0, roll(x, C, 1), far)

    ce = (jnp.where(valid, east, 0.0), jnp.where(valid, roll(east, -R * C, 1), 0.0))
    cs = (jnp.where(valid, south, 0.0), jnp.where(valid, roll(south, -R * C, 1), 0.0))
    cw = tuple(from_west(x) for x in ce)
    cn = tuple(from_north(x) for x in cs)
    mean = 1.0 / float(ndev * R * C)

    def times(a, b):
        return (a[0] * b[0] - a[1] * b[1], a[0] * b[1] + a[1] * b[0])

    def conj_times(a, b):
        return (a[0] * b[0] + a[1] * b[1], a[0] * b[1] - a[1] * b[0])

    now = (ce[0] + cs[0] + cw[0] + cn[0], ce[1] + cs[1] - cw[1] - cn[1])
    now = tuple(jnp.where(valid, x, 0.0) for x in now)
    square = now[0] * now[0] + now[1] * now[1]
    constant = eps_norm
    for step in range(1, ITERS):
        terms = (
            times(ce, tuple(from_east(x) for x in now)),
            times(cs, tuple(from_south(x) for x in now)),
            conj_times(cw, tuple(from_west(x) for x in now)),
            conj_times(cn, tuple(from_north(x) for x in now)),
        )
        now = tuple(
            jnp.where(valid, terms[0][q] + terms[1][q] + terms[2][q] + terms[3][q], 0.0)
            for q in range(2)
        )
        square = eps_norm * square + (now[0] * now[0] + now[1] * now[1])
        constant = constant * eps_norm
    outs = now + tuple(from_east(x) for x in now) + tuple(from_south(x) for x in now)
    for q in range(6):
        fields[q] = outs[q]
    total = jnp.sum(jnp.sum(square, axis=0, keepdims=True), axis=1, keepdims=True)
    factor = 1.0 / jnp.sqrt(total * mean + constant)
    diagonal = lax.broadcasted_iota(jnp.int32, (R * C, S), 0) == lax.broadcasted_iota(
        jnp.int32, (R * C, S), 1
    )
    for q in range(6):
        row = fields[q, pl.ds(me, 1), :] * factor
        phase_out[q : q + 1, :] = row
        spot = jnp.where(diagonal, jnp.broadcast_to(row, (R * C, S)), 0.0)
        factors[q * R * C : (q + 1) * R * C, :] = jnp.broadcast_to(
            jnp.sum(spot, axis=1, keepdims=True), (R * C, S)
        )

    all_gathered().wait_send()

    @pl.when(my_col > 0)
    def _():
        east_run(0, R, 0, my_col - 1).wait_send()

    for i in range(R - n_relay, R):

        @pl.when(forwards(i))
        def _():
            forward_copy(i, my_col - 2).wait_send()

    for i in range(R - n_turn, R):

        @pl.when(turned_here(i))
        def _():
            turn_copy(i, my_col + 1).wait_send()

    @pl.when(my_row > 0)
    def _():
        all_south(my_row - 1).wait_send()


def blend_kernel(dims, aw, ew, sw, factors, phase, out, phases, ov, pad, out_sem, phase_sem):
    R, C, S, pair = dims
    lo = S // 2 - 8
    T = S - lo
    piece = pair * 2 * S

    def save(k):
        return pltpu.make_async_copy(
            ov.at[pl.ds(k * piece, piece)], out.at[pl.ds(k * piece, piece)], out_sem.at[0]
        )

    def at(ref, row):
        return ref[pl.ds(pl.multiple_of(row, 8), 8), :]

    def times(g, a):
        return g[0] * a[0] - g[1] * a[1], g[0] * a[1] + g[1] * a[0]

    def place(p):
        g, ge, gs = (
            [jnp.broadcast_to(factors[pl.ds((2 * k + part) * R * C + p, 1), :], (8, S)) for part in range(2)]
            for k in range(3)
        )
        base = p * 2 * S
        for q in range(0, S, 8):
            own = times(g, (at(aw, base + q), at(aw, base + S + q)))
            east = times(ge, (at(ew, base + q), at(ew, base + S + q)))
            sums = [own[part] + east[part] for part in range(2)]
            if q >= lo:
                down = p * 2 * T + q - lo
                south = times(gs, (at(sw, down), at(sw, down + T)))
                sums = [sums[part] + south[part] for part in range(2)]
            ov[pl.ds(pl.multiple_of(base + q, 8), 8), :] = sums[0]
            ov[pl.ds(pl.multiple_of(base + S + q, 8), 8), :] = sums[1]

    def step(k, carry):
        for n in range(pair):
            place(k * pair + n)
        save(k).start()
        return carry

    lax.fori_loop(0, R * C // pair, step, 0)

    row8 = lax.broadcasted_iota(jnp.int32, (R, S), 0)
    for part in range(2):
        line = jnp.broadcast_to(phase[part : part + 1, :], (R, S))
        plane = line
        for i in range(1, R):
            plane = jnp.where(row8 == i, pltpu.roll(line, S - i * C, 1), plane)
        pad[part] = plane[:, :C]
    send = pltpu.make_async_copy(pad, phases, phase_sem.at[0])
    send.start()
    send.wait()
    pltpu.make_async_copy(ov, out, out_sem.at[0]).wait()


def local(nr, nc, patches, right_offset, right_width, down_offset, down_width):
    R, C, _, S, _ = patches.shape
    H, ndev = S // 2, nr * nc
    T = S - (H - 8)
    dims = (R, C, S, nr, nc)
    flat = patches.reshape(R * C * 2 * S, S)
    anyspec = pl.BlockSpec(memory_space=pl.ANY)
    vmem = pl.BlockSpec(memory_space=pltpu.VMEM)
    dma = pltpu.SemaphoreType.DMA
    tables = (right_offset, right_width, down_offset, down_width)
    parts = pl.pallas_call(
        functools.partial(sync_kernel, dims),
        out_shape=(
            pltpu.VMEM((R * C * 2 * S, S), f32),
            pltpu.VMEM((R * C * 2 * S, S), f32),
            pltpu.VMEM((R * C * 2 * T, S), f32),
            pltpu.VMEM((6 * R * C, S), f32),
            pltpu.VMEM((8, S), f32),
        ),
        in_specs=[pl.BlockSpec(memory_space=pltpu.HBM)] * 5,
        out_specs=(vmem,) * 5,
        scratch_shapes=[
            pltpu.VMEM((PAD + R * C * 2 * S, S), f32),
            pltpu.VMEM((R * S, S), f32),
            pltpu.VMEM((2 * PAD + 2 * C * H, S), f32),
            pltpu.VMEM((R * S, S), f32),
            pltpu.VMEM((4 * R * C, S), f32),
            pltpu.VMEM((3, S), f32),
            pltpu.VMEM((ndev, 3, S), f32),
            pltpu.VMEM((6, ndev, S), f32),
            pltpu.SMEM((4, R, C), jnp.int32),
            pltpu.VMEM((n_relays(R) * S, S), f32),
            pltpu.VMEM((min(2, R) * S, S), f32),
            pltpu.VMEM((min(2, R) * S, S), f32),
            pltpu.VMEM((16, S), f32),
            dma((len(load_groups(R)),)), dma((1,)),
            dma((1,)), dma((len(arrive_groups(R)),)),
            dma((1,)), dma((1,)),
            dma((1,)), dma((1,)),
            dma((1,)),
            pltpu.SemaphoreType.REGULAR((n_rounds(nr) + n_rounds(nc),)),
            dma((n_relays(R),)), dma((n_relays(R),)),
            dma((min(2, R),)), dma((min(2, R),)),
            pltpu.SemaphoreType.REGULAR((1,)),
        ],
        compiler_params=pltpu.CompilerParams(
            collective_id=0, has_side_effects=True, vmem_limit_bytes=24 << 20
        ),
        name="sync_patches",
    )(*(pltpu.with_memory_space_constraint(x, pltpu.HBM) for x in (flat, *tables)))
    pair = 2
    blended, phases = pl.pallas_call(
        functools.partial(blend_kernel, (R, C, S, pair)),
        out_shape=(
            jax.ShapeDtypeStruct((R * C * 2 * S, S), f32),
            jax.ShapeDtypeStruct((2, R, C), f32),
        ),
        in_specs=[vmem] * 5,
        out_specs=(anyspec, anyspec),
        scratch_shapes=[
            pltpu.VMEM((R * C * 2 * S, S), f32),
            pltpu.VMEM((2, R, C), f32),
            dma((1,)),
            dma((1,)),
        ],
        compiler_params=pltpu.CompilerParams(vmem_limit_bytes=24 << 20),
        name="blend_patches",
    )(*parts)
    return blended.reshape(patches.shape), phases


def solution(mesh):
    return jax.shard_map(
        functools.partial(local, mesh.shape["row"], mesh.shape["col"]),
        mesh=mesh,
        in_specs=(P("row", "col", None, None, None),) + (P("row", "col"),) * 4,
        out_specs=(P("row", "col", None, None, None), P(None, "row", "col")),
        check_vma=False,
    )
```

```python
import functools

import jax
import jax.numpy as jnp
from jax import lax
from jax.experimental import pallas as pl
from jax.experimental.pallas import tpu as pltpu
from jax.sharding import PartitionSpec as P

ITERS = 2
PAD = 64
eps_norm = 1.0
highest = lax.Precision.HIGHEST
MESH = pl.DeviceIdType.MESH
f32 = jnp.float32


def fold_rows(x):
    return jnp.sum(x, axis=0, keepdims=True)


def doubling(pos, n, at):
    if n == 1:
        return []
    rounds = [[at(-1) + (pos > 0, pos < n - 1)]]
    known = 1
    while known < n - 1:
        rounds.append([
            at(-known) + (pos >= known, pos < n - known),
            at(known) + (pos < n - known, pos >= known),
        ])
        known *= 2
    return rounds


def groups(n, sizes):
    runs, first = [], 0
    while first < n:
        size = sizes[min(len(runs), len(sizes) - 1)]
        runs.append(range(first, min(n, first + size)))
        first += size
    return runs


def n_relays(n):
    return min(3, n // 2)


def load_groups(n):
    return groups(n, (1, 1, 2, 4))


def arrive_groups(n):
    return groups(n - 2, (max(1, n - 4), 2)) + [range(n - 2, n - 1), range(n - 1, n)] if n > 4 else groups(n, (1,))


def send_runs(n):
    runs = []
    for run in arrive_groups(n):
        runs += [run[:1], run[1:]] if run[0] == 0 and len(run) > 1 else [run]
    return runs


def n_rounds(n):
    return len(doubling(0, n, lambda k: (0, 0)))


def sync_kernel(
    dims, patches, ro_in, rw_in, do_in, dw_in, aw, ew, sw, factors, phase_out,
    pv, east_recv, south_recv,
    epack, acc, send_buf, recv, fields, table, relay_buf, strips, turned, late,
    col_sem, rest_sem, e_send, e_recv, s_send, s_recv, g_send, g_recv, table_sem, round_sem,
    relay_recv, relay_send, turn_recv, turn_send, pair_sem,
):
    R, C, S, nr, nc = dims
    H, ndev = S // 2, nr * nc
    lo = H - 8
    T = S - lo
    my_row, my_col = lax.axis_index("row"), lax.axis_index("col")
    me = my_row * nc + my_col
    last_col, last_row = my_col == nc - 1, my_row == nr - 1
    even = lax.rem(my_col, 2) == 0
    opens = even & (my_col >= max(2, nc - 4)) & (my_col < nc - 1)
    closes = jnp.logical_not(even) & (my_col >= max(3, nc - 3))
    n_relay, n_turn = n_relays(R), min(2, R)

    def relayed(c):
        return jnp.where(c == nc - 2, n_relay, 0)

    def turned_of(c):
        return jnp.where(c == nc - 2, n_turn, 1)

    def sent_around(i):
        return opens & (i >= R - relayed(my_col))

    def turned_here(i):
        return opens & (i >= R - turned_of(my_col))

    def skip(k, mine):
        return k + (k >= mine).astype(jnp.int32)

    others = [(a, skip(b, my_col)) for b in range(nc - 1) for a in range(nr)]
    others += [(skip(a, my_row), my_col) for a in range(nr - 1)]
    barrier = pltpu.get_barrier_semaphore()

    def signal(sem, row, col, there):
        @pl.when(there)
        def _():
            pl.semaphore_signal(sem, inc=1, device_id=(row, col), device_id_type=MESH)

    def await_all(sem, *due):
        amount = sum(one.astype(jnp.int32) for one in due)

        @pl.when(amount > 0)
        def _():
            pl.semaphore_wait(sem, amount)

    steps = doubling(my_row, nr, lambda k: (my_row + k, my_col))
    steps += doubling(my_col, nc, lambda k: (my_row, my_col + k))

    def tell(k):
        for row, col, there, _ in steps[k]:
            signal(round_sem.at[k], row, col, there)

    def spread(k):
        if k < len(steps):
            await_all(round_sem.at[k], *(here for _, _, _, here in steps[k]))
            if k + 1 < len(steps):
                tell(k + 1)

    load_sem = {i: g for g, run in enumerate(load_groups(R)) for i in run}
    cols = [
        pltpu.make_async_copy(
            patches.at[pl.ds(i * C * 2 * S, 2 * S)],
            pv.at[pl.ds(PAD + i * C * 2 * S, 2 * S)],
            col_sem.at[load_sem[i]],
        )
        for i in range(R)
    ]
    rests = [
        pltpu.make_async_copy(
            patches.at[pl.ds((i * C + 1) * 2 * S, (C - 1) * 2 * S)],
            pv.at[pl.ds(PAD + (i * C + 1) * 2 * S, (C - 1) * 2 * S)],
            rest_sem.at[0],
        )
        for i in range(R)
    ]
    tables = [
        pltpu.make_async_copy(here, table.at[k], table_sem.at[0])
        for k, here in enumerate((ro_in, rw_in, do_in, dw_in))
    ]
    ro, rw, do, dw = (table.at[k] for k in range(4))

    def whole(src, dst, sem):
        return pltpu.make_async_copy(src, dst, sem)

    signal(barrier, my_row, my_col + 1, my_col < nc - 1)
    for copy in cols:
        copy.start()
    signal(barrier, my_row + 1, my_col, my_row < nr - 1)
    lane = lax.broadcasted_iota(jnp.int32, (S, S), 1)

    def load(g):
        size = len(load_groups(R)[g]) * 2 * S
        whole(patches.at[pl.ds(0, size)], pv.at[pl.ds(PAD, size)], col_sem.at[g]).wait()

    def pack(i):
        base = PAD + i * C * 2 * S
        re = pv[pl.ds(base, S), :]
        im = pv[pl.ds(base + S, S), :]
        epack[pl.ds(i * S, S), :] = jnp.where(lane < H, re, pltpu.roll(im, H, 1))

    def south_copy(k, row):
        return pltpu.make_async_remote_copy(
            src_ref=patches.at[pl.ds(k * S, H)],
            dst_ref=south_recv.at[pl.ds(PAD + k * H, H)],
            send_sem=s_send.at[0],
            recv_sem=s_recv.at[0],
            device_id=(row, my_col),
            device_id_type=MESH,
        )

    def all_south(row):
        return pltpu.make_async_remote_copy(
            src_ref=patches.at[pl.ds(0, 2 * C * H)],
            dst_ref=south_recv.at[pl.ds(PAD, 2 * C * H)],
            send_sem=s_send.at[0],
            recv_sem=s_recv.at[0],
            device_id=(row, my_col),
            device_id_type=MESH,
        )

    arrive_sem = {i: g for g, run in enumerate(arrive_groups(R)) for i in run}

    def east_run(first, n, sem, col):
        return pltpu.make_async_remote_copy(
            src_ref=epack.at[pl.ds(first * S, n * S)],
            dst_ref=east_recv.at[pl.ds(first * S, n * S)],
            send_sem=e_send.at[0],
            recv_sem=e_recv.at[sem],
            device_id=(my_row, col),
            device_id_type=MESH,
        )

    def east_copy(k, col):
        return east_run(k, 1, arrive_sem[k], col)

    def send_east(run):
        around = sent_around(run[-1]) if run[-1] >= R - n_relay else False

        @pl.when((my_col > 0) & jnp.logical_not(around))
        def _():
            east_run(run[0], len(run), arrive_sem[run[0]], my_col - 1).start()

        if len(run) > 1 and run[-1] >= R - n_relay:
            for i in run:

                @pl.when(around & jnp.logical_not(sent_around(i)))
                def _():
                    east_copy(i, my_col - 1).start()

    def relay_copy(i, col):
        k = i - (R - n_relay)
        return pltpu.make_async_remote_copy(
            src_ref=epack.at[pl.ds(i * S, S)],
            dst_ref=relay_buf.at[pl.ds(k * S, S)],
            send_sem=e_send.at[0],
            recv_sem=relay_recv.at[k],
            device_id=(my_row, col),
            device_id_type=MESH,
        )

    def forward_copy(i, col):
        k = i - (R - n_relay)
        return pltpu.make_async_remote_copy(
            src_ref=relay_buf.at[pl.ds(k * S, S)],
            dst_ref=east_recv.at[pl.ds(i * S, S)],
            send_sem=relay_send.at[k],
            recv_sem=e_recv.at[arrive_sem[i]],
            device_id=(my_row, col),
            device_id_type=MESH,
        )

    def forwards(i):
        return closes & (i >= R - relayed(my_col - 1))

    def forward(i):
        if i < R:

            @pl.when(forwards(i))
            def _():
                relay_copy(i, my_col).wait_recv()
                forward_copy(i, my_col - 2).start()

    def turn_copy(i, col):
        k = i - (R - n_turn)
        return pltpu.make_async_remote_copy(
            src_ref=strips.at[pl.ds(k * S, S)],
            dst_ref=turned.at[pl.ds(k * S, S)],
            send_sem=turn_send.at[k],
            recv_sem=turn_recv.at[k],
            device_id=(my_row, col),
            device_id_type=MESH,
        )

    @pl.when(closes)
    def _():
        await_all(barrier, my_row > 0, my_col > 0)
        signal(pair_sem.at[0], my_row, my_col - 1, closes)

    load(0)
    for copy in tables:
        copy.start()
    for copy in rests:
        copy.start()
    pack(0)

    @pl.when(jnp.logical_not(closes))
    def _():
        await_all(barrier, my_row > 0, my_col > 0)

    send_east(send_runs(R)[0])
    sent = 1
    for g, run in enumerate(load_groups(R)):
        if g:
            load(g)
            for i in run:
                pack(i)
                if i == send_runs(R)[sent][-1]:
                    send_east(send_runs(R)[sent])
                    sent += 1
        if g == 1 or len(load_groups(R)) == 1:

            @pl.when(my_row > 0)
            def _():
                for k in range(2 * C):
                    south_copy(k, my_row - 1).start()

            if steps:
                tell(0)
    acc[...] = jnp.zeros_like(acc)
    late[...] = jnp.zeros_like(late)
    await_all(pair_sem.at[0], opens)
    for i in range(R - n_relay, R):

        @pl.when(sent_around(i))
        def _():
            relay_copy(i, my_col + 1).start()

    spread(0)
    whole(table, table, table_sem.at[0]).wait()
    size = R * (C - 1) * 2 * S
    whole(patches.at[pl.ds(0, size)], pv.at[pl.ds(PAD, size)], rest_sem.at[0]).wait()

    lane1 = lax.broadcasted_iota(jnp.int32, (1, S), 1)
    row8 = lax.broadcasted_iota(jnp.int32, (8, S), 0)

    for i in range(R - n_turn, R):

        @pl.when(turned_here(i))
        def _():
            o, w = ro[i, C - 1], rw[i, C - 1]
            base = PAD + (i * C + C - 1) * 2 * S
            scale = 1.0 / jnp.sqrt(jnp.full((1, S), S * w, jnp.int32).astype(f32))
            weight = jnp.where((lane1 & (H - 1)) < w, scale, 0.0)
            re = pltpu.roll(pv[pl.ds(base, S), :], S - o, 1)
            im = pltpu.roll(pv[pl.ds(base + S, S), :], lax.rem(S + H - o, S), 1)
            strips[pl.ds((i - R + n_turn) * S, S), :] = jnp.where(lane < H, re, im) * weight
            turn_copy(i, my_col + 1).start()

    def at(ref, row):
        return ref[pl.ds(pl.multiple_of(row, 8), 8), :]

    def put_at(ref, row, value):
        ref[pl.ds(pl.multiple_of(row, 8), 8), :] = value

    def scaled(re, im, width):
        scale = 1.0 / jnp.sqrt(jnp.full((1, S), S * width, jnp.int32).astype(f32))
        return fold_rows(re) * scale, fold_rows(im) * scale

    def put(plane, p, re, im, width):
        re, im = scaled(re, im, width)
        acc[pl.ds(plane * R * C + p, 1), :] = re
        acc[pl.ds((plane + 1) * R * C + p, 1), :] = im

    def gathered(pieces):
        re, im = None, None
        for a_re, a_im, b_re, b_im in pieces:
            u, v = a_re * b_re + a_im * b_im, a_re * b_im - a_im * b_re
            re, im = (u, v) if re is None else (re + u, im + v)
        return re, im

    def weights(i, j, within):
        o, w = ro[i, j], rw[i, j]
        keep = (lane1 >= o) & (lane1 < o + w)
        live = keep if j < C - 1 else keep & jnp.logical_not(last_col)
        half = jnp.where(live, f32(0.5), f32(1.0))
        third = jnp.where(live, f32(1.0 / 3.0), f32(0.5))
        down = jnp.logical_not((i == R - 1) & last_row)
        third = jnp.where(jnp.full((1, S), down), third, half)
        if within:
            half, third = jnp.where(keep, half, 0.0), jnp.where(keep, third, 0.0)
        return jnp.broadcast_to(half, (8, S)), jnp.broadcast_to(third, (8, S))

    def reached(i, j, q):
        o, w = do[i, j], dw[i, j]
        return row8 >= o - q if q < S - 8 else row8 < o + w - q

    def weight_at(i, j, q, half, third):
        return half if q < lo else jnp.where(reached(i, j, q), third, half)

    def rows_of(p):
        return PAD + p * 2 * S

    def east_of(i, j):
        base = rows_of(i * C + j + 1)

        def load(q, o):
            return pltpu.roll(at(pv, base + q), o, 1), pltpu.roll(at(pv, base + S + q), o, 1)

        return load

    def east_rim(i):
        def load(q, o):
            both = at(east_recv, i * S + q)
            return pltpu.roll(both, o, 1), pltpu.roll(both, lax.rem(o + H, S), 1)

        return load

    def place_east(i, j, q, b, half, third):
        to = (i * C + j) * 2 * S + q
        weight = weight_at(i, j, q, half, third)
        put_at(ew, to, b[0] * weight)
        put_at(ew, to + S, b[1] * weight)

    def east_sums(i, j, load, place):
        p = i * C + j
        o, w = ro[i, j], rw[i, j]
        base = rows_of(p)
        half, third = weights(i, j, True)

        def piece(q):
            b = load(q, o)
            if place:
                place_east(i, j, q, b, half, third)
            return (at(pv, base + q), at(pv, base + S + q)) + b

        re, im = gathered(piece(q) for q in range(0, S, 8))
        keep = (lane1 >= o) & (lane1 < o + w)
        return p, jnp.where(keep, re, 0.0), jnp.where(keep, im, 0.0), w

    def east_inner(i, carry):
        for j in range(C - 1):
            put(0, *east_sums(i, j, east_of(i, j), True))
        return carry

    def south_store(i, j, ref, start, gap):
        p = i * C + j
        o, w = do[i, j], dw[i, j]
        base = rows_of(p)
        _, third = weights(i, j, False)

        def piece(q):
            keep = reached(i, j, q)
            b_re = jnp.where(keep, ref[pl.ds(start + (q - o), 8), :], 0.0)
            b_im = jnp.where(keep, ref[pl.ds(start + gap + (q - o), 8), :], 0.0)
            to = p * 2 * T + q - lo
            put_at(sw, to, b_re * third)
            put_at(sw, to + T, b_im * third)
            return at(pv, base + q), at(pv, base + S + q), b_re, b_im

        re, im = gathered(piece(q) for q in range(lo, S, 8))
        put(2, p, re, im, w)

    def south_inner(i, carry):
        for j in range(C):
            south_store(i, j, pv, rows_of((i + 1) * C + j), S)
        return carry

    spread(1)
    lax.fori_loop(0, R // 2, east_inner, 0)
    spread(2)
    forward(R - n_relay)
    lax.fori_loop(R // 2, R, east_inner, 0)
    spread(3)
    forward(R - n_relay + 1)
    lax.fori_loop(0, R // 2, south_inner, 0)
    spread(4)
    forward(R - n_relay + 2)
    lax.fori_loop(R // 2, R - 1, south_inner, 0)
    spread(5)

    @pl.when(my_row < nr - 1)
    def _():
        all_south(my_row).wait_recv()

    @pl.when(last_row)
    def _():
        south_recv[...] = jnp.zeros_like(south_recv)

    for j in range(C):
        south_store(R - 1, j, south_recv, PAD + j * 2 * H, H)

    for k in range(6, len(steps)):
        spread(k)

    @pl.when(last_col)
    def _():
        east_recv[...] = jnp.zeros_like(east_recv)

    def east_wait(g):
        run = arrive_groups(R)[g]
        east_run(run[0], len(run), g, my_col).wait_recv()

    def rim_row(i):
        return 2 * (i - (R - n_late))

    n_late = min(2, R)
    for g, run in enumerate(arrive_groups(R)):
        if run[-1] < R - n_late:

            @pl.when(jnp.logical_not(last_col))
            def _():
                east_wait(g)

            for i in run:
                put(0, *east_sums(i, C - 1, east_rim(i), False))
    sums = lax.dot_general(
        jnp.ones((8, S), f32), acc[...], (((1,), (1,)), ((), ())),
        precision=highest, preferred_element_type=f32,
    )

    def rim(i):
        @pl.when(jnp.logical_not(last_col) & jnp.logical_not(turned_here(i)))
        def _():
            east_wait(arrive_sem[i])
            _, re, im, width = east_sums(i, C - 1, east_rim(i), False)
            re, im = scaled(re, im, width)
            late[rim_row(i) : rim_row(i) + 1, :] = re
            late[rim_row(i) + 1 : rim_row(i) + 2, :] = im

    def turn_row(i):
        return 2 * n_late + 2 * (i - (R - n_turn))

    def turn(i):
        @pl.when(closes & (i >= R - turned_of(my_col - 1)))
        def _():
            turn_copy(i, my_col).wait_recv()
            re, im = None, None
            for q in range(0, S, 8):
                a = at(turned, (i - R + n_turn) * S + q)
                b = at(epack, i * S + q)
                u, v = a * b, a * pltpu.roll(b, H, 1)
                re, im = (u, v) if re is None else (re + u, im + v)
            im = jnp.where(lane1 < H, im, -im)
            late[turn_row(i) : turn_row(i) + 1, :] = fold_rows(re)
            late[turn_row(i) + 1 : turn_row(i) + 2, :] = fold_rows(im)

    for i in range(R - n_late, R):
        if i == R - 1:
            for k in range(R - n_turn, R):
                turn(k)
        rim(i)
    tails = jnp.sum(late[...], axis=1, keepdims=True)

    def spot(i, part, row):
        return jnp.where(lane1 == part * R * C + i * C + C - 1, tails[row : row + 1, :], 0.0)

    east_row, turn_line = sums[0:1, :S], jnp.zeros((1, S), f32)
    for part in range(2):
        for i in range(R - n_late, R):
            east_row = east_row + spot(i, part, rim_row(i) + part)
        for i in range(R - n_turn, R):
            turn_line = turn_line + spot(i, part, turn_row(i) + part)
    mine = jnp.concatenate([east_row, sums[0:1, S:], turn_line], axis=0)
    send_buf[...] = mine
    recv[me] = mine

    def index(d):
        return d[0] * nc + d[1]

    def gather_copy(target, source):
        return pltpu.make_async_remote_copy(
            src_ref=send_buf,
            dst_ref=recv.at[index(source)],
            send_sem=g_send.at[0],
            recv_sem=g_recv.at[0],
            device_id=target,
            device_id_type=MESH,
        )

    def all_gathered():
        return pltpu.make_async_remote_copy(
            src_ref=recv.at[pl.ds(0, ndev - 1)],
            dst_ref=recv.at[pl.ds(0, ndev - 1)],
            send_sem=g_send.at[0],
            recv_sem=g_recv.at[0],
            device_id=others[0],
            device_id_type=MESH,
        )

    for other in others:
        gather_copy(other, (my_row, my_col)).start()

    def weigh(i, carry):
        for j in range(C):
            half, third = weights(i, j, False)
            base, to = rows_of(i * C + j), (i * C + j) * 2 * S
            for q in range(0, S, 8):
                weight = weight_at(i, j, q, half, third)
                put_at(aw, to + q, at(pv, base + q) * weight)
                put_at(aw, to + S + q, at(pv, base + S + q) * weight)
        return carry

    def weigh_rim(i, carry):
        half, third = weights(i, C - 1, True)
        load, o = east_rim(i), ro[i, C - 1]
        for q in range(0, S, 8):
            place_east(i, C - 1, q, load(q, o), half, third)
        return carry

    lax.fori_loop(0, R, weigh, 0)
    for i in range(R - n_turn, R):

        @pl.when(turned_here(i))
        def _():
            east_wait(arrive_sem[i])

    lax.fori_loop(0, R, weigh_rim, 0)

    all_gathered().wait_recv()

    got = recv[...]
    east, south = got[:, 0, :] + pltpu.roll(got[:, 2, :], ndev - 1, 0), got[:, 1, :]
    field = lax.broadcasted_iota(jnp.int32, (ndev, S), 0)
    slot = lax.broadcasted_iota(jnp.int32, (ndev, S), 1)
    valid = slot < R * C
    j_of, i_of = slot % C, (slot // C) % R
    dc, dr = field % nc, field // nc

    def roll(x, by, axis):
        return pltpu.roll(x, by % x.shape[axis], axis)

    def from_east(x):
        far = roll(roll(x, -1, 0), C - 1, 1)
        far = jnp.where(dc < nc - 1, far, 0.0)
        return jnp.where(j_of < C - 1, roll(x, -1, 1), far)

    def from_west(x):
        far = roll(roll(x, 1, 0), 1 - C, 1)
        far = jnp.where(dc > 0, far, 0.0)
        return jnp.where(j_of > 0, roll(x, 1, 1), far)

    def from_south(x):
        far = roll(roll(x, -nc, 0), (R - 1) * C, 1)
        far = jnp.where(dr < nr - 1, far, 0.0)
        return jnp.where(i_of < R - 1, roll(x, -C, 1), far)

    def from_north(x):
        far = roll(roll(x, nc, 0), -(R - 1) * C, 1)
        far = jnp.where(dr > 0, far, 0.0)
        return jnp.where(i_of > 0, roll(x, C, 1), far)

    ce = (jnp.where(valid, east, 0.0), jnp.where(valid, roll(east, -R * C, 1), 0.0))
    cs = (jnp.where(valid, south, 0.0), jnp.where(valid, roll(south, -R * C, 1), 0.0))
    cw = tuple(from_west(x) for x in ce)
    cn = tuple(from_north(x) for x in cs)
    mean = 1.0 / float(ndev * R * C)

    def times(a, b):
        return (a[0] * b[0] - a[1] * b[1], a[0] * b[1] + a[1] * b[0])

    def conj_times(a, b):
        return (a[0] * b[0] + a[1] * b[1], a[0] * b[1] - a[1] * b[0])

    now = (ce[0] + cs[0] + cw[0] + cn[0], ce[1] + cs[1] - cw[1] - cn[1])
    now = tuple(jnp.where(valid, x, 0.0) for x in now)
    square = now[0] * now[0] + now[1] * now[1]
    constant = eps_norm
    for step in range(1, ITERS):
        terms = (
            times(ce, tuple(from_east(x) for x in now)),
            times(cs, tuple(from_south(x) for x in now)),
            conj_times(cw, tuple(from_west(x) for x in now)),
            conj_times(cn, tuple(from_north(x) for x in now)),
        )
        now = tuple(
            jnp.where(valid, terms[0][q] + terms[1][q] + terms[2][q] + terms[3][q], 0.0)
            for q in range(2)
        )
        square = eps_norm * square + (now[0] * now[0] + now[1] * now[1])
        constant = constant * eps_norm
    outs = now + tuple(from_east(x) for x in now) + tuple(from_south(x) for x in now)
    for q in range(6):
        fields[q] = outs[q]
    total = jnp.sum(jnp.sum(square, axis=0, keepdims=True), axis=1, keepdims=True)
    factor = 1.0 / jnp.sqrt(total * mean + constant)
    diagonal = lax.broadcasted_iota(jnp.int32, (R * C, S), 0) == lax.broadcasted_iota(
        jnp.int32, (R * C, S), 1
    )
    for q in range(6):
        row = fields[q, pl.ds(me, 1), :]
        phase_out[q : q + 1, :] = row * factor
        only = jnp.where(diagonal, jnp.broadcast_to(row, (R * C, S)), 0.0)
        factors[q * R * C : (q + 1) * R * C, :] = (
            jnp.broadcast_to(jnp.sum(only, axis=1, keepdims=True), (R * C, S)) * factor
        )

    all_gathered().wait_send()

    @pl.when(my_col > 0)
    def _():
        east_run(0, R, 0, my_col - 1).wait_send()

    for i in range(R - n_relay, R):

        @pl.when(forwards(i))
        def _():
            forward_copy(i, my_col - 2).wait_send()

    for i in range(R - n_turn, R):

        @pl.when(turned_here(i))
        def _():
            turn_copy(i, my_col + 1).wait_send()

    @pl.when(my_row > 0)
    def _():
        all_south(my_row - 1).wait_send()


def blend_kernel(dims, aw, ew, sw, factors, phase, out, phases, ov, pad, out_sem, phase_sem):
    R, C, S, pair = dims
    lo = S // 2 - 8
    T = S - lo
    piece = pair * 2 * S

    def save(k):
        return pltpu.make_async_copy(
            ov.at[pl.ds(k * piece, piece)], out.at[pl.ds(k * piece, piece)], out_sem.at[0]
        )

    def at(ref, row):
        return ref[pl.ds(pl.multiple_of(row, 8), 8), :]

    def times(g, a):
        return g[0] * a[0] - g[1] * a[1], g[0] * a[1] + g[1] * a[0]

    def place(p):
        g, ge, gs = (
            [jnp.broadcast_to(factors[pl.ds((2 * k + part) * R * C + p, 1), :], (8, S)) for part in range(2)]
            for k in range(3)
        )
        base = p * 2 * S
        for q in range(0, S, 8):
            own = times(g, (at(aw, base + q), at(aw, base + S + q)))
            east = times(ge, (at(ew, base + q), at(ew, base + S + q)))
            sums = [own[part] + east[part] for part in range(2)]
            if q >= lo:
                down = p * 2 * T + q - lo
                south = times(gs, (at(sw, down), at(sw, down + T)))
                sums = [sums[part] + south[part] for part in range(2)]
            ov[pl.ds(pl.multiple_of(base + q, 8), 8), :] = sums[0]
            ov[pl.ds(pl.multiple_of(base + S + q, 8), 8), :] = sums[1]

    def step(k, carry):
        for n in range(pair):
            place(k * pair + n)
        save(k).start()
        return carry

    lax.fori_loop(0, R * C // pair, step, 0)

    row8 = lax.broadcasted_iota(jnp.int32, (R, S), 0)
    for part in range(2):
        line = jnp.broadcast_to(phase[part : part + 1, :], (R, S))
        plane = line
        for i in range(1, R):
            plane = jnp.where(row8 == i, pltpu.roll(line, S - i * C, 1), plane)
        pad[part] = plane[:, :C]
    send = pltpu.make_async_copy(pad, phases, phase_sem.at[0])
    send.start()
    send.wait()
    pltpu.make_async_copy(ov, out, out_sem.at[0]).wait()


def local(nr, nc, patches, right_offset, right_width, down_offset, down_width):
    R, C, _, S, _ = patches.shape
    H, ndev = S // 2, nr * nc
    T = S - (H - 8)
    dims = (R, C, S, nr, nc)
    flat = patches.reshape(R * C * 2 * S, S)
    anyspec = pl.BlockSpec(memory_space=pl.ANY)
    vmem = pl.BlockSpec(memory_space=pltpu.VMEM)
    dma = pltpu.SemaphoreType.DMA
    tables = (right_offset, right_width, down_offset, down_width)
    parts = pl.pallas_call(
        functools.partial(sync_kernel, dims),
        out_shape=(
            pltpu.VMEM((R * C * 2 * S, S), f32),
            pltpu.VMEM((R * C * 2 * S, S), f32),
            pltpu.VMEM((R * C * 2 * T, S), f32),
            pltpu.VMEM((6 * R * C, S), f32),
            pltpu.VMEM((8, S), f32),
        ),
        in_specs=[pl.BlockSpec(memory_space=pltpu.HBM)] * 5,
        out_specs=(vmem,) * 5,
        scratch_shapes=[
            pltpu.VMEM((PAD + R * C * 2 * S, S), f32),
            pltpu.VMEM((R * S, S), f32),
            pltpu.VMEM((2 * PAD + 2 * C * H, S), f32),
            pltpu.VMEM((R * S, S), f32),
            pltpu.VMEM((4 * R * C, S), f32),
            pltpu.VMEM((3, S), f32),
            pltpu.VMEM((ndev, 3, S), f32),
            pltpu.VMEM((6, ndev, S), f32),
            pltpu.SMEM((4, R, C), jnp.int32),
            pltpu.VMEM((n_relays(R) * S, S), f32),
            pltpu.VMEM((min(2, R) * S, S), f32),
            pltpu.VMEM((min(2, R) * S, S), f32),
            pltpu.VMEM((16, S), f32),
            dma((len(load_groups(R)),)), dma((1,)),
            dma((1,)), dma((len(arrive_groups(R)),)),
            dma((1,)), dma((1,)),
            dma((1,)), dma((1,)),
            dma((1,)),
            pltpu.SemaphoreType.REGULAR((n_rounds(nr) + n_rounds(nc),)),
            dma((n_relays(R),)), dma((n_relays(R),)),
            dma((min(2, R),)), dma((min(2, R),)),
            pltpu.SemaphoreType.REGULAR((1,)),
        ],
        compiler_params=pltpu.CompilerParams(
            collective_id=0, has_side_effects=True, vmem_limit_bytes=24 << 20
        ),
        name="sync_patches",
    )(*(pltpu.with_memory_space_constraint(x, pltpu.HBM) for x in (flat, *tables)))
    pair = 2
    blended, phases = pl.pallas_call(
        functools.partial(blend_kernel, (R, C, S, pair)),
        out_shape=(
            jax.ShapeDtypeStruct((R * C * 2 * S, S), f32),
            jax.ShapeDtypeStruct((2, R, C), f32),
        ),
        in_specs=[vmem] * 5,
        out_specs=(anyspec, anyspec),
        scratch_shapes=[
            pltpu.VMEM((R * C * 2 * S, S), f32),
            pltpu.VMEM((2, R, C), f32),
            dma((1,)),
            dma((1,)),
        ],
        compiler_params=pltpu.CompilerParams(vmem_limit_bytes=24 << 20),
        name="blend_patches",
    )(*parts)
    return blended.reshape(patches.shape), phases


def solution(mesh):
    return jax.shard_map(
        functools.partial(local, mesh.shape["row"], mesh.shape["col"]),
        mesh=mesh,
        in_specs=(P("row", "col", None, None, None),) + (P("row", "col"),) * 4,
        out_specs=(P("row", "col", None, None, None), P(None, "row", "col")),
        check_vma=False,
    )
```

```python
import functools

import jax
import jax.numpy as jnp
from jax import lax
from jax.experimental import pallas as pl
from jax.experimental.pallas import tpu as pltpu
from jax.sharding import PartitionSpec as P

ITERS = 2
PAD = 64
eps_norm = 1.0
highest = lax.Precision.HIGHEST
MESH = pl.DeviceIdType.MESH
f32 = jnp.float32


def fold_rows(x):
    return jnp.sum(x, axis=0, keepdims=True)


def doubling(pos, n, at):
    if n == 1:
        return []
    rounds = [[at(-1) + (pos > 0, pos < n - 1)]]
    known = 1
    while known < n - 1:
        rounds.append([
            at(-known) + (pos >= known, pos < n - known),
            at(known) + (pos < n - known, pos >= known),
        ])
        known *= 2
    return rounds


def groups(n, sizes):
    runs, first = [], 0
    while first < n:
        size = sizes[min(len(runs), len(sizes) - 1)]
        runs.append(range(first, min(n, first + size)))
        first += size
    return runs


def n_relays(n):
    return min(3, n // 2)


def load_groups(n):
    return groups(n, (1, 1, 2, 4))


def arrive_groups(n):
    return groups(n - 2, (max(1, n - 4), 2)) + [range(n - 2, n - 1), range(n - 1, n)] if n > 4 else groups(n, (1,))


def send_runs(n):
    runs = []
    for run in arrive_groups(n):
        runs += [run[:1], run[1:]] if run[0] == 0 and len(run) > 1 else [run]
    return runs


def n_rounds(n):
    return len(doubling(0, n, lambda k: (0, 0)))


def sync_kernel(
    dims, patches, ro_in, rw_in, do_in, dw_in, aw, ew, sw, factors, phase_out,
    pv, east_recv, south_recv,
    epack, acc, send_buf, recv, fields, table, relay_buf, strips, turned, late,
    col_sem, rest_sem, e_send, e_recv, s_send, s_recv, g_send, g_recv, table_sem, round_sem,
    relay_recv, turn_recv, pair_sem,
):
    R, C, S, nr, nc = dims
    H, ndev = S // 2, nr * nc
    lo = H - 8
    T = S - lo
    my_row, my_col = lax.axis_index("row"), lax.axis_index("col")
    me = my_row * nc + my_col
    last_col, last_row = my_col == nc - 1, my_row == nr - 1
    even = lax.rem(my_col, 2) == 0
    opens = even & (my_col >= max(2, nc - 4)) & (my_col < nc - 1)
    closes = jnp.logical_not(even) & (my_col >= max(3, nc - 3))
    n_relay, n_turn = n_relays(R), min(2, R)

    def relayed(c):
        return jnp.where(c == nc - 2, n_relay, 0)

    def turned_of(c):
        return jnp.where(c == nc - 2, n_turn, 1)

    def sent_around(i):
        return opens & (i >= R - relayed(my_col))

    def turned_here(i):
        return opens & (i >= R - turned_of(my_col))

    def skip(k, mine):
        return k + (k >= mine).astype(jnp.int32)

    others = [(a, skip(b, my_col)) for b in range(nc - 1) for a in range(nr)]
    others += [(skip(a, my_row), my_col) for a in range(nr - 1)]
    barrier = pltpu.get_barrier_semaphore()

    def signal(sem, row, col, there):
        @pl.when(there)
        def _():
            pl.semaphore_signal(sem, inc=1, device_id=(row, col), device_id_type=MESH)

    def await_all(sem, *due):
        amount = sum(one.astype(jnp.int32) for one in due)

        @pl.when(amount > 0)
        def _():
            pl.semaphore_wait(sem, amount)

    steps = doubling(my_row, nr, lambda k: (my_row + k, my_col))
    steps += doubling(my_col, nc, lambda k: (my_row, my_col + k))

    def tell(k):
        for row, col, there, _ in steps[k]:
            signal(round_sem.at[k], row, col, there)

    def spread(k):
        if k < len(steps):
            await_all(round_sem.at[k], *(here for _, _, _, here in steps[k]))
            if k + 1 < len(steps):
                tell(k + 1)

    load_sem = {i: g for g, run in enumerate(load_groups(R)) for i in run}
    cols = [
        pltpu.make_async_copy(
            patches.at[pl.ds(i * C * 2 * S, 2 * S)],
            pv.at[pl.ds(PAD + i * C * 2 * S, 2 * S)],
            col_sem.at[load_sem[i]],
        )
        for i in range(R)
    ]
    rests = [
        pltpu.make_async_copy(
            patches.at[pl.ds((i * C + 1) * 2 * S, (C - 1) * 2 * S)],
            pv.at[pl.ds(PAD + (i * C + 1) * 2 * S, (C - 1) * 2 * S)],
            rest_sem.at[0],
        )
        for i in range(R)
    ]
    tables = [
        pltpu.make_async_copy(here, table.at[k], table_sem.at[0])
        for k, here in enumerate((ro_in, rw_in, do_in, dw_in))
    ]
    ro, rw, do, dw = (table.at[k] for k in range(4))

    def whole(src, dst, sem):
        return pltpu.make_async_copy(src, dst, sem)

    signal(barrier, my_row, my_col + 1, my_col < nc - 1)
    for copy in cols:
        copy.start()
    signal(barrier, my_row + 1, my_col, my_row < nr - 1)
    lane = lax.broadcasted_iota(jnp.int32, (S, S), 1)

    def load(g):
        size = len(load_groups(R)[g]) * 2 * S
        whole(patches.at[pl.ds(0, size)], pv.at[pl.ds(PAD, size)], col_sem.at[g]).wait()

    def pack(i):
        base = PAD + i * C * 2 * S
        re = pv[pl.ds(base, S), :]
        im = pv[pl.ds(base + S, S), :]
        epack[pl.ds(i * S, S), :] = jnp.where(lane < H, re, pltpu.roll(im, H, 1))

    def south_copy(k, row):
        return pltpu.make_async_remote_copy(
            src_ref=patches.at[pl.ds(k * S, H)],
            dst_ref=south_recv.at[pl.ds(PAD + k * H, H)],
            send_sem=s_send.at[0],
            recv_sem=s_recv.at[0],
            device_id=(row, my_col),
            device_id_type=MESH,
        )

    def all_south(row):
        return pltpu.make_async_remote_copy(
            src_ref=patches.at[pl.ds(0, 2 * C * H)],
            dst_ref=south_recv.at[pl.ds(PAD, 2 * C * H)],
            send_sem=s_send.at[0],
            recv_sem=s_recv.at[0],
            device_id=(row, my_col),
            device_id_type=MESH,
        )

    arrive_sem = {i: g for g, run in enumerate(arrive_groups(R)) for i in run}

    def east_run(first, n, sem, col):
        return pltpu.make_async_remote_copy(
            src_ref=epack.at[pl.ds(first * S, n * S)],
            dst_ref=east_recv.at[pl.ds(first * S, n * S)],
            send_sem=e_send.at[0],
            recv_sem=e_recv.at[sem],
            device_id=(my_row, col),
            device_id_type=MESH,
        )

    def east_copy(k, col):
        return east_run(k, 1, arrive_sem[k], col)

    def send_east(run):
        around = sent_around(run[-1]) if run[-1] >= R - n_relay else False

        @pl.when((my_col > 0) & jnp.logical_not(around))
        def _():
            east_run(run[0], len(run), arrive_sem[run[0]], my_col - 1).start()

        if len(run) > 1 and run[-1] >= R - n_relay:
            for i in run:

                @pl.when(around & jnp.logical_not(sent_around(i)))
                def _():
                    east_copy(i, my_col - 1).start()

    def relay_copy(i, col):
        k = i - (R - n_relay)
        return pltpu.make_async_remote_copy(
            src_ref=epack.at[pl.ds(i * S, S)],
            dst_ref=relay_buf.at[pl.ds(k * S, S)],
            send_sem=e_send.at[0],
            recv_sem=relay_recv.at[k],
            device_id=(my_row, col),
            device_id_type=MESH,
        )

    def forward_copy(i, col):
        k = i - (R - n_relay)
        return pltpu.make_async_remote_copy(
            src_ref=relay_buf.at[pl.ds(k * S, S)],
            dst_ref=east_recv.at[pl.ds(i * S, S)],
            send_sem=e_send.at[0],
            recv_sem=e_recv.at[arrive_sem[i]],
            device_id=(my_row, col),
            device_id_type=MESH,
        )

    def forwards(i):
        return closes & (i >= R - relayed(my_col - 1))

    def forward(i):
        if i < R:

            @pl.when(forwards(i))
            def _():
                relay_copy(i, my_col).wait_recv()
                forward_copy(i, my_col - 2).start()

    def turn_copy(i, col):
        k = i - (R - n_turn)
        return pltpu.make_async_remote_copy(
            src_ref=strips.at[pl.ds(k * S, S)],
            dst_ref=turned.at[pl.ds(k * S, S)],
            send_sem=e_send.at[0],
            recv_sem=turn_recv.at[k],
            device_id=(my_row, col),
            device_id_type=MESH,
        )

    @pl.when(closes)
    def _():
        await_all(barrier, my_row > 0, my_col > 0)
        signal(pair_sem.at[0], my_row, my_col - 1, closes)

    load(0)
    for copy in tables:
        copy.start()
    for copy in rests:
        copy.start()
    pack(0)

    @pl.when(jnp.logical_not(closes))
    def _():
        await_all(barrier, my_row > 0, my_col > 0)

    send_east(send_runs(R)[0])
    sent = 1
    for g, run in enumerate(load_groups(R)):
        if g:
            load(g)
            for i in run:
                pack(i)
                if i == send_runs(R)[sent][-1]:
                    send_east(send_runs(R)[sent])
                    sent += 1
        if g == 1 or len(load_groups(R)) == 1:

            @pl.when(my_row > 0)
            def _():
                for k in range(2 * C):
                    south_copy(k, my_row - 1).start()

            if steps:
                tell(0)
    acc[...] = jnp.zeros_like(acc)
    late[...] = jnp.zeros_like(late)
    await_all(pair_sem.at[0], opens)
    for i in range(R - n_relay, R):

        @pl.when(sent_around(i))
        def _():
            relay_copy(i, my_col + 1).start()

    spread(0)
    whole(table, table, table_sem.at[0]).wait()
    size = R * (C - 1) * 2 * S
    whole(patches.at[pl.ds(0, size)], pv.at[pl.ds(PAD, size)], rest_sem.at[0]).wait()

    lane1 = lax.broadcasted_iota(jnp.int32, (1, S), 1)
    row8 = lax.broadcasted_iota(jnp.int32, (8, S), 0)

    for i in range(R - n_turn, R):

        @pl.when(turned_here(i))
        def _():
            o, w = ro[i, C - 1], rw[i, C - 1]
            base = PAD + (i * C + C - 1) * 2 * S
            scale = 1.0 / jnp.sqrt(jnp.full((1, S), S * w, jnp.int32).astype(f32))
            weight = jnp.where((lane1 & (H - 1)) < w, scale, 0.0)
            re = pltpu.roll(pv[pl.ds(base, S), :], S - o, 1)
            im = pltpu.roll(pv[pl.ds(base + S, S), :], lax.rem(S + H - o, S), 1)
            strips[pl.ds((i - R + n_turn) * S, S), :] = jnp.where(lane < H, re, im) * weight
            turn_copy(i, my_col + 1).start()

    def at(ref, row):
        return ref[pl.ds(pl.multiple_of(row, 8), 8), :]

    def put_at(ref, row, value):
        ref[pl.ds(pl.multiple_of(row, 8), 8), :] = value

    def scaled(re, im, width):
        scale = 1.0 / jnp.sqrt(jnp.full((1, S), S * width, jnp.int32).astype(f32))
        return fold_rows(re) * scale, fold_rows(im) * scale

    def put(plane, p, re, im, width):
        re, im = scaled(re, im, width)
        acc[pl.ds(plane * R * C + p, 1), :] = re
        acc[pl.ds((plane + 1) * R * C + p, 1), :] = im

    def gathered(pieces):
        re, im = None, None
        for a_re, a_im, b_re, b_im in pieces:
            u, v = a_re * b_re + a_im * b_im, a_re * b_im - a_im * b_re
            re, im = (u, v) if re is None else (re + u, im + v)
        return re, im

    def weights(i, j, within):
        o, w = ro[i, j], rw[i, j]
        keep = (lane1 >= o) & (lane1 < o + w)
        live = keep if j < C - 1 else keep & jnp.logical_not(last_col)
        half = jnp.where(live, f32(0.5), f32(1.0))
        third = jnp.where(live, f32(1.0 / 3.0), f32(0.5))
        down = jnp.logical_not((i == R - 1) & last_row)
        third = jnp.where(jnp.full((1, S), down), third, half)
        if within:
            half, third = jnp.where(keep, half, 0.0), jnp.where(keep, third, 0.0)
        return jnp.broadcast_to(half, (8, S)), jnp.broadcast_to(third, (8, S))

    def reached(i, j, q):
        o, w = do[i, j], dw[i, j]
        return row8 >= o - q if q < S - 8 else row8 < o + w - q

    def weight_at(i, j, q, half, third):
        return half if q < lo else jnp.where(reached(i, j, q), third, half)

    def rows_of(p):
        return PAD + p * 2 * S

    def east_of(i, j):
        base = rows_of(i * C + j + 1)

        def load(q, o):
            return pltpu.roll(at(pv, base + q), o, 1), pltpu.roll(at(pv, base + S + q), o, 1)

        return load

    def east_rim(i):
        def load(q, o):
            both = at(east_recv, i * S + q)
            return pltpu.roll(both, o, 1), pltpu.roll(both, lax.rem(o + H, S), 1)

        return load

    def place_east(i, j, q, b, half, third):
        to = (i * C + j) * 2 * S + q
        weight = weight_at(i, j, q, half, third)
        put_at(ew, to, b[0] * weight)
        put_at(ew, to + S, b[1] * weight)

    def east_sums(i, j, load, place):
        p = i * C + j
        o, w = ro[i, j], rw[i, j]
        base = rows_of(p)
        half, third = weights(i, j, True)

        def piece(q):
            b = load(q, o)
            if place:
                place_east(i, j, q, b, half, third)
            return (at(pv, base + q), at(pv, base + S + q)) + b

        re, im = gathered(piece(q) for q in range(0, S, 8))
        keep = (lane1 >= o) & (lane1 < o + w)
        return p, jnp.where(keep, re, 0.0), jnp.where(keep, im, 0.0), w

    def east_inner(i, carry):
        for j in range(C - 1):
            put(0, *east_sums(i, j, east_of(i, j), True))
        return carry

    def south_store(i, j, ref, start, gap):
        p = i * C + j
        o, w = do[i, j], dw[i, j]
        base = rows_of(p)
        _, third = weights(i, j, False)

        def piece(q):
            keep = reached(i, j, q)
            b_re = jnp.where(keep, ref[pl.ds(start + (q - o), 8), :], 0.0)
            b_im = jnp.where(keep, ref[pl.ds(start + gap + (q - o), 8), :], 0.0)
            to = p * 2 * T + q - lo
            put_at(sw, to, b_re * third)
            put_at(sw, to + T, b_im * third)
            return at(pv, base + q), at(pv, base + S + q), b_re, b_im

        re, im = gathered(piece(q) for q in range(lo, S, 8))
        put(2, p, re, im, w)

    def south_inner(i, carry):
        for j in range(C):
            south_store(i, j, pv, rows_of((i + 1) * C + j), S)
        return carry

    spread(1)
    lax.fori_loop(0, R // 2, east_inner, 0)
    spread(2)
    forward(R - n_relay)
    lax.fori_loop(R // 2, R, east_inner, 0)
    spread(3)
    forward(R - n_relay + 1)
    lax.fori_loop(0, R // 2, south_inner, 0)
    spread(4)
    forward(R - n_relay + 2)
    lax.fori_loop(R // 2, R - 1, south_inner, 0)
    spread(5)

    @pl.when(my_row < nr - 1)
    def _():
        all_south(my_row).wait_recv()

    @pl.when(last_row)
    def _():
        south_recv[...] = jnp.zeros_like(south_recv)

    for j in range(C):
        south_store(R - 1, j, south_recv, PAD + j * 2 * H, H)

    for k in range(6, len(steps)):
        spread(k)

    @pl.when(last_col)
    def _():
        east_recv[...] = jnp.zeros_like(east_recv)

    def east_wait(g):
        run = arrive_groups(R)[g]
        east_run(run[0], len(run), g, my_col).wait_recv()

    def rim_row(i):
        return 2 * (i - (R - n_late))

    n_late = min(2, R)
    for g, run in enumerate(arrive_groups(R)):
        if run[-1] < R - n_late:

            @pl.when(jnp.logical_not(last_col))
            def _():
                east_wait(g)

            for i in run:
                put(0, *east_sums(i, C - 1, east_rim(i), False))
    sums = lax.dot_general(
        jnp.ones((8, S), f32), acc[...], (((1,), (1,)), ((), ())),
        precision=highest, preferred_element_type=f32,
    )

    def rim(i):
        @pl.when(jnp.logical_not(last_col) & jnp.logical_not(turned_here(i)))
        def _():
            east_wait(arrive_sem[i])
            _, re, im, width = east_sums(i, C - 1, east_rim(i), False)
            re, im = scaled(re, im, width)
            late[rim_row(i) : rim_row(i) + 1, :] = re
            late[rim_row(i) + 1 : rim_row(i) + 2, :] = im

    def turn_row(i):
        return 2 * n_late + 2 * (i - (R - n_turn))

    def turn(i):
        @pl.when(closes & (i >= R - turned_of(my_col - 1)))
        def _():
            turn_copy(i, my_col).wait_recv()
            re, im = None, None
            for q in range(0, S, 8):
                a = at(turned, (i - R + n_turn) * S + q)
                b = at(epack, i * S + q)
                u, v = a * b, a * pltpu.roll(b, H, 1)
                re, im = (u, v) if re is None else (re + u, im + v)
            im = jnp.where(lane1 < H, im, -im)
            late[turn_row(i) : turn_row(i) + 1, :] = fold_rows(re)
            late[turn_row(i) + 1 : turn_row(i) + 2, :] = fold_rows(im)

    for i in range(R - n_late, R):
        if i == R - 1:
            for k in range(R - n_turn, R):
                turn(k)
        rim(i)
    tails = jnp.sum(late[...], axis=1, keepdims=True)

    def spot(i, part, row):
        return jnp.where(lane1 == part * R * C + i * C + C - 1, tails[row : row + 1, :], 0.0)

    east_row, turn_line = sums[0:1, :S], jnp.zeros((1, S), f32)
    for part in range(2):
        for i in range(R - n_late, R):
            east_row = east_row + spot(i, part, rim_row(i) + part)
        for i in range(R - n_turn, R):
            turn_line = turn_line + spot(i, part, turn_row(i) + part)
    for k, row in enumerate((east_row, sums[0:1, S:], turn_line)):
        send_buf[k] = row
        recv[k, pl.ds(me, 1), :] = row

    def index(d):
        return d[0] * nc + d[1]

    def gather_copy(target, source):
        return pltpu.make_async_remote_copy(
            src_ref=send_buf,
            dst_ref=recv.at[:, pl.ds(index(source), 1), :],
            send_sem=g_send.at[0],
            recv_sem=g_recv.at[0],
            device_id=target,
            device_id_type=MESH,
        )

    def all_gathered():
        return pltpu.make_async_remote_copy(
            src_ref=recv.at[:, pl.ds(0, ndev - 1), :],
            dst_ref=recv.at[:, pl.ds(0, ndev - 1), :],
            send_sem=g_send.at[0],
            recv_sem=g_recv.at[0],
            device_id=others[0],
            device_id_type=MESH,
        )

    for other in others:
        gather_copy(other, (my_row, my_col)).start()

    def weigh(i, carry):
        for j in range(C):
            half, third = weights(i, j, False)
            base, to = rows_of(i * C + j), (i * C + j) * 2 * S
            for q in range(0, S, 8):
                weight = weight_at(i, j, q, half, third)
                put_at(aw, to + q, at(pv, base + q) * weight)
                put_at(aw, to + S + q, at(pv, base + S + q) * weight)
        return carry

    def weigh_rim(i, carry):
        half, third = weights(i, C - 1, True)
        load, o = east_rim(i), ro[i, C - 1]
        for q in range(0, S, 8):
            place_east(i, C - 1, q, load(q, o), half, third)
        return carry

    lax.fori_loop(0, R, weigh, 0)
    for i in range(R - n_turn, R):

        @pl.when(turned_here(i))
        def _():
            east_wait(arrive_sem[i])

    lax.fori_loop(0, R, weigh_rim, 0)

    all_gathered().wait_recv()

    east, south = recv[0] + pltpu.roll(recv[2], ndev - 1, 0), recv[1]
    field = lax.broadcasted_iota(jnp.int32, (ndev, S), 0)
    slot = lax.broadcasted_iota(jnp.int32, (ndev, S), 1)
    real = slot < R * C
    j_of, i_of = slot % C, (slot // C) % R
    dc, dr = field % nc, field // nc

    def roll(x, by, axis):
        return pltpu.roll(x, by % x.shape[axis], axis)

    def from_east(x):
        far = roll(roll(x, -1, 0), C - 1, 1)
        far = jnp.where(dc < nc - 1, far, 0.0)
        return jnp.where(j_of < C - 1, roll(x, -1, 1), far)

    def from_west(x):
        far = roll(roll(x, 1, 0), 1 - C, 1)
        far = jnp.where(dc > 0, far, 0.0)
        return jnp.where(j_of > 0, roll(x, 1, 1), far)

    def from_south(x):
        far = roll(roll(x, -nc, 0), (R - 1) * C, 1)
        far = jnp.where(dr < nr - 1, far, 0.0)
        return jnp.where(i_of < R - 1, roll(x, -C, 1), far)

    def from_north(x):
        far = roll(roll(x, nc, 0), -(R - 1) * C, 1)
        far = jnp.where(dr > 0, far, 0.0)
        return jnp.where(i_of > 0, roll(x, C, 1), far)

    def swap(x):
        return roll(x, R * C, 1)

    def conj(x):
        return jnp.where(real, x, -x)

    steps_to = (
        (east, from_east),
        (south, from_south),
        (conj(from_west(east)), from_west),
        (conj(from_north(south)), from_north),
    )
    straight, crossed = [], []
    for corr, _ in steps_to:
        other = swap(corr)
        straight.append(jnp.where(real, corr, other))
        crossed.append(jnp.where(real, other, -corr))

    now = sum(corr for corr, _ in steps_to)
    square = now * now
    constant = eps_norm
    for step in range(1, ITERS):
        moved = [move(now) for _, move in steps_to]
        now = sum(a * b for a, b in zip(straight, moved))
        now = now + swap(sum(a * b for a, b in zip(crossed, moved)))
        square = eps_norm * square + now * now
        constant = constant * eps_norm
    fields[...] = now
    total = jnp.sum(jnp.sum(square, axis=0, keepdims=True), axis=1, keepdims=True)
    factor = 1.0 / jnp.sqrt(total * (1.0 / float(ndev * R * C)) + constant)
    own = fields[pl.ds(me, 1), :]
    east_own = fields[pl.ds(jnp.minimum(me + 1, ndev - 1), 1), :]
    east_own = jnp.where(jnp.full((1, S), last_col), 0.0, east_own)
    south_own = fields[pl.ds(jnp.minimum(me + nc, ndev - 1), 1), :]
    south_own = jnp.where(jnp.full((1, S), last_row), 0.0, south_own)
    phase_out[0:1, :] = own * factor
    patch = lax.broadcasted_iota(jnp.int32, (R * C, S), 0)
    ahead = lax.broadcasted_iota(jnp.int32, (R * C, S), 1) - patch
    inner_j, inner_i = patch % C < C - 1, patch // C < R - 1

    def spread_out(q, only):
        factors[q * R * C : (q + 1) * R * C, :] = (
            jnp.broadcast_to(jnp.sum(only, axis=1, keepdims=True), (R * C, S)) * factor
        )

    for part in range(2):
        at_part = ahead - part * R * C
        spread_out(part, jnp.where(at_part == 0, own, 0.0))
        near = jnp.where(inner_j & (at_part == 1), own, 0.0)
        spread_out(2 + part, jnp.where(jnp.logical_not(inner_j) & (at_part == 1 - C), east_own, near))
        near = jnp.where(inner_i & (at_part == C), own, 0.0)
        spread_out(
            4 + part, jnp.where(jnp.logical_not(inner_i) & (at_part == -(R - 1) * C), south_own, near)
        )

    all_gathered().wait_send()

    def chunks_sent(n):
        pltpu.make_async_remote_copy(
            src_ref=pv.at[pl.ds(0, n * S)],
            dst_ref=pv.at[pl.ds(0, n * S)],
            send_sem=e_send.at[0],
            recv_sem=e_recv.at[0],
            device_id=others[0],
            device_id_type=MESH,
        ).wait_send()

    pair_first = opens & (my_col == nc - 2)
    pair_last = closes & last_col
    for n, sender in (
        (R + n_turn, pair_first),
        (R + 1, opens & (my_col < nc - 2)),
        (R + n_relay, pair_last),
        (R, (my_col > 0) & jnp.logical_not(opens | pair_last)),
    ):

        @pl.when(sender)
        def _():
            chunks_sent(n)

    @pl.when(my_row > 0)
    def _():
        all_south(my_row - 1).wait_send()


def blend_kernel(dims, aw, ew, sw, factors, phase, out, phases, ov, pad, out_sem, phase_sem):
    R, C, S, pair = dims
    lo = S // 2 - 8
    T = S - lo
    piece = pair * 2 * S

    def save(k):
        return pltpu.make_async_copy(
            ov.at[pl.ds(k * piece, piece)], out.at[pl.ds(k * piece, piece)], out_sem.at[0]
        )

    def at(ref, row):
        return ref[pl.ds(pl.multiple_of(row, 8), 8), :]

    def times(g, a):
        return g[0] * a[0] - g[1] * a[1], g[0] * a[1] + g[1] * a[0]

    def place(p):
        g, ge, gs = (
            [jnp.broadcast_to(factors[pl.ds((2 * k + part) * R * C + p, 1), :], (8, S)) for part in range(2)]
            for k in range(3)
        )
        base = p * 2 * S
        for q in range(0, S, 8):
            own = times(g, (at(aw, base + q), at(aw, base + S + q)))
            east = times(ge, (at(ew, base + q), at(ew, base + S + q)))
            sums = [own[part] + east[part] for part in range(2)]
            if q >= lo:
                down = p * 2 * T + q - lo
                south = times(gs, (at(sw, down), at(sw, down + T)))
                sums = [sums[part] + south[part] for part in range(2)]
            ov[pl.ds(pl.multiple_of(base + q, 8), 8), :] = sums[0]
            ov[pl.ds(pl.multiple_of(base + S + q, 8), 8), :] = sums[1]

    def step(k, carry):
        for n in range(pair):
            place(k * pair + n)
        save(k).start()
        return carry

    lax.fori_loop(0, R * C // pair, step, 0)

    row8 = lax.broadcasted_iota(jnp.int32, (R, S), 0)
    line = jnp.broadcast_to(phase[0:1, :], (R, S))
    for part in range(2):
        plane = line if part == 0 else pltpu.roll(line, S - R * C, 1)
        for i in range(1, R):
            plane = jnp.where(row8 == i, pltpu.roll(line, S - part * R * C - i * C, 1), plane)
        pad[part] = plane[:, :C]
    send = pltpu.make_async_copy(pad, phases, phase_sem.at[0])
    send.start()
    send.wait()
    pltpu.make_async_copy(ov, out, out_sem.at[0]).wait()


def local(nr, nc, patches, right_offset, right_width, down_offset, down_width):
    R, C, _, S, _ = patches.shape
    H, ndev = S // 2, nr * nc
    T = S - (H - 8)
    dims = (R, C, S, nr, nc)
    flat = patches.reshape(R * C * 2 * S, S)
    anyspec = pl.BlockSpec(memory_space=pl.ANY)
    vmem = pl.BlockSpec(memory_space=pltpu.VMEM)
    dma = pltpu.SemaphoreType.DMA
    tables = (right_offset, right_width, down_offset, down_width)
    parts = pl.pallas_call(
        functools.partial(sync_kernel, dims),
        out_shape=(
            pltpu.VMEM((R * C * 2 * S, S), f32),
            pltpu.VMEM((R * C * 2 * S, S), f32),
            pltpu.VMEM((R * C * 2 * T, S), f32),
            pltpu.VMEM((6 * R * C, S), f32),
            pltpu.VMEM((8, S), f32),
        ),
        in_specs=[pl.BlockSpec(memory_space=pltpu.HBM)] * 5,
        out_specs=(vmem,) * 5,
        scratch_shapes=[
            pltpu.VMEM((PAD + R * C * 2 * S, S), f32),
            pltpu.VMEM((R * S, S), f32),
            pltpu.VMEM((2 * PAD + 2 * C * H, S), f32),
            pltpu.VMEM((R * S, S), f32),
            pltpu.VMEM((4 * R * C, S), f32),
            pltpu.VMEM((3, 1, S), f32),
            pltpu.VMEM((3, ndev, S), f32),
            pltpu.VMEM((ndev, S), f32),
            pltpu.SMEM((4, R, C), jnp.int32),
            pltpu.VMEM((n_relays(R) * S, S), f32),
            pltpu.VMEM((min(2, R) * S, S), f32),
            pltpu.VMEM((min(2, R) * S, S), f32),
            pltpu.VMEM((16, S), f32),
            dma((len(load_groups(R)),)), dma((1,)),
            dma((1,)), dma((len(arrive_groups(R)),)),
            dma((1,)), dma((1,)),
            dma((1,)), dma((1,)),
            dma((1,)),
            pltpu.SemaphoreType.REGULAR((n_rounds(nr) + n_rounds(nc),)),
            dma((n_relays(R),)), dma((min(2, R),)),
            pltpu.SemaphoreType.REGULAR((1,)),
        ],
        compiler_params=pltpu.CompilerParams(
            collective_id=0, has_side_effects=True, vmem_limit_bytes=24 << 20
        ),
        name="sync_patches",
    )(*(pltpu.with_memory_space_constraint(x, pltpu.HBM) for x in (flat, *tables)))
    pair = 2
    blended, phases = pl.pallas_call(
        functools.partial(blend_kernel, (R, C, S, pair)),
        out_shape=(
            jax.ShapeDtypeStruct((R * C * 2 * S, S), f32),
            jax.ShapeDtypeStruct((2, R, C), f32),
        ),
        in_specs=[vmem] * 5,
        out_specs=(anyspec, anyspec),
        scratch_shapes=[
            pltpu.VMEM((R * C * 2 * S, S), f32),
            pltpu.VMEM((2, R, C), f32),
            dma((1,)),
            dma((1,)),
        ],
        compiler_params=pltpu.CompilerParams(vmem_limit_bytes=24 << 20),
        name="blend_patches",
    )(*parts)
    return blended.reshape(patches.shape), phases


def solution(mesh):
    return jax.shard_map(
        functools.partial(local, mesh.shape["row"], mesh.shape["col"]),
        mesh=mesh,
        in_specs=(P("row", "col", None, None, None),) + (P("row", "col"),) * 4,
        out_specs=(P("row", "col", None, None, None), P(None, "row", "col")),
        check_vma=False,
    )
```

```python
import functools

import jax
import jax.numpy as jnp
from jax import lax
from jax.experimental import pallas as pl
from jax.experimental.pallas import tpu as pltpu
from jax.sharding import PartitionSpec as P

ITERS = 2
PAD = 64
eps_norm = 1.0
highest = lax.Precision.HIGHEST
MESH = pl.DeviceIdType.MESH
f32 = jnp.float32


def fold_rows(x):
    return jnp.sum(x, axis=0, keepdims=True)


def doubling(pos, n, at):
    if n == 1:
        return []
    rounds = [[at(-1) + (pos > 0, pos < n - 1)]]
    known = 1
    while known < n - 1:
        rounds.append([
            at(-known) + (pos >= known, pos < n - known),
            at(known) + (pos < n - known, pos >= known),
        ])
        known *= 2
    return rounds


def groups(n, sizes):
    runs, first = [], 0
    while first < n:
        size = sizes[min(len(runs), len(sizes) - 1)]
        runs.append(range(first, min(n, first + size)))
        first += size
    return runs


def n_relays(n):
    return min(3, n // 2)


def load_groups(n):
    return groups(n, (1, n))


def arrive_groups(n):
    return groups(n - 2, (max(1, n - 4), 2)) + [range(n - 2, n - 1), range(n - 1, n)] if n > 4 else groups(n, (1,))


def send_runs(n):
    runs = []
    for run in arrive_groups(n):
        runs += [run[:1], run[1:]] if run[0] == 0 and len(run) > 1 else [run]
    return runs


def n_rounds(n):
    return len(doubling(0, n, lambda k: (0, 0)))


def sync_kernel(
    dims, patches, ro_in, rw_in, do_in, dw_in, aw, ew, sw, factors, phase_out,
    pv, east_recv, south_recv,
    epack, acc, send_buf, recv, fields, table, relay_buf, strips, turned, late,
    col_sem, rest_sem, e_send, e_recv, s_send, s_recv, g_send, g_recv, table_sem, round_sem,
    relay_recv, turn_recv, pair_sem,
):
    R, C, S, nr, nc = dims
    H, ndev = S // 2, nr * nc
    lo = H - 8
    T = S - lo
    my_row, my_col = lax.axis_index("row"), lax.axis_index("col")
    me = my_row * nc + my_col
    last_col, last_row = my_col == nc - 1, my_row == nr - 1
    even = lax.rem(my_col, 2) == 0
    opens = even & (my_col >= max(2, nc - 4)) & (my_col < nc - 1)
    closes = jnp.logical_not(even) & (my_col >= max(3, nc - 3))
    n_relay, n_turn = n_relays(R), min(2, R)

    def relayed(c):
        return jnp.where(c == nc - 2, n_relay, 0)

    def turned_of(c):
        return jnp.where(c == nc - 2, n_turn, 1)

    def sent_around(i):
        return opens & (i >= R - relayed(my_col))

    def turned_here(i):
        return opens & (i >= R - turned_of(my_col))

    def skip(k, mine):
        return k + (k >= mine).astype(jnp.int32)

    others = [(a, skip(b, my_col)) for b in range(nc - 1) for a in range(nr)]
    others += [(skip(a, my_row), my_col) for a in range(nr - 1)]
    barrier = pltpu.get_barrier_semaphore()

    def signal(sem, row, col, there):
        @pl.when(there)
        def _():
            pl.semaphore_signal(sem, inc=1, device_id=(row, col), device_id_type=MESH)

    def await_all(sem, *due):
        amount = sum(one.astype(jnp.int32) for one in due)

        @pl.when(amount > 0)
        def _():
            pl.semaphore_wait(sem, amount)

    steps = doubling(my_row, nr, lambda k: (my_row + k, my_col))
    steps += doubling(my_col, nc, lambda k: (my_row, my_col + k))

    def tell(k):
        for row, col, there, _ in steps[k]:
            signal(round_sem.at[k], row, col, there)

    def spread(k):
        if k < len(steps):
            await_all(round_sem.at[k], *(here for _, _, _, here in steps[k]))
            if k + 1 < len(steps):
                tell(k + 1)

    load_sem = {i: g for g, run in enumerate(load_groups(R)) for i in run}
    cols = [
        pltpu.make_async_copy(
            patches.at[pl.ds(i * C * 2 * S, 2 * S)],
            pv.at[pl.ds(PAD + i * C * 2 * S, 2 * S)],
            col_sem.at[load_sem[i]],
        )
        for i in range(R)
    ]
    rests = [
        pltpu.make_async_copy(
            patches.at[pl.ds((i * C + 1) * 2 * S, (C - 1) * 2 * S)],
            pv.at[pl.ds(PAD + (i * C + 1) * 2 * S, (C - 1) * 2 * S)],
            rest_sem.at[0],
        )
        for i in range(R)
    ]
    tables = [
        pltpu.make_async_copy(here, table.at[k], table_sem.at[0])
        for k, here in enumerate((ro_in, rw_in, do_in, dw_in))
    ]
    ro, rw, do, dw = (table.at[k] for k in range(4))

    def whole(src, dst, sem):
        return pltpu.make_async_copy(src, dst, sem)

    signal(barrier, my_row, my_col + 1, my_col < nc - 1)
    for copy in cols:
        copy.start()
    signal(barrier, my_row + 1, my_col, my_row < nr - 1)
    lane = lax.broadcasted_iota(jnp.int32, (S, S), 1)

    def load(g):
        size = len(load_groups(R)[g]) * 2 * S
        whole(patches.at[pl.ds(0, size)], pv.at[pl.ds(PAD, size)], col_sem.at[g]).wait()

    def pack(i):
        base = PAD + i * C * 2 * S
        re = pv[pl.ds(base, S), :]
        im = pv[pl.ds(base + S, S), :]
        epack[pl.ds(i * S, S), :] = jnp.where(lane < H, re, pltpu.roll(im, H, 1))

    def south_copy(k, row):
        return pltpu.make_async_remote_copy(
            src_ref=patches.at[pl.ds(k * S, H)],
            dst_ref=south_recv.at[pl.ds(PAD + k * H, H)],
            send_sem=s_send.at[0],
            recv_sem=s_recv.at[0],
            device_id=(row, my_col),
            device_id_type=MESH,
        )

    def all_south(row):
        return pltpu.make_async_remote_copy(
            src_ref=patches.at[pl.ds(0, 2 * C * H)],
            dst_ref=south_recv.at[pl.ds(PAD, 2 * C * H)],
            send_sem=s_send.at[0],
            recv_sem=s_recv.at[0],
            device_id=(row, my_col),
            device_id_type=MESH,
        )

    arrive_sem = {i: g for g, run in enumerate(arrive_groups(R)) for i in run}

    def east_run(first, n, sem, col):
        return pltpu.make_async_remote_copy(
            src_ref=epack.at[pl.ds(first * S, n * S)],
            dst_ref=east_recv.at[pl.ds(first * S, n * S)],
            send_sem=e_send.at[0],
            recv_sem=e_recv.at[sem],
            device_id=(my_row, col),
            device_id_type=MESH,
        )

    def east_copy(k, col):
        return east_run(k, 1, arrive_sem[k], col)

    def send_east(run):
        around = sent_around(run[-1]) if run[-1] >= R - n_relay else False

        @pl.when((my_col > 0) & jnp.logical_not(around))
        def _():
            east_run(run[0], len(run), arrive_sem[run[0]], my_col - 1).start()

        if len(run) > 1 and run[-1] >= R - n_relay:
            for i in run:

                @pl.when(around & jnp.logical_not(sent_around(i)))
                def _():
                    east_copy(i, my_col - 1).start()

    def relay_copy(i, col):
        k = i - (R - n_relay)
        return pltpu.make_async_remote_copy(
            src_ref=epack.at[pl.ds(i * S, S)],
            dst_ref=relay_buf.at[pl.ds(k * S, S)],
            send_sem=e_send.at[0],
            recv_sem=relay_recv.at[k],
            device_id=(my_row, col),
            device_id_type=MESH,
        )

    def forward_copy(i, col):
        k = i - (R - n_relay)
        return pltpu.make_async_remote_copy(
            src_ref=relay_buf.at[pl.ds(k * S, S)],
            dst_ref=east_recv.at[pl.ds(i * S, S)],
            send_sem=e_send.at[0],
            recv_sem=e_recv.at[arrive_sem[i]],
            device_id=(my_row, col),
            device_id_type=MESH,
        )

    def forwards(i):
        return closes & (i >= R - relayed(my_col - 1))

    def forward(i):
        if i < R:

            @pl.when(forwards(i))
            def _():
                relay_copy(i, my_col).wait_recv()
                forward_copy(i, my_col - 2).start()

    def turn_copy(i, col):
        k = i - (R - n_turn)
        return pltpu.make_async_remote_copy(
            src_ref=strips.at[pl.ds(k * S, S)],
            dst_ref=turned.at[pl.ds(k * S, S)],
            send_sem=e_send.at[0],
            recv_sem=turn_recv.at[k],
            device_id=(my_row, col),
            device_id_type=MESH,
        )

    @pl.when(closes)
    def _():
        await_all(barrier, my_row > 0, my_col > 0)
        signal(pair_sem.at[0], my_row, my_col - 1, closes)

    load(0)
    for copy in tables:
        copy.start()
    for copy in rests:
        copy.start()
    pack(0)

    @pl.when(jnp.logical_not(closes))
    def _():
        await_all(barrier, my_row > 0, my_col > 0)

    send_east(send_runs(R)[0])
    sent = 1
    for g, run in enumerate(load_groups(R)):
        if g:
            load(g)
            for i in run:
                pack(i)
                if i == send_runs(R)[sent][-1]:
                    send_east(send_runs(R)[sent])
                    sent += 1
        if g == 1 or len(load_groups(R)) == 1:

            @pl.when(my_row > 0)
            def _():
                for k in range(2 * C):
                    south_copy(k, my_row - 1).start()

            if steps:
                tell(0)
    acc[...] = jnp.zeros_like(acc)
    late[...] = jnp.zeros_like(late)
    await_all(pair_sem.at[0], opens)
    for i in range(R - n_relay, R):

        @pl.when(sent_around(i))
        def _():
            relay_copy(i, my_col + 1).start()

    spread(0)
    whole(table, table, table_sem.at[0]).wait()
    size = R * (C - 1) * 2 * S
    whole(patches.at[pl.ds(0, size)], pv.at[pl.ds(PAD, size)], rest_sem.at[0]).wait()

    lane1 = lax.broadcasted_iota(jnp.int32, (1, S), 1)
    row8 = lax.broadcasted_iota(jnp.int32, (8, S), 0)

    for i in range(R - n_turn, R):

        @pl.when(turned_here(i))
        def _():
            o, w = ro[i, C - 1], rw[i, C - 1]
            base = PAD + (i * C + C - 1) * 2 * S
            scale = 1.0 / jnp.sqrt(jnp.full((1, S), S * w, jnp.int32).astype(f32))
            weight = jnp.where((lane1 & (H - 1)) < w, scale, 0.0)
            re = pltpu.roll(pv[pl.ds(base, S), :], S - o, 1)
            im = pltpu.roll(pv[pl.ds(base + S, S), :], lax.rem(S + H - o, S), 1)
            strips[pl.ds((i - R + n_turn) * S, S), :] = jnp.where(lane < H, re, im) * weight
            turn_copy(i, my_col + 1).start()

    def at(ref, row):
        return ref[pl.ds(pl.multiple_of(row, 8), 8), :]

    def put_at(ref, row, value):
        ref[pl.ds(pl.multiple_of(row, 8), 8), :] = value

    def scaled(re, im, width):
        scale = 1.0 / jnp.sqrt(jnp.full((1, S), S * width, jnp.int32).astype(f32))
        return fold_rows(re) * scale, fold_rows(im) * scale

    def put(plane, p, re, im, width):
        re, im = scaled(re, im, width)
        acc[pl.ds(plane * R * C + p, 1), :] = re
        acc[pl.ds((plane + 1) * R * C + p, 1), :] = im

    def gathered(pieces):
        re, im = None, None
        for a_re, a_im, b_re, b_im in pieces:
            u, v = a_re * b_re + a_im * b_im, a_re * b_im - a_im * b_re
            re, im = (u, v) if re is None else (re + u, im + v)
        return re, im

    def weights(i, j, within):
        o, w = ro[i, j], rw[i, j]
        keep = (lane1 >= o) & (lane1 < o + w)
        live = keep if j < C - 1 else keep & jnp.logical_not(last_col)
        half = jnp.where(live, f32(0.5), f32(1.0))
        third = jnp.where(live, f32(1.0 / 3.0), f32(0.5))
        down = jnp.logical_not((i == R - 1) & last_row)
        third = jnp.where(jnp.full((1, S), down), third, half)
        if within:
            half, third = jnp.where(keep, half, 0.0), jnp.where(keep, third, 0.0)
        return jnp.broadcast_to(half, (8, S)), jnp.broadcast_to(third, (8, S))

    def reached(i, j, q):
        o, w = do[i, j], dw[i, j]
        return row8 >= o - q if q < S - 8 else row8 < o + w - q

    def weight_at(i, j, q, half, third):
        return half if q < lo else jnp.where(reached(i, j, q), third, half)

    def rows_of(p):
        return PAD + p * 2 * S

    def east_of(i, j):
        base = rows_of(i * C + j + 1)

        def load(q, o):
            return pltpu.roll(at(pv, base + q), o, 1), pltpu.roll(at(pv, base + S + q), o, 1)

        return load

    def east_rim(i):
        def load(q, o):
            both = at(east_recv, i * S + q)
            return pltpu.roll(both, o, 1), pltpu.roll(both, lax.rem(o + H, S), 1)

        return load

    def place_east(i, j, q, b, half, third):
        to = (i * C + j) * 2 * S + q
        weight = weight_at(i, j, q, half, third)
        put_at(ew, to, b[0] * weight)
        put_at(ew, to + S, b[1] * weight)

    def east_sums(i, j, load, place):
        p = i * C + j
        o, w = ro[i, j], rw[i, j]
        base = rows_of(p)
        half, third = weights(i, j, True)

        def piece(q):
            b = load(q, o)
            if place:
                place_east(i, j, q, b, half, third)
            return (at(pv, base + q), at(pv, base + S + q)) + b

        re, im = gathered(piece(q) for q in range(0, S, 8))
        keep = (lane1 >= o) & (lane1 < o + w)
        return p, jnp.where(keep, re, 0.0), jnp.where(keep, im, 0.0), w

    def east_inner(i, carry):
        for j in range(C - 1):
            put(0, *east_sums(i, j, east_of(i, j), True))
        return carry

    def south_store(i, j, ref, start, gap):
        p = i * C + j
        o, w = do[i, j], dw[i, j]
        base = rows_of(p)
        _, third = weights(i, j, False)

        def piece(q):
            keep = reached(i, j, q)
            b_re = jnp.where(keep, ref[pl.ds(start + (q - o), 8), :], 0.0)
            b_im = jnp.where(keep, ref[pl.ds(start + gap + (q - o), 8), :], 0.0)
            to = p * 2 * T + q - lo
            put_at(sw, to, b_re * third)
            put_at(sw, to + T, b_im * third)
            return at(pv, base + q), at(pv, base + S + q), b_re, b_im

        re, im = gathered(piece(q) for q in range(lo, S, 8))
        put(2, p, re, im, w)

    def south_inner(i, carry):
        for j in range(C):
            south_store(i, j, pv, rows_of((i + 1) * C + j), S)
        return carry

    spread(1)
    lax.fori_loop(0, R // 2, east_inner, 0)
    spread(2)
    forward(R - n_relay)
    lax.fori_loop(R // 2, R, east_inner, 0)
    spread(3)
    forward(R - n_relay + 1)
    lax.fori_loop(0, R // 2, south_inner, 0)
    spread(4)
    forward(R - n_relay + 2)
    lax.fori_loop(R // 2, R - 1, south_inner, 0)
    spread(5)

    @pl.when(my_row < nr - 1)
    def _():
        all_south(my_row).wait_recv()

    @pl.when(last_row)
    def _():
        south_recv[...] = jnp.zeros_like(south_recv)

    for j in range(C):
        south_store(R - 1, j, south_recv, PAD + j * 2 * H, H)

    for k in range(6, len(steps)):
        spread(k)

    @pl.when(last_col)
    def _():
        east_recv[...] = jnp.zeros_like(east_recv)

    def east_wait(g):
        run = arrive_groups(R)[g]
        east_run(run[0], len(run), g, my_col).wait_recv()

    def rim_row(i):
        return 2 * (i - (R - n_late))

    n_late = min(2, R)
    for g, run in enumerate(arrive_groups(R)):
        if run[-1] < R - n_late:

            @pl.when(jnp.logical_not(last_col))
            def _():
                east_wait(g)

            for i in run:
                put(0, *east_sums(i, C - 1, east_rim(i), False))
    sums = lax.dot_general(
        jnp.ones((8, S), f32), acc[...], (((1,), (1,)), ((), ())),
        precision=highest, preferred_element_type=f32,
    )

    def rim(i):
        @pl.when(jnp.logical_not(last_col) & jnp.logical_not(turned_here(i)))
        def _():
            east_wait(arrive_sem[i])
            _, re, im, width = east_sums(i, C - 1, east_rim(i), False)
            re, im = scaled(re, im, width)
            late[rim_row(i) : rim_row(i) + 1, :] = re
            late[rim_row(i) + 1 : rim_row(i) + 2, :] = im

    def turn_row(i):
        return 2 * n_late + 2 * (i - (R - n_turn))

    def turn(i):
        @pl.when(closes & (i >= R - turned_of(my_col - 1)))
        def _():
            turn_copy(i, my_col).wait_recv()
            re, im = None, None
            for q in range(0, S, 8):
                a = at(turned, (i - R + n_turn) * S + q)
                b = at(epack, i * S + q)
                u, v = a * b, a * pltpu.roll(b, H, 1)
                re, im = (u, v) if re is None else (re + u, im + v)
            im = jnp.where(lane1 < H, im, -im)
            late[turn_row(i) : turn_row(i) + 1, :] = fold_rows(re)
            late[turn_row(i) + 1 : turn_row(i) + 2, :] = fold_rows(im)

    for i in range(R - n_late, R):
        if i == R - 1:
            for k in range(R - n_turn, R):
                turn(k)
        rim(i)
    tails = jnp.sum(late[...], axis=1, keepdims=True)

    def spot(i, part, row):
        return jnp.where(lane1 == part * R * C + i * C + C - 1, tails[row : row + 1, :], 0.0)

    east_row, turn_line = sums[0:1, :S], jnp.zeros((1, S), f32)
    for part in range(2):
        for i in range(R - n_late, R):
            east_row = east_row + spot(i, part, rim_row(i) + part)
        for i in range(R - n_turn, R):
            turn_line = turn_line + spot(i, part, turn_row(i) + part)
    for k, row in enumerate((east_row, sums[0:1, S:], turn_line)):
        send_buf[k] = row
        recv[k, pl.ds(me, 1), :] = row

    def index(d):
        return d[0] * nc + d[1]

    def gather_copy(target, source):
        return pltpu.make_async_remote_copy(
            src_ref=send_buf,
            dst_ref=recv.at[:, pl.ds(index(source), 1), :],
            send_sem=g_send.at[0],
            recv_sem=g_recv.at[0],
            device_id=target,
            device_id_type=MESH,
        )

    def all_gathered():
        return pltpu.make_async_remote_copy(
            src_ref=recv.at[:, pl.ds(0, ndev - 1), :],
            dst_ref=recv.at[:, pl.ds(0, ndev - 1), :],
            send_sem=g_send.at[0],
            recv_sem=g_recv.at[0],
            device_id=others[0],
            device_id_type=MESH,
        )

    for other in others:
        gather_copy(other, (my_row, my_col)).start()

    def weigh(i, carry):
        for j in range(C):
            half, third = weights(i, j, False)
            base, to = rows_of(i * C + j), (i * C + j) * 2 * S
            for q in range(0, S, 8):
                weight = weight_at(i, j, q, half, third)
                put_at(aw, to + q, at(pv, base + q) * weight)
                put_at(aw, to + S + q, at(pv, base + S + q) * weight)
        return carry

    def weigh_rim(i, carry):
        half, third = weights(i, C - 1, True)
        load, o = east_rim(i), ro[i, C - 1]
        for q in range(0, S, 8):
            place_east(i, C - 1, q, load(q, o), half, third)
        return carry

    lax.fori_loop(0, R, weigh, 0)
    for i in range(R - n_turn, R):

        @pl.when(turned_here(i))
        def _():
            east_wait(arrive_sem[i])

    lax.fori_loop(0, R, weigh_rim, 0)

    all_gathered().wait_recv()

    east, south = recv[0] + pltpu.roll(recv[2], ndev - 1, 0), recv[1]
    field = lax.broadcasted_iota(jnp.int32, (ndev, S), 0)
    slot = lax.broadcasted_iota(jnp.int32, (ndev, S), 1)
    real = slot < R * C
    j_of, i_of = slot % C, (slot // C) % R
    dc, dr = field % nc, field // nc

    def roll(x, by, axis):
        return pltpu.roll(x, by % x.shape[axis], axis)

    def from_east(x):
        far = roll(roll(x, -1, 0), C - 1, 1)
        far = jnp.where(dc < nc - 1, far, 0.0)
        return jnp.where(j_of < C - 1, roll(x, -1, 1), far)

    def from_west(x):
        far = roll(roll(x, 1, 0), 1 - C, 1)
        far = jnp.where(dc > 0, far, 0.0)
        return jnp.where(j_of > 0, roll(x, 1, 1), far)

    def from_south(x):
        far = roll(roll(x, -nc, 0), (R - 1) * C, 1)
        far = jnp.where(dr < nr - 1, far, 0.0)
        return jnp.where(i_of < R - 1, roll(x, -C, 1), far)

    def from_north(x):
        far = roll(roll(x, nc, 0), -(R - 1) * C, 1)
        far = jnp.where(dr > 0, far, 0.0)
        return jnp.where(i_of > 0, roll(x, C, 1), far)

    def swap(x):
        return roll(x, R * C, 1)

    def conj(x):
        return jnp.where(real, x, -x)

    steps_to = (
        (east, from_east),
        (south, from_south),
        (conj(from_west(east)), from_west),
        (conj(from_north(south)), from_north),
    )
    straight, crossed = [], []
    for corr, _ in steps_to:
        other = swap(corr)
        straight.append(jnp.where(real, corr, other))
        crossed.append(jnp.where(real, other, -corr))

    now = sum(corr for corr, _ in steps_to)
    square = now * now
    constant = eps_norm
    for step in range(1, ITERS):
        moved = [move(now) for _, move in steps_to]
        now = sum(a * b for a, b in zip(straight, moved))
        now = now + swap(sum(a * b for a, b in zip(crossed, moved)))
        square = eps_norm * square + now * now
        constant = constant * eps_norm
    fields[...] = now
    total = jnp.sum(jnp.sum(square, axis=0, keepdims=True), axis=1, keepdims=True)
    factor = 1.0 / jnp.sqrt(total * (1.0 / float(ndev * R * C)) + constant)
    own = fields[pl.ds(me, 1), :]
    east_own = fields[pl.ds(jnp.minimum(me + 1, ndev - 1), 1), :]
    east_own = jnp.where(jnp.full((1, S), last_col), 0.0, east_own)
    south_own = fields[pl.ds(jnp.minimum(me + nc, ndev - 1), 1), :]
    south_own = jnp.where(jnp.full((1, S), last_row), 0.0, south_own)
    phase_out[0:1, :] = own * factor
    patch = lax.broadcasted_iota(jnp.int32, (R * C, S), 0)
    ahead = lax.broadcasted_iota(jnp.int32, (R * C, S), 1) - patch
    inner_j, inner_i = patch % C < C - 1, patch // C < R - 1

    def spread_out(q, only):
        factors[q * R * C : (q + 1) * R * C, :] = (
            jnp.broadcast_to(jnp.sum(only, axis=1, keepdims=True), (R * C, S)) * factor
        )

    for part in range(2):
        at_part = ahead - part * R * C
        spread_out(part, jnp.where(at_part == 0, own, 0.0))
        near = jnp.where(inner_j & (at_part == 1), own, 0.0)
        spread_out(2 + part, jnp.where(jnp.logical_not(inner_j) & (at_part == 1 - C), east_own, near))
        near = jnp.where(inner_i & (at_part == C), own, 0.0)
        spread_out(
            4 + part, jnp.where(jnp.logical_not(inner_i) & (at_part == -(R - 1) * C), south_own, near)
        )

    all_gathered().wait_send()

    def chunks_sent(n):
        pltpu.make_async_remote_copy(
            src_ref=pv.at[pl.ds(0, n * S)],
            dst_ref=pv.at[pl.ds(0, n * S)],
            send_sem=e_send.at[0],
            recv_sem=e_recv.at[0],
            device_id=others[0],
            device_id_type=MESH,
        ).wait_send()

    pair_first = opens & (my_col == nc - 2)
    pair_last = closes & last_col
    for n, sender in (
        (R + n_turn, pair_first),
        (R + 1, opens & (my_col < nc - 2)),
        (R + n_relay, pair_last),
        (R, (my_col > 0) & jnp.logical_not(opens | pair_last)),
    ):

        @pl.when(sender)
        def _():
            chunks_sent(n)

    @pl.when(my_row > 0)
    def _():
        all_south(my_row - 1).wait_send()


def blend_kernel(dims, aw, ew, sw, factors, phase, out, phases, ov, pad, out_sem, phase_sem):
    R, C, S, pair = dims
    lo = S // 2 - 8
    T = S - lo
    piece = pair * 2 * S // 2

    def save(k):
        return pltpu.make_async_copy(
            ov.at[pl.ds(k * piece, piece)], out.at[pl.ds(k * piece, piece)], out_sem.at[0]
        )

    def at(ref, row):
        return ref[pl.ds(pl.multiple_of(row, 8), 8), :]

    def times(g, a):
        return g[0] * a[0] - g[1] * a[1], g[0] * a[1] + g[1] * a[0]

    def place(p):
        g, ge, gs = (
            [jnp.broadcast_to(factors[pl.ds((2 * k + part) * R * C + p, 1), :], (8, S)) for part in range(2)]
            for k in range(3)
        )
        base = p * 2 * S
        for q in range(0, S, 8):
            own = times(g, (at(aw, base + q), at(aw, base + S + q)))
            east = times(ge, (at(ew, base + q), at(ew, base + S + q)))
            sums = [own[part] + east[part] for part in range(2)]
            if q >= lo:
                down = p * 2 * T + q - lo
                south = times(gs, (at(sw, down), at(sw, down + T)))
                sums = [sums[part] + south[part] for part in range(2)]
            ov[pl.ds(pl.multiple_of(base + q, 8), 8), :] = sums[0]
            ov[pl.ds(pl.multiple_of(base + S + q, 8), 8), :] = sums[1]

    def step(k, carry):
        for n in range(pair):
            place(k * pair + n)
        for n in range(2):
            save(2 * k + n).start()
        return carry

    lax.fori_loop(0, R * C // pair, step, 0)

    row8 = lax.broadcasted_iota(jnp.int32, (R, S), 0)
    line = jnp.broadcast_to(phase[0:1, :], (R, S))
    for part in range(2):
        plane = line if part == 0 else pltpu.roll(line, S - R * C, 1)
        for i in range(1, R):
            plane = jnp.where(row8 == i, pltpu.roll(line, S - part * R * C - i * C, 1), plane)
        pad[part] = plane[:, :C]
    send = pltpu.make_async_copy(pad, phases, phase_sem.at[0])
    send.start()
    send.wait()
    pltpu.make_async_copy(ov, out, out_sem.at[0]).wait()


def local(nr, nc, patches, right_offset, right_width, down_offset, down_width):
    R, C, _, S, _ = patches.shape
    H, ndev = S // 2, nr * nc
    T = S - (H - 8)
    dims = (R, C, S, nr, nc)
    flat = patches.reshape(R * C * 2 * S, S)
    anyspec = pl.BlockSpec(memory_space=pl.ANY)
    vmem = pl.BlockSpec(memory_space=pltpu.VMEM)
    dma = pltpu.SemaphoreType.DMA
    tables = (right_offset, right_width, down_offset, down_width)
    parts = pl.pallas_call(
        functools.partial(sync_kernel, dims),
        out_shape=(
            pltpu.VMEM((R * C * 2 * S, S), f32),
            pltpu.VMEM((R * C * 2 * S, S), f32),
            pltpu.VMEM((R * C * 2 * T, S), f32),
            pltpu.VMEM((6 * R * C, S), f32),
            pltpu.VMEM((8, S), f32),
        ),
        in_specs=[pl.BlockSpec(memory_space=pltpu.HBM)] * 5,
        out_specs=(vmem,) * 5,
        scratch_shapes=[
            pltpu.VMEM((PAD + R * C * 2 * S, S), f32),
            pltpu.VMEM((R * S, S), f32),
            pltpu.VMEM((2 * PAD + 2 * C * H, S), f32),
            pltpu.VMEM((R * S, S), f32),
            pltpu.VMEM((4 * R * C, S), f32),
            pltpu.VMEM((3, 1, S), f32),
            pltpu.VMEM((3, ndev, S), f32),
            pltpu.VMEM((ndev, S), f32),
            pltpu.SMEM((4, R, C), jnp.int32),
            pltpu.VMEM((n_relays(R) * S, S), f32),
            pltpu.VMEM((min(2, R) * S, S), f32),
            pltpu.VMEM((min(2, R) * S, S), f32),
            pltpu.VMEM((16, S), f32),
            dma((len(load_groups(R)),)), dma((1,)),
            dma((1,)), dma((len(arrive_groups(R)),)),
            dma((1,)), dma((1,)),
            dma((1,)), dma((1,)),
            dma((1,)),
            pltpu.SemaphoreType.REGULAR((n_rounds(nr) + n_rounds(nc),)),
            dma((n_relays(R),)), dma((min(2, R),)),
            pltpu.SemaphoreType.REGULAR((1,)),
        ],
        compiler_params=pltpu.CompilerParams(
            collective_id=0, has_side_effects=True, vmem_limit_bytes=24 << 20
        ),
        name="sync_patches",
    )(*(pltpu.with_memory_space_constraint(x, pltpu.HBM) for x in (flat, *tables)))
    pair = 2
    blended, phases = pl.pallas_call(
        functools.partial(blend_kernel, (R, C, S, pair)),
        out_shape=(
            jax.ShapeDtypeStruct((R * C * 2 * S, S), f32),
            jax.ShapeDtypeStruct((2, R, C), f32),
        ),
        in_specs=[vmem] * 5,
        out_specs=(anyspec, anyspec),
        scratch_shapes=[
            pltpu.VMEM((R * C * 2 * S, S), f32),
            pltpu.VMEM((2, R, C), f32),
            dma((1,)),
            dma((1,)),
        ],
        compiler_params=pltpu.CompilerParams(vmem_limit_bytes=24 << 20),
        name="blend_patches",
    )(*parts)
    return blended.reshape(patches.shape), phases


def solution(mesh):
    return jax.shard_map(
        functools.partial(local, mesh.shape["row"], mesh.shape["col"]),
        mesh=mesh,
        in_specs=(P("row", "col", None, None, None),) + (P("row", "col"),) * 4,
        out_specs=(P("row", "col", None, None, None), P(None, "row", "col")),
        check_vma=False,
    )
```
